32 devices in a mesh: rep: 4 (over y, x), shard: 8 (over z, core).
Axes of the slice: x: 2, y: 2, z: 4, core: 2. Of those that a mesh axis runs over, the one named last changes fastest.
Arguments:
- tokens: bfloat16 [20480, 768], P(('rep', 'shard')), may hold values from -6 to 6
- ln1_gain: bfloat16 [768], P('shard'), may hold values from 0.5 to 1.5
- ln1_bias: bfloat16 [768], P('shard'), may hold values from -1.5 to 1.5
- w_qkv: bfloat16 [768, 2304], P('shard'), may hold values from -0.21875 to 0.21875
- qv_bias: bfloat16 [1536], P('shard'), may hold values from -1.5 to 1.5
- w_out: bfloat16 [768, 768], P('shard'), may hold values from -1.75 to 1.75
- out_bias: bfloat16 [768], P('shard'), may hold values from -1.5 to 1.5
- ln2_gain: bfloat16 [768], P('shard'), may hold values from 0.5 to 1.5
- ln2_bias: bfloat16 [768], P('shard'), may hold values from -1.5 to 1.5
- w_fc: bfloat16 [768, 3072], P('shard'), may hold values from -0.21875 to 0.21875
- fc_bias: bfloat16 [3072], P('shard'), may hold values from -1.5 to 1.5
- w_proj: bfloat16 [3072, 768], P('shard'), may hold values from -0.109375 to 0.109375
- proj_bias: bfloat16 [768], P('shard'), may hold values from -1.5 to 1.5
- teacher: bfloat16 [20480, 768], P(('rep', 'shard')), may hold values from -6 to 6
- cotangent: bfloat16 [20480, 768], P(('rep', 'shard')), may hold values from -12 to 12
- valid_mask: int32 [20480], P(('rep', 'shard')), may hold values from 0 to 1, as said below
Outputs:
- block_out: bfloat16 [20480, 768], P(('rep', 'shard'))
- input_grad: float32 [20480, 768], P(('rep', 'shard'))
- grad_ln1_gain: float32 [768], P('shard')
- grad_ln1_bias: float32 [768], P('shard')
- grad_w_qkv: float32 [768, 2304], P('shard')
- grad_qv_bias: float32 [1536], P('shard')
- grad_w_out: float32 [768, 768], P('shard')
- grad_out_bias: float32 [768], P('shard')
- grad_ln2_gain: float32 [768], P('shard')
- grad_ln2_bias: float32 [768], P('shard')
- grad_w_fc: float32 [768, 3072], P('shard')
- grad_fc_bias: float32 [3072], P('shard')
- grad_w_proj: float32 [3072, 768], P('shard')
- grad_proj_bias: float32 [768], P('shard')
The draws below stay inside these ranges and needn't reach their ends.
Inputs may be any that keep to these rules, and one draw needn't show every extreme that they name: `valid_mask`: the first of each device's 640 rows is 1.
All inputs are finite; a program needn't handle non-finite values.
Results may differ from the reference program's by a relative error of at most 0.012.
Values may be sent and summed in bfloat16 or wider, within the bound.
No kernel may reach another device: no remote copies, remote signals or barrier semaphores. Data moves between devices by JAX's collectives and lax.ppermute only.
A program may use at most 256 MiB of HBM per device.

```python
import jax
import jax.numpy as jnp
from jax import lax

D = 768
HEADS = 12
HEAD = 64
FF = 3072
PR_DEV = 128
CONT_LEN = 512
TOK = 640
PROMPT = 1024
ALL_TOK = 20480
N_REP = 4
N_SHARD = 8


def draw_valid_mask(key, part):
    row_ids = jnp.arange(ALL_TOK, dtype=jnp.int32)
    device_ids = row_ids // TOK
    last_device = max(ALL_TOK // TOK - 1, 1)
    threshold = 300 + 600 * device_ids // last_device
    drawn = jax.random.randint(key, (ALL_TOK,), 0, 1000, dtype=jnp.int32)
    picked = (drawn < threshold).astype(jnp.int32)
    return jnp.where(row_ids % TOK == 0, 1, picked).astype(jnp.int32)


def raised(values, key, source, target, blocks, factor):
    def block_of(dim):
        return (jnp.arange(values.shape[dim]) // (values.shape[dim] // blocks)).reshape((-1,) + (1,) * (values.ndim - 1 - dim))

    one_side = jax.random.permutation(key, blocks)[block_of(target)]
    far = (block_of(target) + blocks // 2) % blocks
    return jnp.where((block_of(source) == one_side) | (block_of(source) == far), factor * values, values)


def levels(stream_key, shape, pieces, smallest, top_value):
    loudness = 1.0
    for position, shards_of in pieces:
        heights = jax.random.uniform(jax.random.fold_in(jax.random.fold_in(stream_key, 6), position), (shards_of,), jnp.float32, smallest / len(pieces), top_value / len(pieces))
        loudness = loudness * jnp.repeat(jnp.exp(heights), shape[position] // shards_of).reshape((-1,) + (1,) * (len(shape) - 1 - position))
    return loudness


def centred(rng, dims, spread, reach, cuts=(), kind=jnp.bfloat16):
    values = spread * jax.random.normal(rng, dims, jnp.float32)
    if cuts:
        values = values * levels(rng, dims, cuts, -0.22, 0.18)
    return jnp.clip(values, -reach, reach).astype(kind)


def bell_draw_with(key, extent, deviation, bound, pieces, heavy, kind=jnp.bfloat16):
    array = deviation * jax.random.normal(key, extent, jnp.float32)
    if pieces:
        array = array * levels(key, extent, pieces, -0.22, 0.18)
    return jnp.clip(raised(array, jax.random.fold_in(key, 3), *heavy), -bound, bound).astype(kind)


def setup_inputs(seed: int = 0) -> dict:
    streams_of = jax.random.split(jax.random.key(seed), 17)
    tokens = centred(streams_of[0], (ALL_TOK, D), 1.0, 6.0, ((0, 32),))
    ln1_gain = jnp.clip(1.0 + 0.1 * jax.random.normal(streams_of[1], (D,), jnp.float32), 0.5, 1.5).astype(jnp.bfloat16)
    ln1_bias = centred(streams_of[2], (D,), 0.3, 1.5, ((0, 8),))
    w_qkv = centred(streams_of[3], (D, 3 * D), D ** -0.5, 0.21875, ((0, 8),))
    qv_bias = centred(streams_of[4], (2 * D,), 0.3, 1.5, ((0, 8),))
    w_out = centred(streams_of[5], (D, D), 12 ** -0.5, 1.75, ((0, 8),))
    out_bias = centred(streams_of[6], (D,), 0.3, 1.5, ((0, 8),))
    ln2_gain = jnp.clip(1.0 + 0.1 * jax.random.normal(streams_of[7], (D,), jnp.float32), 0.5, 1.5).astype(jnp.bfloat16)
    ln2_bias = centred(streams_of[8], (D,), 0.3, 1.5, ((0, 8),))
    w_fc = centred(streams_of[9], (D, FF), D ** -0.5, 0.21875, ((0, 8),))
    fc_bias = centred(streams_of[10], (FF,), 0.3, 1.5, ((0, 8),))
    w_proj = centred(streams_of[11], (FF, D), FF ** -0.5, 0.109375, ((0, 8),))
    proj_bias = centred(streams_of[12], (D,), 0.3, 1.5, ((0, 8),))
    teacher = centred(streams_of[13], (ALL_TOK, D), 1.0, 6.0, ((0, 32),))
    cotangent = bell_draw_with(streams_of[14], (ALL_TOK, D), 1.0, 12.0, ((0, 32),), (0, 1, 32, 2.75))
    valid_mask = draw_valid_mask(jax.random.fold_in(streams_of[16], 71), 0)
    return dict(tokens=tokens, ln1_gain=ln1_gain, ln1_bias=ln1_bias, w_qkv=w_qkv, qv_bias=qv_bias, w_out=w_out, out_bias=out_bias, ln2_gain=ln2_gain, ln2_bias=ln2_bias, w_fc=w_fc, fc_bias=fc_bias, w_proj=w_proj, proj_bias=proj_bias, teacher=teacher, cotangent=cotangent, valid_mask=valid_mask)


@jax.custom_vjp
def low(v):
    return lax.optimization_barrier(v.astype(jnp.bfloat16)).astype(jnp.float32)

@jax.custom_vjp
def low_back(v):
    return v

def low_keep(v):
    return (low(v), None)

def low_pass(kept, grad):
    return (grad,)

def back_keep(v):
    return (v, None)

def back_low(kept, grad):
    return (low(grad),)
low.defvjp(low_keep, low_pass)
low_back.defvjp(back_keep, back_low)

def matmul(left, right):
    return jnp.dot(left, right, precision=lax.Precision.HIGHEST, preferred_element_type=jnp.float32)

def layer_norm(values, gain_vec, bias_vec):
    centered = values - lax.optimization_barrier(jnp.mean(values, axis=-1, keepdims=True))
    variance = lax.optimization_barrier(jnp.mean(centered * centered, axis=-1, keepdims=True))
    return centered * lax.rsqrt(variance + 1e-05) * gain_vec + bias_vec

def gelu_tanh(values):
    return 0.5 * values * (1.0 + jnp.tanh(0.7978845608028654 * (values + 0.044715 * values * values * values)))

def attend(queries, keys_all, values_all):
    query_groups = queries.reshape(N_REP, N_SHARD, TOK, D)
    key_groups = keys_all.reshape(N_REP, N_SHARD, TOK, D)
    value_groups = values_all.reshape(N_REP, N_SHARD, TOK, D)

    def one_group(operands):
        group_q, group_k, group_v = operands
        prompt_keys = group_k[:, :PR_DEV].reshape(PROMPT, D)
        prompt_values = group_v[:, :PR_DEV].reshape(PROMPT, D)

        def one_block(block_ops):
            block_q, cont_k, cont_v, block_id = block_ops
            key_rows = jnp.concatenate([prompt_keys, cont_k], axis=0)
            value_rows = jnp.concatenate([prompt_values, cont_v], axis=0)
            query_three = block_q.reshape(TOK, HEADS, HEAD)
            key_three = key_rows.reshape(PROMPT + CONT_LEN, HEADS, HEAD)
            value_three = value_rows.reshape(PROMPT + CONT_LEN, HEADS, HEAD)
            scores = low_back(jnp.einsum('qhd,khd->hqk', query_three, key_three, precision=lax.Precision.HIGHEST) * 0.125)
            row_ids = jnp.arange(TOK, dtype=jnp.int32)[:, None]
            key_ids = jnp.arange(PROMPT + CONT_LEN, dtype=jnp.int32)[None, :]
            in_prompt = key_ids < PROMPT
            prompt_ok = in_prompt & (key_ids <= block_id * PR_DEV + row_ids)
            cont_ok = in_prompt | (key_ids - PROMPT <= row_ids - PR_DEV)
            allowed = jnp.where(row_ids < PR_DEV, prompt_ok, cont_ok)
            scores = jnp.where(allowed[None], scores, jnp.float32(-1e+30))
            expo = jnp.exp(scores - lax.optimization_barrier(jnp.max(scores, axis=-1, keepdims=True)))
            probs = low(expo / lax.optimization_barrier(jnp.sum(expo, axis=-1, keepdims=True)))
            mixed = jnp.einsum('hqk,khd->qhd', probs, value_three, precision=lax.Precision.HIGHEST)
            return mixed.reshape(TOK, D)
        block_fn = jax.checkpoint(one_block)
        return lax.map(block_fn, (group_q, group_k[:, PR_DEV:], group_v[:, PR_DEV:], jnp.arange(N_SHARD, dtype=jnp.int32)))
    mixed_all = lax.map(one_group, (query_groups, key_groups, value_groups))
    return mixed_all.reshape(ALL_TOK, D)

def forward(inputs, ln1_gain, ln1_bias, w_qkv, qv_bias, w_out, out_bias, ln2_gain, ln2_bias, w_fc, fc_bias, w_proj, proj_bias):
    normed_one = low(layer_norm(inputs, ln1_gain, ln1_bias))
    bias_row = jnp.concatenate([qv_bias[:D], jnp.zeros((D,), jnp.float32), qv_bias[D:]])
    proj_qkv = low(low_back(matmul(normed_one, w_qkv) + bias_row))
    mixed = attend(proj_qkv[:, :D], proj_qkv[:, D:2 * D], proj_qkv[:, 2 * D:])
    mixed = low(low_back(mixed))
    branch_one = low_back(matmul(mixed, w_out) + out_bias)
    resid_one = inputs + branch_one
    normed_two = low(layer_norm(resid_one, ln2_gain, ln2_bias))
    hidden_pre = low_back(matmul(normed_two, w_fc) + fc_bias)
    hidden_act = low(gelu_tanh(hidden_pre))
    branch_two = low_back(matmul(hidden_act, w_proj) + proj_bias)
    return resid_one + branch_two

def reference(tokens, ln1_gain, ln1_bias, w_qkv, qv_bias, w_out, out_bias, ln2_gain, ln2_bias, w_fc, fc_bias, w_proj, proj_bias, teacher, cotangent, valid_mask):
    weights = (ln1_gain, ln1_bias, w_qkv, qv_bias, w_out, out_bias, ln2_gain, ln2_bias, w_fc, fc_bias, w_proj, proj_bias)
    weights = tuple((item.astype(jnp.float32) for item in weights))
    inputs = tokens.astype(jnp.float32)
    output, pullback = jax.vjp(forward, inputs, *weights)
    mask_f = valid_mask.astype(jnp.float32)
    token_total = jnp.sum(mask_f)
    factor = ALL_TOK / token_total
    grad_output = cotangent.astype(jnp.float32) + factor * mask_f[:, None] * (output - teacher.astype(jnp.float32))
    grads = pullback(grad_output)
    return (output.astype(jnp.bfloat16), grads[0], grads[1], grads[2], grads[3], grads[4], grads[5], grads[6], grads[7], grads[8], grads[9], grads[10], grads[11], grads[12])
```

```python
import jax
import jax.numpy as jnp
from jax import lax
from jax.experimental import pallas as pl
from jax.experimental.pallas import tpu as pltpu
from jax.sharding import PartitionSpec as P

F32 = jnp.float32
BF = jnp.bfloat16
HEAD = 64
PR_DEV = 128
PAIR = 2 * HEAD
SCALE = 0.125
EPS = 1e-05
NEG = -1e30
VMEM_LIMIT = 60 * 1024 * 1024


def dot_nt(a, b):
    return lax.dot_general(a, b, (((1,), (1,)), ((), ())), preferred_element_type=F32)


def dot_nn(a, b):
    return lax.dot_general(a, b, (((1,), (0,)), ((), ())), preferred_element_type=F32)


def dot_tn(a, b):
    return lax.dot_general(a, b, (((0,), (0,)), ((), ())), preferred_element_type=F32)


def normalize(values):
    centered = values - jnp.mean(values, axis=-1, keepdims=True)
    inv = lax.rsqrt(jnp.mean(centered * centered, axis=-1, keepdims=True) + EPS)
    return centered * inv, inv


def norm_back(e, z, inv):
    return inv * (
        e - jnp.mean(e, axis=-1, keepdims=True) - z * jnp.mean(e * z, axis=-1, keepdims=True)
    )


def layer_norm(values, gain_vec, bias_vec):
    return normalize(values)[0] * gain_vec + bias_vec


def gelu_tanh(values):
    return (
        0.5
        * values
        * (1.0 + jnp.tanh(0.7978845608028654 * (values + 0.044715 * values * values * values)))
    )


def column_sums(matrix):
    return jnp.sum(matrix.astype(F32), axis=0)


def cost(flops, nbytes, trans=0):
    return pl.CostEstimate(flops=int(flops), bytes_accessed=int(nbytes), transcendentals=int(trans))


def qkv_call(bundle, tokens, vecs, shard):
    ns, _, width = bundle.shape
    tok = tokens.shape[0]
    cont = tok - PR_DEV
    plen = ns * PR_DEV
    keys = plen + cont
    dsh = width // ns

    def kern(sh_ref, g_ref, t_ref, vec_ref, h_ref, q_ref, k_ref, v_ref):
        gain, bias, bq, bv = vec_ref[0:1], vec_ref[1:2], vec_ref[2:3], vec_ref[3:4]
        wq, wk, wv = (
            g_ref[:, j * dsh : (j + 1) * dsh, :].reshape(width, width) for j in range(3)
        )
        step = 4

        def chunk(x, r0):
            h = (normalize(x.astype(F32))[0] * gain + bias).astype(BF)
            rows = pl.ds(r0, h.shape[0])
            h_ref[rows, :] = h
            k_ref[rows, :] = dot_nn(h, wk).astype(BF)
            v_ref[rows, :] = (dot_nn(h, wv) + bv).astype(BF)

        def to_q(h):
            return ((dot_nn(h, wq) + bq).astype(BF).astype(F32) * SCALE).astype(BF)

        for b in range(0, ns, step):
            x = g_ref[b : b + step, 3 * dsh : 3 * dsh + PR_DEV, :]
            chunk(x.reshape(x.shape[0] * PR_DEV, width), b * PR_DEV)
        chunk(t_ref[PR_DEV:, :], plen)
        own = pl.multiple_of(sh_ref[0] * PR_DEV, PR_DEV)
        q_ref[:PR_DEV, :] = to_q(h_ref[pl.ds(own, PR_DEV), :])
        q_ref[PR_DEV:, :] = to_q(h_ref[plen:, :])

    shape = lambda r: jax.ShapeDtypeStruct((r, width), BF)
    vm = pl.BlockSpec(memory_space=pltpu.VMEM)
    return pl.pallas_call(
        kern,
        in_specs=[pl.BlockSpec(memory_space=pltpu.SMEM), vm, vm, vm],
        out_specs=[vm] * 4,
        out_shape=[shape(keys), shape(tok), shape(keys), shape(keys)],
        compiler_params=pltpu.CompilerParams(vmem_limit_bytes=VMEM_LIMIT),
        cost_estimate=cost(2 * width * width * (2 * keys + tok), 2 * width * (6 * keys)),
        name="qkv",
    )(shard, bundle, tokens, vecs)


def attn_fwd(q, k, v, shard, rb):
    tok, width = q.shape
    keys = k.shape[0]
    cont = tok - PR_DEV
    plen = keys - cont
    npair = width // PAIR

    def kern(sh_ref, q_ref, k_ref, v_ref, o_ref, lse_ref):
        sh = sh_ref[0]
        first = lax.broadcasted_iota(jnp.int32, (1, PAIR), 1) < HEAD

        def block(r0, rows, n, offset, masked):
            outs, lses = [], []
            for h in range(2):
                mine = first if h == 0 else jnp.logical_not(first)
                qq = jnp.where(mine, q_ref[pl.ds(r0, rows), :], 0).astype(BF)
                s = dot_nt(qq, k_ref[pl.ds(0, n), :])
                tail = s[:, n - masked :]
                row = lax.broadcasted_iota(jnp.int32, tail.shape, 0)
                col = lax.broadcasted_iota(jnp.int32, tail.shape, 1)
                tail = jnp.where(col <= row + offset, tail, NEG)
                s = tail if masked == n else jnp.concatenate([s[:, : n - masked], tail], axis=1)
                top = jnp.max(s, axis=1, keepdims=True)
                p = jnp.exp(s - top)
                total = jnp.sum(p, axis=1, keepdims=True)
                outs.append(dot_nn(p.astype(BF), v_ref[pl.ds(0, n), :]) * (1.0 / total))
                lses.append(top + jnp.log(total))
            o_ref[pl.ds(r0, rows), :] = jnp.where(first, outs[0], outs[1]).astype(BF)
            turned = jnp.transpose(jnp.where(first, lses[0], lses[1]))
            lse_ref[0, 0:1, pl.ds(r0, rows)] = turned[0:1]
            lse_ref[0, 1:2, pl.ds(r0, rows)] = turned[HEAD : HEAD + 1]

        block(0, PR_DEV, plen, sh * PR_DEV, plen)
        for i in range(cont // rb):
            block(PR_DEV + i * rb, rb, plen + (i + 1) * rb, 0, rb)

    spq = pl.BlockSpec((tok, PAIR), lambda i: (0, i))
    spk = pl.BlockSpec((keys, PAIR), lambda i: (0, i))
    return pl.pallas_call(
        kern,
        grid=(npair,),
        in_specs=[pl.BlockSpec(memory_space=pltpu.SMEM), spq, spk, spk],
        out_specs=[spq, pl.BlockSpec((1, 2, tok), lambda i: (i, 0, 0))],
        out_shape=[
            jax.ShapeDtypeStruct((tok, width), BF),
            jax.ShapeDtypeStruct((npair, 2, tok), F32),
        ],
        compiler_params=pltpu.CompilerParams(vmem_limit_bytes=VMEM_LIMIT),
        cost_estimate=cost(16 * width * tok * keys, 4 * width * (tok + keys)),
        name="attn_fwd",
    )(shard, q, k, v)


def attn_bwd(q, k, v, o, do, lse, shard, rb):
    tok, width = q.shape
    keys = k.shape[0]
    cont = tok - PR_DEV
    plen = keys - cont
    npair = width // PAIR

    def kern(sh_ref, q_ref, k_ref, v_ref, o_ref, do_ref, lse_ref, dq_ref, dk_ref, dv_ref, ka, va):
        sh = sh_ref[0]
        first = lax.broadcasted_iota(jnp.int32, (1, PAIR), 1) < HEAD
        ka[...] = jnp.zeros_like(ka)
        va[...] = jnp.zeros_like(va)
        hr = lax.broadcasted_iota(jnp.int32, (8, PAIR), 0)
        hc = lax.broadcasted_iota(jnp.int32, (8, PAIR), 1)
        pick = jnp.where(hc // HEAD == hr, 1.0, 0.0).astype(F32)

        def block(r0, rows, n, offset, masked):
            prod = o_ref[pl.ds(r0, rows), :].astype(F32) * do_ref[pl.ds(r0, rows), :].astype(F32)
            row_dot = lax.dot_general(
                pick,
                prod,
                (((1,), (1,)), ((), ())),
                precision=lax.Precision.HIGHEST,
                preferred_element_type=F32,
            )
            dqs = []
            for h in range(2):
                mine = first if h == 0 else jnp.logical_not(first)
                qq = jnp.where(mine, q_ref[pl.ds(r0, rows), :], 0).astype(BF)
                gg = jnp.where(mine, do_ref[pl.ds(r0, rows), :], 0).astype(BF)
                kk = k_ref[pl.ds(0, n), :]
                s = dot_nt(kk, qq)
                tail = s[n - masked :]
                col = lax.broadcasted_iota(jnp.int32, tail.shape, 0)
                row = lax.broadcasted_iota(jnp.int32, tail.shape, 1)
                tail = jnp.where(col <= row + offset, tail, NEG)
                s = tail if masked == n else jnp.concatenate([s[: n - masked], tail], axis=0)
                p = jnp.exp(s - lse_ref[0, h : h + 1, pl.ds(r0, rows)])
                dp = dot_nt(v_ref[pl.ds(0, n), :], gg)
                ds = (p * (dp - row_dot[h : h + 1, :])).astype(BF)
                va[pl.ds(0, n), :] += dot_nn(p.astype(BF), gg)
                ka[pl.ds(0, n), :] += dot_nn(ds, qq)
                dqs.append(dot_tn(ds, kk))
            dq_ref[pl.ds(r0, rows), :] = (jnp.where(first, dqs[0], dqs[1]) * SCALE).astype(BF)

        block(0, PR_DEV, plen, sh * PR_DEV, plen)
        for i in range(cont // rb):
            block(PR_DEV + i * rb, rb, plen + (i + 1) * rb, 0, rb)
        dk_ref[...] = ka[...].astype(BF)
        dv_ref[...] = va[...].astype(BF)

    spq = pl.BlockSpec((tok, PAIR), lambda i: (0, i))
    spk = pl.BlockSpec((keys, PAIR), lambda i: (0, i))
    return pl.pallas_call(
        kern,
        grid=(npair,),
        in_specs=[
            pl.BlockSpec(memory_space=pltpu.SMEM),
            spq,
            spk,
            spk,
            spq,
            spq,
            pl.BlockSpec((1, 2, tok), lambda i: (i, 0, 0)),
        ],
        out_specs=[spq, spk, spk],
        out_shape=[
            jax.ShapeDtypeStruct((tok, width), BF),
            jax.ShapeDtypeStruct((keys, width), BF),
            jax.ShapeDtypeStruct((keys, width), BF),
        ],
        scratch_shapes=[pltpu.VMEM((keys, PAIR), F32), pltpu.VMEM((keys, PAIR), F32)],
        compiler_params=pltpu.CompilerParams(vmem_limit_bytes=VMEM_LIMIT),
        cost_estimate=cost(40 * width * tok * keys, 8 * width * (tok + keys)),
        name="attn_bwd",
    )(shard, q, k, v, o, do, lse)


def dh1_call(bundle, tokens, vecs, dq, dk, dv, dx1, shard):
    ns, _, width = bundle.shape
    tok = tokens.shape[0]
    cont = tok - PR_DEV
    plen = ns * PR_DEV
    dsh = width // ns

    def kern(sh_ref, g_ref, t_ref, vec_ref, dq_ref, dk_ref, dv_ref, dx_ref, pd_ref, ig_ref, sm_ref):
        gain = vec_ref[0:1]
        wq, wk, wv = (
            g_ref[:, j * dsh : (j + 1) * dsh, :].reshape(width, width) for j in range(3)
        )
        step = 4
        g_gain = jnp.zeros((1, width), F32)
        g_bias = jnp.zeros((1, width), F32)
        g_v = jnp.zeros((1, width), F32)
        total = lambda m: jnp.sum(m, axis=0, keepdims=True)
        for b in range(0, ns, step):
            x = g_ref[b : b + step, 3 * dsh : 3 * dsh + PR_DEV, :]
            rows = x.shape[0] * PR_DEV
            z, _ = normalize(x.reshape(rows, width).astype(F32))
            dvr = dv_ref[b * PR_DEV : b * PR_DEV + rows, :]
            dh = dot_nt(dk_ref[b * PR_DEV : b * PR_DEV + rows, :], wk) + dot_nt(dvr, wv)
            g_gain += total(dh * z)
            g_bias += total(dh)
            g_v += total(dvr.astype(F32))
            pd_ref[b * PR_DEV : b * PR_DEV + rows, :] = dh.astype(BF)
        z, inv = normalize(t_ref[PR_DEV:, :].astype(F32))
        dvr = dv_ref[plen:, :]
        dh = dot_nt(dk_ref[plen:, :], wk) + dot_nt(dvr, wv) + dot_nt(dq_ref[PR_DEV:, :], wq)
        g_gain += total(dh * z)
        g_bias += total(dh)
        g_v += total(dvr.astype(F32))
        ig_ref[PR_DEV:, :] = dx_ref[PR_DEV:, :] + norm_back(dh * gain, z, inv)
        ig_ref[:PR_DEV, :] = dx_ref[:PR_DEV, :]
        own = pl.ds(pl.multiple_of(sh_ref[0] * PR_DEV, PR_DEV), PR_DEV)
        z, _ = normalize(t_ref[:PR_DEV, :].astype(F32))
        part = dot_nt(dq_ref[:PR_DEV, :], wq)
        g_gain += total(part * z)
        g_bias += total(part)
        both = dot_nt(dk_ref[own, :], wk) + dot_nt(dv_ref[own, :], wv)
        pd_ref[own, :] = (both + part).astype(BF)
        sm_ref[0:1, :] = g_gain
        sm_ref[1:2, :] = g_bias
        sm_ref[2:3, :] = total(dq_ref[...].astype(F32))
        sm_ref[3:4, :] = g_v
        sm_ref[4:8, :] = jnp.zeros((4, width), F32)

    vm = pl.BlockSpec(memory_space=pltpu.VMEM)
    return pl.pallas_call(
        kern,
        in_specs=[pl.BlockSpec(memory_space=pltpu.SMEM)] + [vm] * 7,
        out_specs=[vm] * 3,
        out_shape=[
            jax.ShapeDtypeStruct((plen, width), BF),
            jax.ShapeDtypeStruct((tok, width), F32),
            jax.ShapeDtypeStruct((8, width), F32),
        ],
        compiler_params=pltpu.CompilerParams(vmem_limit_bytes=VMEM_LIMIT),
        cost_estimate=cost(
            2 * width * width * (2 * (plen + cont) + tok), 2 * width * (5 * plen + 8 * cont)
        ),
        name="dh1",
    )(shard, bundle, tokens, vecs, dq, dk, dv, dx1)


def grad_wqkv_call(h1, dq, dk, dv, small, shard, ns):
    keys, width = h1.shape
    tok = dq.shape[0]
    plen = ns * PR_DEV
    dsh = width // ns
    extra = small.shape[1]

    def kern(sh_ref, h_ref, dq_ref, dk_ref, dv_ref, s_ref, o_ref):
        own = pl.ds(pl.multiple_of(sh_ref[0] * PR_DEV, PR_DEV), PR_DEV)
        gq = dot_tn(h_ref[own, :], dq_ref[:PR_DEV, :]) + dot_tn(h_ref[plen:, :], dq_ref[PR_DEV:, :])
        o_ref[:, :dsh, :] = gq.astype(BF).reshape(ns, dsh, width)
        gk = dot_tn(h_ref[...], dk_ref[...])
        o_ref[:, dsh : 2 * dsh, :] = gk.astype(BF).reshape(ns, dsh, width)
        gv = dot_tn(h_ref[...], dv_ref[...])
        o_ref[:, 2 * dsh : 3 * dsh, :] = gv.astype(BF).reshape(ns, dsh, width)
        o_ref[:, 3 * dsh :, :] = s_ref[...]

    vm = pl.BlockSpec(memory_space=pltpu.VMEM)
    return pl.pallas_call(
        kern,
        in_specs=[pl.BlockSpec(memory_space=pltpu.SMEM)] + [vm] * 5,
        out_specs=vm,
        out_shape=jax.ShapeDtypeStruct((ns, 3 * dsh + extra, width), BF),
        compiler_params=pltpu.CompilerParams(vmem_limit_bytes=VMEM_LIMIT),
        cost_estimate=cost(2 * width * width * (2 * keys + tok), 2 * width * (4 * keys)),
        name="grad_wqkv",
    )(shard, h1, dq, dk, dv, small)


def finish_call(grad, summed, tokens, vecs):
    tok, width = grad.shape

    def kern(g_ref, s_ref, t_ref, vec_ref, o_ref):
        z, inv = normalize(t_ref[...].astype(F32))
        e = s_ref[...].astype(F32) * vec_ref[0:1]
        o_ref[...] = g_ref[...] + norm_back(e, z, inv)

    block = pl.BlockSpec((PR_DEV, width), lambda i: (0, 0))
    return pl.pallas_call(
        kern,
        grid=(1,),
        in_specs=[block, block, block, pl.BlockSpec(vecs.shape, lambda i: (0, 0))],
        out_specs=block,
        out_shape=jax.ShapeDtypeStruct((tok, width), F32),
        input_output_aliases={0: 0},
        cost_estimate=cost(20 * PR_DEV * width, 12 * PR_DEV * width),
        name="finish",
    )(grad, summed, tokens, vecs)


def rep_sum(values):
    n = lax.axis_size("rep")
    if n & (n - 1):
        return [lax.psum(v.astype(t), "rep").astype(F32) for v, t in values]
    out = [v for v, _ in values]
    bit = 1
    while bit < n:
        perm = [(i, i ^ bit) for i in range(n)]
        got = [lax.ppermute(v.astype(t), "rep", perm) for v, (_, t) in zip(out, values)]
        out = [v.astype(t).astype(F32) + g.astype(F32) for v, g, (_, t) in zip(out, got, values)]
        bit *= 2
    return out


def local(
    tokens,
    ln1_gain,
    ln1_bias,
    w_qkv,
    qv_bias,
    w_out,
    out_bias,
    ln2_gain,
    ln2_bias,
    w_fc,
    fc_bias,
    w_proj,
    proj_bias,
    teacher,
    cotangent,
    valid_mask,
):
    ns = lax.axis_size("shard")
    shard = lax.axis_index("shard").astype(jnp.int32).reshape(1)
    tok, width = tokens.shape
    hidden = w_fc.shape[1]
    plen = ns * PR_DEV
    dsh = width // ns
    rb = 256

    bundle = lax.all_gather(
        jnp.concatenate(
            [w_qkv[:, :width], w_qkv[:, width : 2 * width], w_qkv[:, 2 * width :], tokens[:PR_DEV]]
        ),
        "shard",
    )
    mask_f = valid_mask.astype(F32)
    counts = jnp.sum(mask_f.reshape(-1, PR_DEV), axis=1).astype(BF)
    sizes = [v.shape[0] for v in (ln1_gain, ln1_bias, qv_bias, out_bias, ln2_gain, ln2_bias, fc_bias, proj_bias)]
    offs = [0]
    for s in sizes:
        offs.append(offs[-1] + s)
    packed = jnp.concatenate(
        [ln1_gain, ln1_bias, qv_bias, out_bias, ln2_gain, ln2_bias, fc_bias, proj_bias, counts]
    )
    packed = jnp.pad(packed, (0, (-packed.shape[0]) % 128))
    params = lax.all_gather(packed.reshape(1, -1), "shard", axis=0, tiled=True).astype(F32)
    gain_one, bias_one, full_qv, full_ob, gain_two, bias_two, full_fb, full_pb = (
        params[:, offs[i] : offs[i + 1]].reshape(-1) for i in range(8)
    )
    count = jnp.sum(params[:, offs[8] : offs[8] + tok // PR_DEV])
    (token_total,) = rep_sum([(jnp.full((8, 128), count, F32), F32)])
    token_total = token_total[0, 0]
    vecs = jnp.stack([gain_one, bias_one, full_qv[:width], full_qv[width:]] + [gain_one] * 4)

    full_out = lax.all_gather(w_out, "shard", axis=0, tiled=True)
    full_fc = lax.all_gather(w_fc, "shard", axis=0, tiled=True)
    full_proj = lax.all_gather(w_proj, "shard", axis=0, tiled=True)

    h1, q, k, v = qkv_call(bundle, tokens, vecs, shard)
    mix, lse = attn_fwd(q, k, v, shard, rb)

    inputs = tokens.astype(F32)
    resid_one = inputs + dot_nn(mix, full_out) + full_ob
    normed_two, norm_two_back = jax.vjp(layer_norm, resid_one, gain_two, bias_two)
    act_two = normed_two.astype(BF)
    hidden_pre = dot_nn(act_two, full_fc) + full_fb
    hidden_act, gelu_back = jax.vjp(gelu_tanh, hidden_pre)
    hidden_low = hidden_act.astype(BF)
    output = resid_one + dot_nn(hidden_low, full_proj) + full_pb
    device_count = lax.axis_size("rep") * ns
    factor = tok * device_count / token_total
    grad_output = cotangent.astype(F32) + factor * mask_f[:, None] * (output - teacher.astype(F32))
    grad_branch = grad_output.astype(BF)
    grad_pb = column_sums(grad_branch)
    grad_proj = dot_tn(hidden_low, grad_branch)
    own_proj = lax.psum_scatter(grad_proj.astype(BF), "shard", scatter_dimension=0, tiled=True)
    grad_hidden = dot_nt(grad_branch, full_proj)
    (grad_pre,) = gelu_back(grad_hidden)
    grad_pre_low = grad_pre.astype(BF)
    grad_fb = column_sums(grad_pre_low)
    grad_fc = dot_tn(act_two, grad_pre_low)
    own_fc = lax.psum_scatter(grad_fc.astype(BF), "shard", scatter_dimension=0, tiled=True)
    grad_act_two = dot_nt(grad_pre_low, full_fc)
    grad_resid_part, grad_gain_two, grad_bias_two = norm_two_back(grad_act_two)
    grad_resid = grad_output + grad_resid_part
    grad_attn = grad_resid.astype(BF)
    grad_ob = column_sums(grad_attn)
    grad_wo = dot_tn(mix, grad_attn)
    own_wo = lax.psum_scatter(grad_wo.astype(BF), "shard", scatter_dimension=0, tiled=True)
    grad_mix = dot_nt(grad_attn, full_out).astype(BF)

    dq, dk, dv = attn_bwd(q, k, v, mix, grad_mix, lse, shard, rb)
    part, ig, small = dh1_call(bundle, tokens, vecs, dq, dk, dv, grad_resid, shard)
    own_dh = lax.psum_scatter(part, "shard", scatter_dimension=0, tiled=True)
    input_grad = finish_call(ig, own_dh, tokens, vecs)

    small_list = [
        small[0],
        small[1],
        jnp.concatenate([small[2], small[3]]),
        grad_ob,
        grad_gain_two,
        grad_bias_two,
        grad_fb,
        grad_pb,
    ]
    rows = jnp.concatenate([s.reshape(ns, -1) for s in small_list], axis=1).astype(BF)
    unit = 16 * width
    rows = jnp.pad(rows, ((0, 0), (0, (-rows.shape[1]) % unit))).reshape(ns, -1, width)
    grads = grad_wqkv_call(h1, dq, dk, dv, rows, shard, ns)
    own_qkv = lax.psum_scatter(
        grads.reshape(-1, width), "shard", scatter_dimension=0, tiled=True
    )
    sum_proj, sum_fc, sum_wo = rep_sum(
        [(own_proj.astype(F32), BF), (own_fc.astype(F32), BF), (own_wo.astype(F32), BF)]
    )
    (sum_qkv,) = rep_sum([(own_qkv.astype(F32), BF)])
    grad_qkv_own = jnp.concatenate(
        [sum_qkv[:dsh], sum_qkv[dsh : 2 * dsh], sum_qkv[2 * dsh : 3 * dsh]], axis=1
    )
    flat = sum_qkv[3 * dsh :].reshape(-1)
    vec = [flat[offs[i] : offs[i + 1]] for i in range(8)]
    return (
        output.astype(BF),
        input_grad,
        vec[0],
        vec[1],
        grad_qkv_own,
        vec[2],
        sum_wo,
        vec[3],
        vec[4],
        vec[5],
        sum_fc,
        vec[6],
        sum_proj,
        vec[7],
    )


def solution(mesh):
    rows = P(("rep", "shard"), None)
    mat = P("shard", None)
    vec = P("shard")
    return jax.shard_map(
        local,
        mesh=mesh,
        in_specs=(
            rows,
            vec,
            vec,
            mat,
            vec,
            mat,
            vec,
            vec,
            vec,
            mat,
            vec,
            mat,
            vec,
            rows,
            rows,
            P(("rep", "shard")),
        ),
        out_specs=(rows, rows, vec, vec, mat, vec, mat, vec, vec, vec, mat, vec, mat, vec),
        check_vma=False,
    )
```

```python
import jax
import jax.numpy as jnp
from jax import lax
from jax.experimental import pallas as pl
from jax.experimental.pallas import tpu as pltpu
from jax.sharding import PartitionSpec as P

F32 = jnp.float32
BF = jnp.bfloat16
HEAD = 64
PR_DEV = 128
PAIR = 2 * HEAD
SCALE = 0.125
EPS = 1e-05
NEG = -1e30
VMEM_LIMIT = 60 * 1024 * 1024
EXTRA = 16


def dot_nt(a, b):
    return lax.dot_general(a, b, (((1,), (1,)), ((), ())), preferred_element_type=F32)


def dot_nn(a, b):
    return lax.dot_general(a, b, (((1,), (0,)), ((), ())), preferred_element_type=F32)


def dot_tn(a, b):
    return lax.dot_general(a, b, (((0,), (0,)), ((), ())), preferred_element_type=F32)


def normalize(values):
    centered = values - jnp.mean(values, axis=-1, keepdims=True)
    inv = lax.rsqrt(jnp.mean(centered * centered, axis=-1, keepdims=True) + EPS)
    return centered * inv, inv


def norm_back(e, z, inv):
    return inv * (
        e - jnp.mean(e, axis=-1, keepdims=True) - z * jnp.mean(e * z, axis=-1, keepdims=True)
    )


def cost(flops, nbytes, trans=0):
    return pl.CostEstimate(flops=int(flops), bytes_accessed=int(nbytes), transcendentals=int(trans))


def fixed(shape):
    return pl.BlockSpec(shape, lambda *_: (0,) * len(shape))


def qkv_call(bundle, tokens, vecs, shard):
    ns, _, width = bundle.shape
    tok = tokens.shape[0]
    cont = tok - PR_DEV
    plen = ns * PR_DEV
    keys = plen + cont
    dsh = width // ns
    step = cont // PR_DEV
    chunks = ns // step

    def kern(sh_ref, g_ref, t_ref, vec_ref, h_ref, q_ref, k_ref, v_ref, x_ref):
        i = pl.program_id(0)
        gain, bias, bq, bv = vec_ref[0:1], vec_ref[1:2], vec_ref[2:3], vec_ref[3:4]
        wq, wk, wv = (
            g_ref[:, j * dsh : (j + 1) * dsh, :].reshape(width, width) for j in range(3)
        )

        def to_q(h):
            return ((dot_nn(h, wq) + bq).astype(BF).astype(F32) * SCALE).astype(BF)

        @pl.when(i < chunks)
        def _():
            x = g_ref[pl.ds(i * step, step), 3 * dsh : 3 * dsh + PR_DEV, :]
            x_ref[...] = x.reshape(cont, width)

        @pl.when(i == chunks)
        def _():
            x_ref[...] = t_ref[PR_DEV:, :]

        h = (normalize(x_ref[...].astype(F32))[0] * gain + bias).astype(BF)
        h_ref[...] = h
        k_ref[...] = dot_nn(h, wk).astype(BF)
        v_ref[...] = (dot_nn(h, wv) + bv).astype(BF)

        @pl.when(i == sh_ref[0] // step)
        def _():
            own = pl.multiple_of((sh_ref[0] % step) * PR_DEV, PR_DEV)
            q_ref[:PR_DEV, :] = to_q(h_ref[pl.ds(own, PR_DEV), :])

        @pl.when(i == chunks)
        def _():
            q_ref[PR_DEV:, :] = to_q(h_ref[...])

    shape = lambda r: jax.ShapeDtypeStruct((r, width), BF)
    rows = pl.BlockSpec((cont, width), lambda i: (i, 0))
    return pl.pallas_call(
        kern,
        grid=(chunks + 1,),
        in_specs=[
            pl.BlockSpec(memory_space=pltpu.SMEM),
            fixed(bundle.shape),
            fixed(tokens.shape),
            fixed(vecs.shape),
        ],
        out_specs=[rows, fixed((tok, width)), rows, rows],
        out_shape=[shape(keys), shape(tok), shape(keys), shape(keys)],
        scratch_shapes=[pltpu.VMEM((cont, width), BF)],
        compiler_params=pltpu.CompilerParams(vmem_limit_bytes=VMEM_LIMIT),
        cost_estimate=cost(2 * width * width * (2 * keys + tok), 2 * width * (6 * keys)),
        name="qkv",
    )(shard, bundle, tokens, vecs)


def attn_fwd(q, k, v, shard, rb):
    tok, width = q.shape
    keys = k.shape[0]
    cont = tok - PR_DEV
    plen = keys - cont
    npair = width // PAIR

    def kern(sh_ref, q_ref, k_ref, v_ref, o_ref, lse_ref):
        sh = sh_ref[0]
        first = lax.broadcasted_iota(jnp.int32, (1, PAIR), 1) < HEAD

        def block(r0, rows, n, offset, masked):
            outs, lses = [], []
            for h in range(2):
                mine = first if h == 0 else jnp.logical_not(first)
                qq = jnp.where(mine, q_ref[pl.ds(r0, rows), :], 0).astype(BF)
                s = dot_nt(qq, k_ref[pl.ds(0, n), :])
                tail = s[:, n - masked :]
                row = lax.broadcasted_iota(jnp.int32, tail.shape, 0)
                col = lax.broadcasted_iota(jnp.int32, tail.shape, 1)
                tail = jnp.where(col <= row + offset, tail, NEG)
                s = tail if masked == n else jnp.concatenate([s[:, : n - masked], tail], axis=1)
                top = jnp.max(s, axis=1, keepdims=True)
                p = jnp.exp(s - top)
                total = jnp.sum(p, axis=1, keepdims=True)
                outs.append(dot_nn(p.astype(BF), v_ref[pl.ds(0, n), :]) * (1.0 / total))
                lses.append(top + jnp.log(total))
            o_ref[pl.ds(r0, rows), :] = jnp.where(first, outs[0], outs[1]).astype(BF)
            turned = jnp.transpose(jnp.where(first, lses[0], lses[1]))
            lse_ref[0, 0:1, pl.ds(r0, rows)] = turned[0:1]
            lse_ref[0, 1:2, pl.ds(r0, rows)] = turned[HEAD : HEAD + 1]

        block(0, PR_DEV, plen, sh * PR_DEV, plen)
        for i in range(cont // rb):
            block(PR_DEV + i * rb, rb, plen + (i + 1) * rb, 0, rb)

    spq = pl.BlockSpec((tok, PAIR), lambda i: (0, i))
    spk = pl.BlockSpec((keys, PAIR), lambda i: (0, i))
    return pl.pallas_call(
        kern,
        grid=(npair,),
        in_specs=[pl.BlockSpec(memory_space=pltpu.SMEM), spq, spk, spk],
        out_specs=[spq, pl.BlockSpec((1, 2, tok), lambda i: (i, 0, 0))],
        out_shape=[
            jax.ShapeDtypeStruct((tok, width), BF),
            jax.ShapeDtypeStruct((npair, 2, tok), F32),
        ],
        compiler_params=pltpu.CompilerParams(vmem_limit_bytes=VMEM_LIMIT),
        cost_estimate=cost(16 * width * tok * keys, 4 * width * (tok + keys)),
        name="attn_fwd",
    )(shard, q, k, v)


def attn_bwd(q, k, v, o, do, lse, shard, rb):
    tok, width = q.shape
    keys = k.shape[0]
    cont = tok - PR_DEV
    plen = keys - cont
    npair = width // PAIR

    def kern(sh_ref, q_ref, k_ref, v_ref, o_ref, do_ref, lse_ref, dq_ref, dkv_ref, ka, va):
        sh = sh_ref[0]
        first = lax.broadcasted_iota(jnp.int32, (1, PAIR), 1) < HEAD
        ka[...] = jnp.zeros_like(ka)
        va[...] = jnp.zeros_like(va)
        hr = lax.broadcasted_iota(jnp.int32, (8, PAIR), 0)
        hc = lax.broadcasted_iota(jnp.int32, (8, PAIR), 1)
        pick = jnp.where(hc // HEAD == hr, 1.0, 0.0).astype(F32)

        def block(r0, rows, n, offset, masked):
            prod = o_ref[pl.ds(r0, rows), :].astype(F32) * do_ref[pl.ds(r0, rows), :].astype(F32)
            row_dot = lax.dot_general(
                pick,
                prod,
                (((1,), (1,)), ((), ())),
                precision=lax.Precision.HIGHEST,
                preferred_element_type=F32,
            )
            dqs = []
            for h in range(2):
                mine = first if h == 0 else jnp.logical_not(first)
                qq = jnp.where(mine, q_ref[pl.ds(r0, rows), :], 0).astype(BF)
                gg = jnp.where(mine, do_ref[pl.ds(r0, rows), :], 0).astype(BF)
                kk = k_ref[pl.ds(0, n), :]
                s = dot_nt(kk, qq)
                tail = s[n - masked :]
                col = lax.broadcasted_iota(jnp.int32, tail.shape, 0)
                row = lax.broadcasted_iota(jnp.int32, tail.shape, 1)
                tail = jnp.where(col <= row + offset, tail, NEG)
                s = tail if masked == n else jnp.concatenate([s[: n - masked], tail], axis=0)
                p = jnp.exp(s - lse_ref[0, h : h + 1, pl.ds(r0, rows)])
                dp = dot_nt(v_ref[pl.ds(0, n), :], gg)
                ds = (p * (dp - row_dot[h : h + 1, :])).astype(BF)
                va[pl.ds(0, n), :] += dot_nn(p.astype(BF), gg)
                ka[pl.ds(0, n), :] += dot_nn(ds, qq)
                dqs.append(dot_tn(ds, kk))
            dq_ref[pl.ds(r0, rows), :] = (jnp.where(first, dqs[0], dqs[1]) * SCALE).astype(BF)

        block(0, PR_DEV, plen, sh * PR_DEV, plen)
        for i in range(cont // rb):
            block(PR_DEV + i * rb, rb, plen + (i + 1) * rb, 0, rb)
        dkv_ref[0] = ka[...].astype(BF)
        dkv_ref[1] = va[...].astype(BF)

    spq = pl.BlockSpec((tok, PAIR), lambda i: (0, i))
    spk = pl.BlockSpec((keys, PAIR), lambda i: (0, i))
    return pl.pallas_call(
        kern,
        grid=(npair,),
        in_specs=[
            pl.BlockSpec(memory_space=pltpu.SMEM),
            spq,
            spk,
            spk,
            spq,
            spq,
            pl.BlockSpec((1, 2, tok), lambda i: (i, 0, 0)),
        ],
        out_specs=[spq, pl.BlockSpec((2, keys, PAIR), lambda i: (0, 0, i))],
        out_shape=[
            jax.ShapeDtypeStruct((tok, width), BF),
            jax.ShapeDtypeStruct((2, keys, width), BF),
        ],
        scratch_shapes=[pltpu.VMEM((keys, PAIR), F32), pltpu.VMEM((keys, PAIR), F32)],
        compiler_params=pltpu.CompilerParams(vmem_limit_bytes=VMEM_LIMIT),
        cost_estimate=cost(40 * width * tok * keys, 8 * width * (tok + keys)),
        name="attn_bwd",
    )(shard, q, k, v, o, do, lse)


def out_proj_call(mix, second, tokens, vecs):
    ns, _, width = second.shape
    tok = tokens.shape[0]
    dsh = width // ns

    def kern(o_ref, w_ref, t_ref, vec_ref, x_ref, h_ref):
        wo = w_ref[...].reshape(width, width)
        x1 = t_ref[...].astype(F32) + (dot_nn(o_ref[...], wo) + vec_ref[4:5])
        x_ref[...] = x1
        h_ref[...] = (normalize(x1)[0] * vec_ref[5:6] + vec_ref[6:7]).astype(BF)

    whole = lambda a: pl.BlockSpec(a.shape, lambda i: (0,) * a.ndim)
    return pl.pallas_call(
        kern,
        grid=(1,),
        in_specs=[
            whole(mix),
            pl.BlockSpec((ns, dsh, width), lambda i: (0, 1, 0)),
            whole(tokens),
            whole(vecs),
        ],
        out_specs=[pl.BlockSpec((tok, width), lambda i: (0, 0))] * 2,
        out_shape=[jax.ShapeDtypeStruct((tok, width), F32), jax.ShapeDtypeStruct((tok, width), BF)],
        compiler_params=pltpu.CompilerParams(vmem_limit_bytes=VMEM_LIMIT),
        cost_estimate=cost(2 * width * width * tok, 12 * width * tok),
        name="out_proj",
    )(mix, second, tokens, vecs)


def fc_call(h2, second, got, other, vecs, where):
    ns, _, width = second.shape
    tok = h2.shape[0]
    dsh = width // ns
    half = ns // 2
    nq = len(got) + 1

    def kern(*refs):
        wh_ref, h_ref, own_ref = refs[:3]
        got_refs = refs[3 : 2 + nq]
        other_refs = refs[2 + nq : 1 + 2 * nq]
        vec_ref, g_ref, gp_ref, w_ref = refs[1 + 2 * nq :]
        me, core = wh_ref[0], wh_ref[1]
        step = pl.program_id(0)
        rows = half * dsh

        @pl.when(step == 0)
        def _():
            w_ref[0] = own_ref[...].reshape(width, width)

        for j in range(1, nq):

            @pl.when(step == j)
            def _():
                first = pl.multiple_of(core * rows, rows)
                second_half = pl.multiple_of((1 - core) * rows, rows)
                w_ref[0, pl.ds(first, rows), :] = got_refs[j - 1][...].reshape(rows, width)
                w_ref[0, pl.ds(second_half, rows), :] = other_refs[j - 1][...].reshape(rows, width)

        c = jnp.bitwise_xor(me, step)
        f = dot_nn(h_ref[...], w_ref[0]) + vec_ref[pl.ds(8 + c, 1), :]
        square = f * f
        t = jnp.tanh(0.7978845608028654 * f * (1.0 + 0.044715 * square))
        up = 0.5 * (1.0 + t)
        g_ref[0] = (f * up).astype(BF)
        slope = 0.5 * f * (1.0 - t * t) * (0.7978845608028654 + 0.1070322243 * square)
        gp_ref[0] = (up + slope).astype(BF)

    pick = lambda j, wh: (jnp.bitwise_xor(wh[0], j), 0, 0)
    return pl.pallas_call(
        kern,
        grid_spec=pltpu.PrefetchScalarGridSpec(
            num_scalar_prefetch=1,
            grid=(nq,),
            in_specs=[fixed(h2.shape), fixed((ns, dsh, width))]
            + [fixed(a.shape) for a in got]
            + [fixed(a.shape) for a in other]
            + [fixed(vecs.shape)],
            out_specs=[
                pl.BlockSpec((1, tok, width), pick),
                pl.BlockSpec((1, tok, width), pick),
                pl.BlockSpec((1, width, width), pick),
            ],
        ),
        out_shape=[
            jax.ShapeDtypeStruct((nq, tok, width), BF),
            jax.ShapeDtypeStruct((nq, tok, width), BF),
            jax.ShapeDtypeStruct((nq, width, width), BF),
        ],
        compiler_params=pltpu.CompilerParams(vmem_limit_bytes=VMEM_LIMIT),
        cost_estimate=cost(2 * nq * width * width * tok, 4 * nq * width * (tok + width)),
        name="fc",
    )(where, h2, second, *got, *other, vecs)


def proj_call(g, w_proj, x1, teacher, cotangent, weight, vecs):
    nq, tok, width = g.shape

    def kern(g_ref, w_ref, x_ref, te_ref, co_ref, wt_ref, vec_ref, y_ref, dy_ref, dm_ref, gw_ref, pb_ref, acc, keep):
        i = pl.program_id(0)

        @pl.when(i == 0)
        def _():
            acc[...] = x_ref[...] + vec_ref[7:8]

        @pl.when(i < nq)
        def _():
            keep[i] = g_ref[0]
            acc[...] += dot_nn(g_ref[0], w_ref[...])

        @pl.when(i == nq - 1)
        def _():
            y = acc[...]
            y_ref[...] = y.astype(BF)
            dy = co_ref[...].astype(F32) + wt_ref[...] * (y - te_ref[...].astype(F32))
            dy_ref[...] = dy
            dm = dy.astype(BF)
            dm_ref[...] = dm
            pb_ref[0:1, :] = jnp.sum(dm.astype(F32), axis=0, keepdims=True)
            pb_ref[1:8, :] = jnp.zeros((7, width), F32)

        @pl.when(i >= nq)
        def _():
            gw_ref[...] = dot_tn(keep[i - nq], dm_ref[...]).astype(BF)

    last = nq - 1
    return pl.pallas_call(
        kern,
        grid=(2 * nq,),
        in_specs=[
            pl.BlockSpec((1, tok, width), lambda i: (jnp.minimum(i, last), 0, 0)),
            pl.BlockSpec((width, width), lambda i: (jnp.minimum(i, last), 0)),
        ]
        + [fixed(a.shape) for a in (x1, teacher, cotangent, weight, vecs)],
        out_specs=[
            fixed((tok, width)),
            fixed((tok, width)),
            fixed((tok, width)),
            pl.BlockSpec((width, width), lambda i: (jnp.maximum(i - nq, 0), 0)),
            fixed((8, width)),
        ],
        out_shape=[
            jax.ShapeDtypeStruct((tok, width), BF),
            jax.ShapeDtypeStruct((tok, width), F32),
            jax.ShapeDtypeStruct((tok, width), BF),
            jax.ShapeDtypeStruct((nq * width, width), BF),
            jax.ShapeDtypeStruct((8, width), F32),
        ],
        scratch_shapes=[pltpu.VMEM((tok, width), F32), pltpu.VMEM((nq, tok, width), BF)],
        compiler_params=pltpu.CompilerParams(vmem_limit_bytes=VMEM_LIMIT),
        cost_estimate=cost(4 * nq * width * width * tok, 2 * nq * width * (tok + 2 * width)),
        name="proj",
    )(g, w_proj, x1, teacher, cotangent, weight, vecs)


def mid_call(dm, dy, w_proj, gp, h2, w_fc, x1, mix, second, vecs, core):
    nq, tok, width = gp.shape
    ns = second.shape[0]
    dsh = width // ns
    nz = ns // 2

    def kern(*refs):
        (co_ref, dm_ref, dy_ref, wp_ref, gp_ref, h_ref, wf_ref, x_ref, o_ref, wo_ref, vec_ref) = refs[:11]
        (fm_ref, ft_ref, om_ref, ot_ref, dx_ref, do_ref, sm_ref, fb_ref, ht, dh2) = refs[11:]
        j = pl.program_id(0)
        total = lambda m: jnp.sum(m, axis=0, keepdims=True)

        def split(gw, mine, theirs):
            gw = gw.astype(BF).reshape(nz, 2, dsh, width)
            for c in range(2):

                @pl.when(co_ref[0] == c)
                def _():
                    mine[...] = gw[:, c]
                    theirs[...] = gw[:, 1 - c]

        @pl.when(j == 0)
        def _():
            ht[...] = jnp.transpose(h_ref[...])
            dh2[...] = jnp.zeros_like(dh2)

        @pl.when(j < nq)
        def _():
            dg = dot_nt(dm_ref[...], wp_ref[...])
            df = (dg * gp_ref[0].astype(F32)).astype(BF)
            fb_ref[pl.ds(j, 1), :] = total(df.astype(F32))
            split(dot_nn(ht[...], df), fm_ref.at[0], ft_ref.at[0])
            dh2[...] += dot_nt(df, wf_ref[0])

        @pl.when(j == nq)
        def _():
            z, inv = normalize(x_ref[...])
            grad = dh2[...]
            sm_ref[0:1, :] = total(grad * z)
            sm_ref[1:2, :] = total(grad)
            dx = dy_ref[...] + norm_back(grad * vec_ref[5:6], z, inv)
            dx_ref[...] = dx
            da = dx.astype(BF)
            sm_ref[2:3, :] = total(da.astype(F32))
            do_ref[...] = dot_nt(da, wo_ref[...].reshape(width, width)).astype(BF)
            split(dot_tn(o_ref[...], da), om_ref, ot_ref)

    last = nq - 1
    pick = lambda j: (jnp.minimum(j, last), 0, 0)
    out = pl.BlockSpec((1, nz, dsh, width), lambda j: (jnp.minimum(j, last), 0, 0, 0))
    return pl.pallas_call(
        kern,
        grid=(nq + 1,),
        in_specs=[
            pl.BlockSpec(memory_space=pltpu.SMEM),
            fixed(dm.shape),
            fixed(dy.shape),
            pl.BlockSpec((width, width), lambda j: (jnp.minimum(j, last), 0)),
            pl.BlockSpec((1, tok, width), pick),
            fixed(h2.shape),
            pl.BlockSpec((1, width, width), pick),
            fixed(x1.shape),
            fixed(mix.shape),
            pl.BlockSpec((ns, dsh, width), lambda j: (0, 1, 0)),
            fixed(vecs.shape),
        ],
        out_specs=[
            out,
            out,
            fixed((nz, dsh, width)),
            fixed((nz, dsh, width)),
            fixed((tok, width)),
            fixed((tok, width)),
            fixed((8, width)),
            fixed((nq, width)),
        ],
        out_shape=[
            jax.ShapeDtypeStruct((nq, nz, dsh, width), BF),
            jax.ShapeDtypeStruct((nq, nz, dsh, width), BF),
            jax.ShapeDtypeStruct((nz, dsh, width), BF),
            jax.ShapeDtypeStruct((nz, dsh, width), BF),
            jax.ShapeDtypeStruct((tok, width), F32),
            jax.ShapeDtypeStruct((tok, width), BF),
            jax.ShapeDtypeStruct((8, width), F32),
            jax.ShapeDtypeStruct((nq, width), F32),
        ],
        scratch_shapes=[pltpu.VMEM((width, tok), BF), pltpu.VMEM((tok, width), F32)],
        compiler_params=pltpu.CompilerParams(vmem_limit_bytes=VMEM_LIMIT),
        cost_estimate=cost(
            2 * width * width * tok * (3 * nq + 2), 2 * width * (nq * (tok + 4 * width) + 8 * tok)
        ),
        name="mid",
    )(core, dm, dy, w_proj, gp, h2, w_fc, x1, mix, second, vecs)


def grads_call(h1, dq, dkv, shard, ns):
    keys, width = h1.shape
    tok = dq.shape[0]
    plen = ns * PR_DEV
    dsh = width // ns

    def kern(sh_ref, h_ref, dq_ref, d_ref, o_ref, ht):
        j = pl.program_id(0)

        @pl.when(j == 0)
        def _():
            ht[...] = jnp.transpose(h_ref[...])

        @pl.when(j < 2)
        def _():
            o_ref[...] = dot_nn(ht[...], d_ref[0]).astype(BF).reshape(ns, dsh, width)

        @pl.when(j == 2)
        def _():
            own = pl.ds(pl.multiple_of(sh_ref[0] * PR_DEV, PR_DEV), PR_DEV)
            gq = dot_nn(ht[:, plen:], dq_ref[PR_DEV:, :]) + dot_tn(h_ref[own, :], dq_ref[:PR_DEV, :])
            o_ref[...] = gq.astype(BF).reshape(ns, dsh, width)

    return pl.pallas_call(
        kern,
        grid=(3,),
        in_specs=[
            pl.BlockSpec(memory_space=pltpu.SMEM),
            fixed(h1.shape),
            fixed(dq.shape),
            pl.BlockSpec((1, keys, width), lambda j: (jnp.minimum(j, 1), 0, 0)),
        ],
        out_specs=pl.BlockSpec((ns, dsh, width), lambda j: (0, (j + 1) % 3, 0)),
        out_shape=jax.ShapeDtypeStruct((ns, 3 * dsh, width), BF),
        scratch_shapes=[pltpu.VMEM((width, keys), BF)],
        compiler_params=pltpu.CompilerParams(vmem_limit_bytes=VMEM_LIMIT),
        cost_estimate=cost(2 * width * width * (2 * keys + tok), 2 * width * 5 * keys),
        name="grads",
    )(shard, h1, dq, dkv)


def dh1_call(bundle, tokens, vecs, dq, dkv, dx1, sums, fc_sums, last, shard):
    ns, _, width = bundle.shape
    tok = tokens.shape[0]
    cont = tok - PR_DEV
    plen = ns * PR_DEV
    dsh = width // ns
    nq = fc_sums.shape[0]
    base = 3 * dsh
    step = cont // PR_DEV
    chunks = ns // step

    def kern(*refs):
        (sh_ref, g_ref, t_ref, vec_ref, dq_ref, dk_ref, dv_ref, dx_ref) = refs[:8]
        (s2_ref, fb_ref, s3_ref, o_ref, ig_ref, sm) = refs[8:]
        i = pl.program_id(0)
        wq, wk, wv = (
            g_ref[:, j * dsh : (j + 1) * dsh, :].reshape(width, width) for j in range(3)
        )
        total = lambda m: jnp.sum(m, axis=0, keepdims=True)

        @pl.when(i == 0)
        def _():
            sm[...] = jnp.zeros_like(sm)

        def add(dh, z):
            sm[0:1, :] += total(dh * z)
            sm[1:2, :] += total(dh)

        dv = dv_ref[0]
        sm[3:4, :] += total(dv.astype(F32))
        dh = dot_nt(dk_ref[0], wk) + dot_nt(dv, wv)

        @pl.when(i < chunks)
        def _():
            x = g_ref[pl.ds(i * step, step), base : base + PR_DEV, :]
            z, _ = normalize(x.reshape(cont, width).astype(F32))
            add(dh, z)
            o_ref[pl.ds(i * step, step), EXTRA:, :] = dh.astype(BF).reshape(step, PR_DEV, width)

        @pl.when(i == sh_ref[0] // step)
        def _():
            own = pl.ds(pl.multiple_of((sh_ref[0] % step) * PR_DEV, PR_DEV), PR_DEV)
            z, _ = normalize(t_ref[:PR_DEV, :].astype(F32))
            part = dot_nt(dq_ref[:PR_DEV, :], wq)
            add(part, z)
            both = dot_nt(dk_ref[0, own, :], wk) + dot_nt(dv_ref[0, own, :], wv)
            o_ref[sh_ref[0], EXTRA:, :] = (both + part).astype(BF)

        @pl.when(i == chunks)
        def _():
            z, inv = normalize(t_ref[PR_DEV:, :].astype(F32))
            full = dh + dot_nt(dq_ref[PR_DEV:, :], wq)
            add(full, z)
            ig_ref[PR_DEV:, :] = dx_ref[PR_DEV:, :] + norm_back(full * vec_ref[0:1], z, inv)
            ig_ref[:PR_DEV, :] = dx_ref[:PR_DEV, :]
            sm[2:3, :] = total(dq_ref[...].astype(F32))
            sm[4:5, :] = s2_ref[2:3, :]
            sm[5:7, :] = s2_ref[0:2, :]
            sm[7:8, :] = s3_ref[0:1, :]
            sm[8 : 8 + nq, :] = fb_ref[...]
            small = sm[...].astype(BF)
            for b in range(ns):
                o_ref[b, :EXTRA, :] = small

    chunk = lambda k: pl.BlockSpec((1, cont, width), lambda i: (k, i, 0))
    out = (ns, EXTRA + PR_DEV, width)
    return pl.pallas_call(
        kern,
        grid=(chunks + 1,),
        in_specs=[
            pl.BlockSpec(memory_space=pltpu.SMEM),
            fixed(bundle.shape),
            fixed(tokens.shape),
            fixed(vecs.shape),
            fixed(dq.shape),
            chunk(0),
            chunk(1),
        ]
        + [fixed(a.shape) for a in (dx1, sums, fc_sums, last)],
        out_specs=[fixed(out), fixed((tok, width))],
        out_shape=[jax.ShapeDtypeStruct(out, BF), jax.ShapeDtypeStruct((tok, width), F32)],
        scratch_shapes=[pltpu.VMEM((EXTRA, width), F32)],
        compiler_params=pltpu.CompilerParams(vmem_limit_bytes=VMEM_LIMIT),
        cost_estimate=cost(
            2 * width * width * (2 * (plen + cont) + tok), 2 * width * (5 * plen + 10 * cont)
        ),
        name="dh1",
    )(shard, bundle, tokens, vecs, dq, dkv, dkv, dx1, sums, fc_sums, last)


def finish_call(grad, summed, tokens, vecs):
    tok, width = grad.shape

    def kern(g_ref, s_ref, t_ref, vec_ref, o_ref):
        z, inv = normalize(t_ref[...].astype(F32))
        e = s_ref[...].astype(F32) * vec_ref[0:1]
        o_ref[...] = g_ref[...] + norm_back(e, z, inv)

    block = pl.BlockSpec((PR_DEV, width), lambda i: (0, 0))
    return pl.pallas_call(
        kern,
        grid=(1,),
        in_specs=[block, block, block, pl.BlockSpec(vecs.shape, lambda i: (0, 0))],
        out_specs=block,
        out_shape=jax.ShapeDtypeStruct((tok, width), F32),
        input_output_aliases={0: 0},
        cost_estimate=cost(20 * PR_DEV * width, 12 * PR_DEV * width),
        name="finish",
    )(grad, summed, tokens, vecs)


def over(axis, values, bit):
    n = lax.axis_size(axis)
    return lax.ppermute(values, axis, [(i, i ^ bit) for i in range(n)])


def rep_sum(values):
    n = lax.axis_size("rep")
    bits = [1 << b for b in range(n.bit_length() - 1)]
    cut = values.shape[0] // 2
    halves = [values[:cut], values[cut:]]
    for i in range(len(bits)):
        steps = (bits[i], bits[-1 - i])
        got = [over("rep", v, b) for v, b in zip(halves, steps)]
        halves = [(v.astype(F32) + g.astype(F32)).astype(v.dtype) for v, g in zip(halves, got)]
    return jnp.concatenate(halves)


def local(
    tokens,
    ln1_gain,
    ln1_bias,
    w_qkv,
    qv_bias,
    w_out,
    out_bias,
    ln2_gain,
    ln2_bias,
    w_fc,
    fc_bias,
    w_proj,
    proj_bias,
    teacher,
    cotangent,
    valid_mask,
):
    ns = lax.axis_size("shard")
    nr = lax.axis_size("rep")
    me = lax.axis_index("shard").astype(jnp.int32)
    shard = me.reshape(1)
    tok, width = tokens.shape
    nq = min(nr, w_fc.shape[1] // width)
    group = lax.axis_index("rep").astype(jnp.int32) % nq
    dsh = width // ns
    rb = 256

    bundle = lax.all_gather(
        jnp.concatenate(
            [w_qkv[:, :width], w_qkv[:, width : 2 * width], w_qkv[:, 2 * width :], tokens[:PR_DEV]]
        ),
        "shard",
    )
    fc_own = lax.dynamic_slice_in_dim(w_fc, group * width, width, 1)
    second = lax.all_gather(jnp.concatenate([fc_own, w_out]), "shard")
    full_proj = lax.all_gather(w_proj, "shard", axis=0, tiled=True)

    mask_f = valid_mask.astype(F32)
    counts = jnp.sum(mask_f.reshape(-1, PR_DEV), axis=1).astype(BF)
    parts = [ln1_gain, ln1_bias, qv_bias, out_bias, ln2_gain, ln2_bias, proj_bias, fc_bias]
    offs = [0]
    for p in parts:
        offs.append(offs[-1] + p.shape[0])
    packed = jnp.concatenate(parts + [counts])
    packed = jnp.pad(packed, (0, (-packed.shape[0]) % 128))
    params = lax.all_gather(packed.reshape(1, -1), "shard", axis=0, tiled=True).astype(F32)
    vecs = jnp.concatenate(
        [params[:, offs[i] : offs[i + 1]].reshape(-1, width) for i in range(8)]
        + [jnp.zeros((16 - 8 - nq, width), F32)]
    )
    count = jnp.sum(params[:, offs[8] : offs[8] + counts.shape[0]])
    token_total = rep_sum(jnp.full((16, 128), count, F32))[0, 0]
    factor = tok * nr * ns / token_total
    weight = (factor * mask_f).reshape(tok, 1)

    h1, q, k, v = qkv_call(bundle, tokens, vecs, shard)
    mix, lse = attn_fwd(q, k, v, shard, rb)
    x1, h2 = out_proj_call(mix, second, tokens, vecs)

    core = me % 2
    piece = lax.dynamic_slice_in_dim(second, core * (ns // 2), ns // 2, 0)[:, :dsh]
    got = [over("rep", piece, j) for j in range(1, nq)]
    other = [over("shard", g, 1) for g in got]
    g, gp, full_fc = fc_call(h2, second, got, other, vecs, jnp.stack([group, core]))
    out, dy, dm, grad_proj, last = proj_call(g, full_proj, x1, teacher, cotangent, weight, vecs)
    own_proj = lax.psum_scatter(grad_proj, "shard", scatter_dimension=0, tiled=True)
    fc_mine, fc_theirs, out_mine, out_theirs, dx1, do, sums, fc_sums = mid_call(
        dm, dy, full_proj, gp, h2, full_fc, x1, mix, second, vecs, core.reshape(1)
    )
    dq, dkv = attn_bwd(q, k, v, mix, do, lse, shard, rb)

    plus = lambda *terms: sum(t.astype(F32) for t in terms).astype(BF)
    nz = ns // 2
    fc_half = plus(fc_mine, over("shard", fc_theirs, 1))
    out_half = plus(out_mine, over("shard", out_theirs, 1))
    out_half = jnp.swapaxes(out_half.reshape(nz, nq, dsh // nq, width), 0, 1)
    pair = jnp.concatenate([fc_half, out_half], axis=2)

    dq, dkv, own_proj, pair = lax.optimization_barrier((dq, dkv, own_proj, pair))
    grads = grads_call(h1, dq, dkv, shard, ns)
    own_qkv = lax.psum_scatter(grads.reshape(-1, width), "shard", scatter_dimension=0, tiled=True)
    dq, dkv, grads = lax.optimization_barrier((dq, dkv, grads))
    last_part, ig = dh1_call(bundle, tokens, vecs, dq, dkv, dx1, sums, fc_sums, last, shard)
    last_part, own_qkv = lax.optimization_barrier((last_part, own_qkv))
    own = lax.psum_scatter(last_part.reshape(-1, width), "shard", scatter_dimension=0, tiled=True)
    input_grad = finish_call(ig, own[EXTRA:], tokens, vecs)

    pick = lambda a, n: lax.dynamic_index_in_dim(a, n, 0, keepdims=False)
    quarter = plus(
        pick(pair, group),
        *[over("rep", pick(pair, jnp.bitwise_xor(group, b)), b) for b in range(1, nq)],
    )
    z = me // 2
    final = plus(
        pick(quarter, z),
        *[over("shard", pick(quarter, jnp.bitwise_xor(z, b)), 2 * b) for b in range(1, nz)],
    )
    bit = nq
    while bit < nr:
        final = plus(final, over("rep", final, bit))
        bit *= 2
    relative = jnp.stack([final] + [over("rep", final, b) for b in range(1, nq)])
    natural = [pick(relative, jnp.bitwise_xor(group, b)) for b in range(nq)]
    sum_fc = jnp.concatenate([n[:dsh] for n in natural], axis=1).astype(F32)
    sum_out = jnp.concatenate([n[dsh:] for n in natural], axis=0).astype(F32)

    sum_proj = rep_sum(own_proj).astype(F32)
    sum_qkv = rep_sum(own_qkv).astype(F32)
    small = rep_sum(own[:EXTRA]).astype(F32)

    def take(first, rows):
        n = rows * dsh
        return lax.dynamic_slice_in_dim(small[first : first + rows].reshape(-1), me * n, n)

    return (
        out,
        input_grad,
        take(0, 1),
        take(1, 1),
        jnp.concatenate([sum_qkv[j * dsh : (j + 1) * dsh] for j in range(3)], axis=1),
        take(2, 2),
        sum_out,
        take(4, 1),
        take(5, 1),
        take(6, 1),
        sum_fc,
        take(8, nq),
        sum_proj,
        take(7, 1),
    )


def solution(mesh):
    rows = P(("rep", "shard"), None)
    mat = P("shard", None)
    vec = P("shard")
    return jax.shard_map(
        local,
        mesh=mesh,
        in_specs=(
            rows,
            vec,
            vec,
            mat,
            vec,
            mat,
            vec,
            vec,
            vec,
            mat,
            vec,
            mat,
            vec,
            rows,
            rows,
            P(("rep", "shard")),
        ),
        out_specs=(rows, rows, vec, vec, mat, vec, mat, vec, vec, vec, mat, vec, mat, vec),
        check_vma=False,
    )
```

```python
import jax
import jax.numpy as jnp
from jax import lax
from jax.experimental import pallas as pl
from jax.experimental.pallas import tpu as pltpu
from jax.sharding import PartitionSpec as P

F32 = jnp.float32
BF = jnp.bfloat16
HEAD = 64
PR_DEV = 128
PAIR = 2 * HEAD
SCALE = 0.125
EPS = 1e-05
NEG = -1e30
VMEM_LIMIT = 60 * 1024 * 1024
EXTRA = 16


def dot_nt(a, b):
    return lax.dot_general(a, b, (((1,), (1,)), ((), ())), preferred_element_type=F32)


def dot_nn(a, b):
    return lax.dot_general(a, b, (((1,), (0,)), ((), ())), preferred_element_type=F32)


def dot_tn(a, b):
    return lax.dot_general(a, b, (((0,), (0,)), ((), ())), preferred_element_type=F32)


def normalize(values):
    centered = values - jnp.mean(values, axis=-1, keepdims=True)
    inv = lax.rsqrt(jnp.mean(centered * centered, axis=-1, keepdims=True) + EPS)
    return centered * inv, inv


def norm_back(e, z, inv):
    return inv * (
        e - jnp.mean(e, axis=-1, keepdims=True) - z * jnp.mean(e * z, axis=-1, keepdims=True)
    )


def cost(flops, nbytes, trans=0):
    return pl.CostEstimate(flops=int(flops), bytes_accessed=int(nbytes), transcendentals=int(trans))


def fixed(shape):
    return pl.BlockSpec(shape, lambda *_: (0,) * len(shape))


def qkv_call(bundle, tokens, vecs, shard):
    ns, _, width = bundle.shape
    tok = tokens.shape[0]
    cont = tok - PR_DEV
    plen = ns * PR_DEV
    keys = plen + cont
    dsh = width // ns

    def kern(sh_ref, g_ref, t_ref, vec_ref, h_ref, q_ref, k_ref, v_ref):
        gain, bias, bq, bv = vec_ref[0:1], vec_ref[1:2], vec_ref[2:3], vec_ref[3:4]
        wq, wk, wv = (
            g_ref[:, j * dsh : (j + 1) * dsh, :].reshape(width, width) for j in range(3)
        )
        step = 4

        def chunk(x, r0):
            h = (normalize(x.astype(F32))[0] * gain + bias).astype(BF)
            rows = pl.ds(r0, h.shape[0])
            h_ref[rows, :] = h
            k_ref[rows, :] = dot_nn(h, wk).astype(BF)
            v_ref[rows, :] = (dot_nn(h, wv) + bv).astype(BF)

        def to_q(h):
            return ((dot_nn(h, wq) + bq).astype(BF).astype(F32) * SCALE).astype(BF)

        for b in range(0, ns, step):
            x = g_ref[b : b + step, 3 * dsh : 3 * dsh + PR_DEV, :]
            chunk(x.reshape(x.shape[0] * PR_DEV, width), b * PR_DEV)
        chunk(t_ref[PR_DEV:, :], plen)
        own = pl.multiple_of(sh_ref[0] * PR_DEV, PR_DEV)
        q_ref[:PR_DEV, :] = to_q(h_ref[pl.ds(own, PR_DEV), :])
        q_ref[PR_DEV:, :] = to_q(h_ref[plen:, :])

    shape = lambda r: jax.ShapeDtypeStruct((r, width), BF)
    vm = pl.BlockSpec(memory_space=pltpu.VMEM)
    return pl.pallas_call(
        kern,
        in_specs=[pl.BlockSpec(memory_space=pltpu.SMEM), vm, vm, vm],
        out_specs=[vm] * 4,
        out_shape=[shape(keys), shape(tok), shape(keys), shape(keys)],
        compiler_params=pltpu.CompilerParams(vmem_limit_bytes=VMEM_LIMIT),
        cost_estimate=cost(2 * width * width * (2 * keys + tok), 2 * width * (6 * keys)),
        name="qkv",
    )(shard, bundle, tokens, vecs)


def attn_fwd(q, k, v, shard, rb):
    tok, width = q.shape
    keys = k.shape[0]
    cont = tok - PR_DEV
    plen = keys - cont
    npair = width // PAIR

    def kern(sh_ref, q_ref, k_ref, v_ref, o_ref, lse_ref):
        sh = sh_ref[0]
        first = lax.broadcasted_iota(jnp.int32, (1, PAIR), 1) < HEAD

        def block(r0, rows, n, offset, masked):
            outs, lses = [], []
            for h in range(2):
                mine = first if h == 0 else jnp.logical_not(first)
                qq = jnp.where(mine, q_ref[pl.ds(r0, rows), :], 0).astype(BF)
                s = dot_nt(qq, k_ref[pl.ds(0, n), :])
                tail = s[:, n - masked :]
                row = lax.broadcasted_iota(jnp.int32, tail.shape, 0)
                col = lax.broadcasted_iota(jnp.int32, tail.shape, 1)
                tail = jnp.where(col <= row + offset, tail, NEG)
                s = tail if masked == n else jnp.concatenate([s[:, : n - masked], tail], axis=1)
                top = jnp.max(s, axis=1, keepdims=True)
                p = jnp.exp(s - top)
                total = jnp.sum(p, axis=1, keepdims=True)
                outs.append(dot_nn(p.astype(BF), v_ref[pl.ds(0, n), :]) * (1.0 / total))
                lses.append(top + jnp.log(total))
            o_ref[pl.ds(r0, rows), :] = jnp.where(first, outs[0], outs[1]).astype(BF)
            turned = jnp.transpose(jnp.where(first, lses[0], lses[1]))
            lse_ref[0, 0:1, pl.ds(r0, rows)] = turned[0:1]
            lse_ref[0, 1:2, pl.ds(r0, rows)] = turned[HEAD : HEAD + 1]

        block(0, PR_DEV, plen, sh * PR_DEV, plen)
        for i in range(cont // rb):
            block(PR_DEV + i * rb, rb, plen + (i + 1) * rb, 0, rb)

    spq = pl.BlockSpec((tok, PAIR), lambda i: (0, i))
    spk = pl.BlockSpec((keys, PAIR), lambda i: (0, i))
    return pl.pallas_call(
        kern,
        grid=(npair,),
        in_specs=[pl.BlockSpec(memory_space=pltpu.SMEM), spq, spk, spk],
        out_specs=[spq, pl.BlockSpec((1, 2, tok), lambda i: (i, 0, 0))],
        out_shape=[
            jax.ShapeDtypeStruct((tok, width), BF),
            jax.ShapeDtypeStruct((npair, 2, tok), F32),
        ],
        compiler_params=pltpu.CompilerParams(vmem_limit_bytes=VMEM_LIMIT),
        cost_estimate=cost(16 * width * tok * keys, 4 * width * (tok + keys)),
        name="attn_fwd",
    )(shard, q, k, v)


def attn_bwd(q, k, v, o, do, lse, shard, rb):
    tok, width = q.shape
    keys = k.shape[0]
    cont = tok - PR_DEV
    plen = keys - cont
    npair = width // PAIR

    def kern(sh_ref, q_ref, k_ref, v_ref, o_ref, do_ref, lse_ref, dq_ref, dkv_ref, ka, va):
        sh = sh_ref[0]
        first = lax.broadcasted_iota(jnp.int32, (1, PAIR), 1) < HEAD
        ka[...] = jnp.zeros_like(ka)
        va[...] = jnp.zeros_like(va)
        hr = lax.broadcasted_iota(jnp.int32, (8, PAIR), 0)
        hc = lax.broadcasted_iota(jnp.int32, (8, PAIR), 1)
        pick = jnp.where(hc // HEAD == hr, 1.0, 0.0).astype(F32)

        def block(r0, rows, n, offset, masked):
            prod = o_ref[pl.ds(r0, rows), :].astype(F32) * do_ref[pl.ds(r0, rows), :].astype(F32)
            row_dot = lax.dot_general(
                pick,
                prod,
                (((1,), (1,)), ((), ())),
                precision=lax.Precision.HIGHEST,
                preferred_element_type=F32,
            )
            dqs = []
            for h in range(2):
                mine = first if h == 0 else jnp.logical_not(first)
                qq = jnp.where(mine, q_ref[pl.ds(r0, rows), :], 0).astype(BF)
                gg = jnp.where(mine, do_ref[pl.ds(r0, rows), :], 0).astype(BF)
                kk = k_ref[pl.ds(0, n), :]
                s = dot_nt(kk, qq)
                tail = s[n - masked :]
                col = lax.broadcasted_iota(jnp.int32, tail.shape, 0)
                row = lax.broadcasted_iota(jnp.int32, tail.shape, 1)
                tail = jnp.where(col <= row + offset, tail, NEG)
                s = tail if masked == n else jnp.concatenate([s[: n - masked], tail], axis=0)
                p = jnp.exp(s - lse_ref[0, h : h + 1, pl.ds(r0, rows)])
                dp = dot_nt(v_ref[pl.ds(0, n), :], gg)
                ds = (p * (dp - row_dot[h : h + 1, :])).astype(BF)
                va[pl.ds(0, n), :] += dot_nn(p.astype(BF), gg)
                ka[pl.ds(0, n), :] += dot_nn(ds, qq)
                dqs.append(dot_tn(ds, kk))
            dq_ref[pl.ds(r0, rows), :] = (jnp.where(first, dqs[0], dqs[1]) * SCALE).astype(BF)

        block(0, PR_DEV, plen, sh * PR_DEV, plen)
        for i in range(cont // rb):
            block(PR_DEV + i * rb, rb, plen + (i + 1) * rb, 0, rb)
        dkv_ref[0] = ka[...].astype(BF)
        dkv_ref[1] = va[...].astype(BF)

    spq = pl.BlockSpec((tok, PAIR), lambda i: (0, i))
    spk = pl.BlockSpec((keys, PAIR), lambda i: (0, i))
    return pl.pallas_call(
        kern,
        grid=(npair,),
        in_specs=[
            pl.BlockSpec(memory_space=pltpu.SMEM),
            spq,
            spk,
            spk,
            spq,
            spq,
            pl.BlockSpec((1, 2, tok), lambda i: (i, 0, 0)),
        ],
        out_specs=[spq, pl.BlockSpec((2, keys, PAIR), lambda i: (0, 0, i))],
        out_shape=[
            jax.ShapeDtypeStruct((tok, width), BF),
            jax.ShapeDtypeStruct((2, keys, width), BF),
        ],
        scratch_shapes=[pltpu.VMEM((keys, PAIR), F32), pltpu.VMEM((keys, PAIR), F32)],
        compiler_params=pltpu.CompilerParams(vmem_limit_bytes=VMEM_LIMIT),
        cost_estimate=cost(40 * width * tok * keys, 8 * width * (tok + keys)),
        name="attn_bwd",
    )(shard, q, k, v, o, do, lse)


def out_proj_call(mix, second, tokens, vecs):
    ns, _, width = second.shape
    tok = tokens.shape[0]
    dsh = width // ns

    def kern(o_ref, w_ref, t_ref, vec_ref, x_ref, h_ref):
        wo = w_ref[...].reshape(width, width)
        x1 = t_ref[...].astype(F32) + (dot_nn(o_ref[...], wo) + vec_ref[4:5])
        x_ref[...] = x1
        h_ref[...] = (normalize(x1)[0] * vec_ref[5:6] + vec_ref[6:7]).astype(BF)

    whole = lambda a: pl.BlockSpec(a.shape, lambda i: (0,) * a.ndim)
    return pl.pallas_call(
        kern,
        grid=(1,),
        in_specs=[
            whole(mix),
            pl.BlockSpec((ns, dsh, width), lambda i: (0, 1, 0)),
            whole(tokens),
            whole(vecs),
        ],
        out_specs=[pl.BlockSpec((tok, width), lambda i: (0, 0))] * 2,
        out_shape=[jax.ShapeDtypeStruct((tok, width), F32), jax.ShapeDtypeStruct((tok, width), BF)],
        compiler_params=pltpu.CompilerParams(vmem_limit_bytes=VMEM_LIMIT),
        cost_estimate=cost(2 * width * width * tok, 12 * width * tok),
        name="out_proj",
    )(mix, second, tokens, vecs)


def fc_call(h2, second, got, other, vecs, where):
    ns, _, width = second.shape
    tok = h2.shape[0]
    dsh = width // ns
    half = ns // 2
    nq = len(got) + 1

    def kern(*refs):
        wh_ref, h_ref, own_ref = refs[:3]
        got_refs = refs[3 : 2 + nq]
        other_refs = refs[2 + nq : 1 + 2 * nq]
        vec_ref, g_ref, gp_ref, w_ref = refs[1 + 2 * nq :]
        me, core = wh_ref[0], wh_ref[1]
        step = pl.program_id(0)
        rows = half * dsh

        @pl.when(step == 0)
        def _():
            w_ref[0] = own_ref[...].reshape(width, width)

        for j in range(1, nq):

            @pl.when(step == j)
            def _():
                first = pl.multiple_of(core * rows, rows)
                second_half = pl.multiple_of((1 - core) * rows, rows)
                w_ref[0, pl.ds(first, rows), :] = got_refs[j - 1][...].reshape(rows, width)
                w_ref[0, pl.ds(second_half, rows), :] = other_refs[j - 1][...].reshape(rows, width)

        c = jnp.bitwise_xor(me, step)
        f = dot_nn(h_ref[...], w_ref[0]) + vec_ref[pl.ds(8 + c, 1), :]
        square = f * f
        t = jnp.tanh(0.7978845608028654 * f * (1.0 + 0.044715 * square))
        up = 0.5 * (1.0 + t)
        g_ref[0] = (f * up).astype(BF)
        slope = 0.5 * f * (1.0 - t * t) * (0.7978845608028654 + 0.1070322243 * square)
        gp_ref[0] = (up + slope).astype(BF)

    pick = lambda j, wh: (jnp.bitwise_xor(wh[0], j), 0, 0)
    return pl.pallas_call(
        kern,
        grid_spec=pltpu.PrefetchScalarGridSpec(
            num_scalar_prefetch=1,
            grid=(nq,),
            in_specs=[fixed(h2.shape), fixed((ns, dsh, width))]
            + [fixed(a.shape) for a in got]
            + [fixed(a.shape) for a in other]
            + [fixed(vecs.shape)],
            out_specs=[
                pl.BlockSpec((1, tok, width), pick),
                pl.BlockSpec((1, tok, width), pick),
                pl.BlockSpec((1, width, width), pick),
            ],
        ),
        out_shape=[
            jax.ShapeDtypeStruct((nq, tok, width), BF),
            jax.ShapeDtypeStruct((nq, tok, width), BF),
            jax.ShapeDtypeStruct((nq, width, width), BF),
        ],
        compiler_params=pltpu.CompilerParams(vmem_limit_bytes=VMEM_LIMIT),
        cost_estimate=cost(2 * nq * width * width * tok, 4 * nq * width * (tok + width)),
        name="fc",
    )(where, h2, second, *got, *other, vecs)


def proj_call(g, w_proj, x1, teacher, cotangent, weight, vecs):
    nq, tok, width = g.shape

    def kern(g_ref, w_ref, x_ref, te_ref, co_ref, wt_ref, vec_ref, y_ref, dy_ref, dm_ref, gw_ref, pb_ref, acc, keep):
        i = pl.program_id(0)

        @pl.when(i == 0)
        def _():
            acc[...] = x_ref[...] + vec_ref[7:8]

        @pl.when(i < nq)
        def _():
            keep[i] = g_ref[0]
            acc[...] += dot_nn(g_ref[0], w_ref[...])

        @pl.when(i == nq - 1)
        def _():
            y = acc[...]
            y_ref[...] = y.astype(BF)
            dy = co_ref[...].astype(F32) + wt_ref[...] * (y - te_ref[...].astype(F32))
            dy_ref[...] = dy
            dm = dy.astype(BF)
            dm_ref[...] = dm
            pb_ref[0:1, :] = jnp.sum(dm.astype(F32), axis=0, keepdims=True)
            pb_ref[1:8, :] = jnp.zeros((7, width), F32)

        @pl.when(i >= nq)
        def _():
            gw_ref[...] = dot_tn(keep[i - nq], dm_ref[...]).astype(BF)

    last = nq - 1
    return pl.pallas_call(
        kern,
        grid=(2 * nq,),
        in_specs=[
            pl.BlockSpec((1, tok, width), lambda i: (jnp.minimum(i, last), 0, 0)),
            pl.BlockSpec((width, width), lambda i: (jnp.minimum(i, last), 0)),
        ]
        + [fixed(a.shape) for a in (x1, teacher, cotangent, weight, vecs)],
        out_specs=[
            fixed((tok, width)),
            fixed((tok, width)),
            fixed((tok, width)),
            pl.BlockSpec((width, width), lambda i: (jnp.maximum(i - nq, 0), 0)),
            fixed((8, width)),
        ],
        out_shape=[
            jax.ShapeDtypeStruct((tok, width), BF),
            jax.ShapeDtypeStruct((tok, width), F32),
            jax.ShapeDtypeStruct((tok, width), BF),
            jax.ShapeDtypeStruct((nq * width, width), BF),
            jax.ShapeDtypeStruct((8, width), F32),
        ],
        scratch_shapes=[pltpu.VMEM((tok, width), F32), pltpu.VMEM((nq, tok, width), BF)],
        compiler_params=pltpu.CompilerParams(vmem_limit_bytes=VMEM_LIMIT),
        cost_estimate=cost(4 * nq * width * width * tok, 2 * nq * width * (tok + 2 * width)),
        name="proj",
    )(g, w_proj, x1, teacher, cotangent, weight, vecs)


def mid_call(dm, dy, w_proj, gp, h2, w_fc, x1, mix, second, vecs, core):
    nq, tok, width = gp.shape
    ns = second.shape[0]
    dsh = width // ns
    nz = ns // 2

    def kern(*refs):
        (co_ref, dm_ref, dy_ref, wp_ref, gp_ref, h_ref, wf_ref, x_ref, o_ref, wo_ref, vec_ref) = refs[:11]
        (fm_ref, ft_ref, om_ref, ot_ref, dx_ref, do_ref, sm_ref, fb_ref, ht, dh2) = refs[11:]
        j = pl.program_id(0)
        total = lambda m: jnp.sum(m, axis=0, keepdims=True)

        def split(gw, mine, theirs):
            gw = gw.astype(BF).reshape(nz, 2, dsh, width)
            for c in range(2):

                @pl.when(co_ref[0] == c)
                def _():
                    mine[...] = gw[:, c]
                    theirs[...] = gw[:, 1 - c]

        @pl.when(j == 0)
        def _():
            ht[...] = jnp.transpose(h_ref[...])
            dh2[...] = jnp.zeros_like(dh2)

        @pl.when(j < nq)
        def _():
            dg = dot_nt(dm_ref[...], wp_ref[...])
            df = (dg * gp_ref[0].astype(F32)).astype(BF)
            fb_ref[pl.ds(j, 1), :] = total(df.astype(F32))
            split(dot_nn(ht[...], df), fm_ref.at[0], ft_ref.at[0])
            dh2[...] += dot_nt(df, wf_ref[0])

        @pl.when(j == nq)
        def _():
            z, inv = normalize(x_ref[...])
            grad = dh2[...]
            sm_ref[0:1, :] = total(grad * z)
            sm_ref[1:2, :] = total(grad)
            dx = dy_ref[...] + norm_back(grad * vec_ref[5:6], z, inv)
            dx_ref[...] = dx
            da = dx.astype(BF)
            sm_ref[2:3, :] = total(da.astype(F32))
            do_ref[...] = dot_nt(da, wo_ref[...].reshape(width, width)).astype(BF)
            split(dot_tn(o_ref[...], da), om_ref, ot_ref)

    last = nq - 1
    pick = lambda j: (jnp.minimum(j, last), 0, 0)
    out = pl.BlockSpec((1, nz, dsh, width), lambda j: (jnp.minimum(j, last), 0, 0, 0))
    return pl.pallas_call(
        kern,
        grid=(nq + 1,),
        in_specs=[
            pl.BlockSpec(memory_space=pltpu.SMEM),
            fixed(dm.shape),
            fixed(dy.shape),
            pl.BlockSpec((width, width), lambda j: (jnp.minimum(j, last), 0)),
            pl.BlockSpec((1, tok, width), pick),
            fixed(h2.shape),
            pl.BlockSpec((1, width, width), pick),
            fixed(x1.shape),
            fixed(mix.shape),
            pl.BlockSpec((ns, dsh, width), lambda j: (0, 1, 0)),
            fixed(vecs.shape),
        ],
        out_specs=[
            out,
            out,
            fixed((nz, dsh, width)),
            fixed((nz, dsh, width)),
            fixed((tok, width)),
            fixed((tok, width)),
            fixed((8, width)),
            fixed((nq, width)),
        ],
        out_shape=[
            jax.ShapeDtypeStruct((nq, nz, dsh, width), BF),
            jax.ShapeDtypeStruct((nq, nz, dsh, width), BF),
            jax.ShapeDtypeStruct((nz, dsh, width), BF),
            jax.ShapeDtypeStruct((nz, dsh, width), BF),
            jax.ShapeDtypeStruct((tok, width), F32),
            jax.ShapeDtypeStruct((tok, width), BF),
            jax.ShapeDtypeStruct((8, width), F32),
            jax.ShapeDtypeStruct((nq, width), F32),
        ],
        scratch_shapes=[pltpu.VMEM((width, tok), BF), pltpu.VMEM((tok, width), F32)],
        compiler_params=pltpu.CompilerParams(vmem_limit_bytes=VMEM_LIMIT),
        cost_estimate=cost(
            2 * width * width * tok * (3 * nq + 2), 2 * width * (nq * (tok + 4 * width) + 8 * tok)
        ),
        name="mid",
    )(core, dm, dy, w_proj, gp, h2, w_fc, x1, mix, second, vecs)


def grads_call(h1, dq, dkv, shard, ns):
    keys, width = h1.shape
    tok = dq.shape[0]
    plen = ns * PR_DEV
    dsh = width // ns

    def kern(sh_ref, h_ref, dq_ref, d_ref, o_ref, ht):
        j = pl.program_id(0)

        @pl.when(j == 0)
        def _():
            ht[...] = jnp.transpose(h_ref[...])

        @pl.when(j < 2)
        def _():
            o_ref[...] = dot_nn(ht[...], d_ref[0]).astype(BF).reshape(ns, dsh, width)

        @pl.when(j == 2)
        def _():
            own = pl.ds(pl.multiple_of(sh_ref[0] * PR_DEV, PR_DEV), PR_DEV)
            gq = dot_nn(ht[:, plen:], dq_ref[PR_DEV:, :]) + dot_tn(h_ref[own, :], dq_ref[:PR_DEV, :])
            o_ref[...] = gq.astype(BF).reshape(ns, dsh, width)

    return pl.pallas_call(
        kern,
        grid=(3,),
        in_specs=[
            pl.BlockSpec(memory_space=pltpu.SMEM),
            fixed(h1.shape),
            fixed(dq.shape),
            pl.BlockSpec((1, keys, width), lambda j: (jnp.minimum(j, 1), 0, 0)),
        ],
        out_specs=pl.BlockSpec((ns, dsh, width), lambda j: (0, (j + 1) % 3, 0)),
        out_shape=jax.ShapeDtypeStruct((ns, 3 * dsh, width), BF),
        scratch_shapes=[pltpu.VMEM((width, keys), BF)],
        compiler_params=pltpu.CompilerParams(vmem_limit_bytes=VMEM_LIMIT),
        cost_estimate=cost(2 * width * width * (2 * keys + tok), 2 * width * 5 * keys),
        name="grads",
    )(shard, h1, dq, dkv)


def dh1_call(bundle, tokens, vecs, dq, dkv, dx1, sums, fc_sums, last, shard):
    ns, _, width = bundle.shape
    tok = tokens.shape[0]
    cont = tok - PR_DEV
    plen = ns * PR_DEV
    dsh = width // ns
    nq = fc_sums.shape[0]
    base = 3 * dsh
    step = cont // PR_DEV
    chunks = ns // step

    def kern(*refs):
        (sh_ref, g_ref, t_ref, vec_ref, dq_ref, dk_ref, dv_ref, dx_ref) = refs[:8]
        (s2_ref, fb_ref, s3_ref, o_ref, ig_ref, sm) = refs[8:]
        i = pl.program_id(0)
        wq, wk, wv = (
            g_ref[:, j * dsh : (j + 1) * dsh, :].reshape(width, width) for j in range(3)
        )
        total = lambda m: jnp.sum(m, axis=0, keepdims=True)

        @pl.when(i == 0)
        def _():
            sm[...] = jnp.zeros_like(sm)

        def add(dh, z):
            sm[0:1, :] += total(dh * z)
            sm[1:2, :] += total(dh)

        dv = dv_ref[0]
        sm[3:4, :] += total(dv.astype(F32))
        dh = dot_nt(dk_ref[0], wk) + dot_nt(dv, wv)

        @pl.when(i < chunks)
        def _():
            x = g_ref[pl.ds(i * step, step), base : base + PR_DEV, :]
            z, _ = normalize(x.reshape(cont, width).astype(F32))
            add(dh, z)
            o_ref[pl.ds(i * step, step), EXTRA:, :] = dh.astype(BF).reshape(step, PR_DEV, width)

        @pl.when(i == sh_ref[0] // step)
        def _():
            own = pl.ds(pl.multiple_of((sh_ref[0] % step) * PR_DEV, PR_DEV), PR_DEV)
            z, _ = normalize(t_ref[:PR_DEV, :].astype(F32))
            part = dot_nt(dq_ref[:PR_DEV, :], wq)
            add(part, z)
            both = dot_nt(dk_ref[0, own, :], wk) + dot_nt(dv_ref[0, own, :], wv)
            o_ref[sh_ref[0], EXTRA:, :] = (both + part).astype(BF)

        @pl.when(i == chunks)
        def _():
            z, inv = normalize(t_ref[PR_DEV:, :].astype(F32))
            full = dh + dot_nt(dq_ref[PR_DEV:, :], wq)
            add(full, z)
            ig_ref[PR_DEV:, :] = dx_ref[PR_DEV:, :] + norm_back(full * vec_ref[0:1], z, inv)
            ig_ref[:PR_DEV, :] = dx_ref[:PR_DEV, :]
            sm[2:3, :] = total(dq_ref[...].astype(F32))
            sm[4:5, :] = s2_ref[2:3, :]
            sm[5:7, :] = s2_ref[0:2, :]
            sm[7:8, :] = s3_ref[0:1, :]
            sm[8 : 8 + nq, :] = fb_ref[...]
            small = sm[...].astype(BF)
            for b in range(ns):
                o_ref[b, :EXTRA, :] = small

    chunk = lambda k: pl.BlockSpec((1, cont, width), lambda i: (k, i, 0))
    out = (ns, EXTRA + PR_DEV, width)
    return pl.pallas_call(
        kern,
        grid=(chunks + 1,),
        in_specs=[
            pl.BlockSpec(memory_space=pltpu.SMEM),
            fixed(bundle.shape),
            fixed(tokens.shape),
            fixed(vecs.shape),
            fixed(dq.shape),
            chunk(0),
            chunk(1),
        ]
        + [fixed(a.shape) for a in (dx1, sums, fc_sums, last)],
        out_specs=[fixed(out), fixed((tok, width))],
        out_shape=[jax.ShapeDtypeStruct(out, BF), jax.ShapeDtypeStruct((tok, width), F32)],
        scratch_shapes=[pltpu.VMEM((EXTRA, width), F32)],
        compiler_params=pltpu.CompilerParams(vmem_limit_bytes=VMEM_LIMIT),
        cost_estimate=cost(
            2 * width * width * (2 * (plen + cont) + tok), 2 * width * (5 * plen + 10 * cont)
        ),
        name="dh1",
    )(shard, bundle, tokens, vecs, dq, dkv, dkv, dx1, sums, fc_sums, last)


def finish_call(grad, summed, tokens, vecs):
    tok, width = grad.shape

    def kern(g_ref, s_ref, t_ref, vec_ref, o_ref):
        z, inv = normalize(t_ref[...].astype(F32))
        e = s_ref[...].astype(F32) * vec_ref[0:1]
        o_ref[...] = g_ref[...] + norm_back(e, z, inv)

    block = pl.BlockSpec((PR_DEV, width), lambda i: (0, 0))
    return pl.pallas_call(
        kern,
        grid=(1,),
        in_specs=[block, block, block, pl.BlockSpec(vecs.shape, lambda i: (0, 0))],
        out_specs=block,
        out_shape=jax.ShapeDtypeStruct((tok, width), F32),
        input_output_aliases={0: 0},
        cost_estimate=cost(20 * PR_DEV * width, 12 * PR_DEV * width),
        name="finish",
    )(grad, summed, tokens, vecs)


def over(axis, values, bit):
    n = lax.axis_size(axis)
    return lax.ppermute(values, axis, [(i, i ^ bit) for i in range(n)])


def halves_sum(halves, step):
    bits = [1 << b for b in range(lax.axis_size("rep").bit_length() - 1)]
    got = [over("rep", v, b) for v, b in zip(halves, (bits[step], bits[-1 - step]))]
    return [(v.astype(F32) + g.astype(F32)).astype(v.dtype) for v, g in zip(halves, got)]


def rep_sum_small(values):
    n = lax.axis_size("rep")
    terms = [values] + [over("rep", values, b) for b in range(1, n)]
    terms = [t.astype(F32) for t in terms]
    while len(terms) > 1:
        terms = [terms[i] + terms[i + 1] for i in range(0, len(terms), 2)]
    return terms[0]


def local(
    tokens,
    ln1_gain,
    ln1_bias,
    w_qkv,
    qv_bias,
    w_out,
    out_bias,
    ln2_gain,
    ln2_bias,
    w_fc,
    fc_bias,
    w_proj,
    proj_bias,
    teacher,
    cotangent,
    valid_mask,
):
    ns = lax.axis_size("shard")
    nr = lax.axis_size("rep")
    me = lax.axis_index("shard").astype(jnp.int32)
    shard = me.reshape(1)
    tok, width = tokens.shape
    nq = min(nr, w_fc.shape[1] // width)
    group = lax.axis_index("rep").astype(jnp.int32) % nq
    dsh = width // ns
    rb = 256

    bundle = lax.all_gather(
        jnp.concatenate(
            [w_qkv[:, :width], w_qkv[:, width : 2 * width], w_qkv[:, 2 * width :], tokens[:PR_DEV]]
        ),
        "shard",
    )
    fc_own = lax.dynamic_slice_in_dim(w_fc, group * width, width, 1)
    second = lax.all_gather(jnp.concatenate([fc_own, w_out]), "shard")
    full_proj = lax.all_gather(w_proj, "shard", axis=0, tiled=True)

    mask_f = valid_mask.astype(F32)
    counts = jnp.sum(mask_f.reshape(-1, PR_DEV), axis=1).astype(BF)
    parts = [ln1_gain, ln1_bias, qv_bias, out_bias, ln2_gain, ln2_bias, proj_bias, fc_bias]
    offs = [0]
    for p in parts:
        offs.append(offs[-1] + p.shape[0])
    packed = jnp.concatenate(parts + [counts])
    packed = jnp.pad(packed, (0, (-packed.shape[0]) % 128))
    params = lax.all_gather(packed.reshape(1, -1), "shard", axis=0, tiled=True).astype(F32)
    vecs = jnp.concatenate(
        [params[:, offs[i] : offs[i + 1]].reshape(-1, width) for i in range(8)]
        + [jnp.zeros((16 - 8 - nq, width), F32)]
    )
    count = jnp.sum(params[:, offs[8] : offs[8] + counts.shape[0]])
    token_total = rep_sum_small(jnp.full((8, 128), count, F32))[0, 0]
    factor = tok * nr * ns / token_total
    weight = (factor * mask_f).reshape(tok, 1)

    h1, q, k, v = qkv_call(bundle, tokens, vecs, shard)
    mix, lse = attn_fwd(q, k, v, shard, rb)
    x1, h2 = out_proj_call(mix, second, tokens, vecs)

    core = me % 2
    piece = lax.dynamic_slice_in_dim(second, core * (ns // 2), ns // 2, 0)[:, :dsh]
    got = [over("rep", piece, j) for j in range(1, nq)]
    other = [over("shard", g, 1) for g in got]
    g, gp, full_fc = fc_call(h2, second, got, other, vecs, jnp.stack([group, core]))
    out, dy, dm, grad_proj, last = proj_call(g, full_proj, x1, teacher, cotangent, weight, vecs)
    own_proj = lax.psum_scatter(grad_proj, "shard", scatter_dimension=0, tiled=True)
    fc_mine, fc_theirs, out_mine, out_theirs, dx1, do, sums, fc_sums = mid_call(
        dm, dy, full_proj, gp, h2, full_fc, x1, mix, second, vecs, core.reshape(1)
    )
    dq, dkv = attn_bwd(q, k, v, mix, do, lse, shard, rb)

    plus = lambda *terms: sum(t.astype(F32) for t in terms).astype(BF)
    nz = ns // 2
    fc_half = plus(fc_mine, over("shard", fc_theirs, 1))
    out_half = plus(out_mine, over("shard", out_theirs, 1))
    out_half = jnp.swapaxes(out_half.reshape(nz, nq, dsh // nq, width), 0, 1)
    pair = jnp.concatenate([fc_half, out_half], axis=2)

    pick = lambda a, n: lax.dynamic_index_in_dim(a, n, 0, keepdims=False)

    dq, dkv, own_proj, pair = lax.optimization_barrier((dq, dkv, own_proj, pair))
    grads = grads_call(h1, dq, dkv, shard, ns)
    own_qkv = lax.psum_scatter(grads.reshape(-1, width), "shard", scatter_dimension=0, tiled=True)
    dq, dkv, grads = lax.optimization_barrier((dq, dkv, grads))
    last_part, ig = dh1_call(bundle, tokens, vecs, dq, dkv, dx1, sums, fc_sums, last, shard)
    quarter = plus(
        pick(pair, group),
        *[over("rep", pick(pair, jnp.bitwise_xor(group, b)), b) for b in range(1, nq)],
    )
    last_part, own_qkv, quarter, own_proj = lax.optimization_barrier(
        (last_part, own_qkv, quarter, own_proj)
    )
    own = lax.psum_scatter(last_part.reshape(-1, width), "shard", scatter_dimension=0, tiled=True)
    input_grad = finish_call(ig, own[EXTRA:], tokens, vecs)

    z = me // 2
    final = plus(
        pick(quarter, z),
        *[over("shard", pick(quarter, jnp.bitwise_xor(z, b)), 2 * b) for b in range(1, nz)],
    )
    bit = nq
    while bit < nr:
        final = plus(final, over("rep", final, bit))
        bit *= 2
    both = jnp.concatenate([own_qkv, own_proj])
    cut = both.shape[0] // 2
    both = halves_sum([both[:cut], both[cut:]], 0)
    final, *both = lax.optimization_barrier((final, *both))
    for step in range(1, nr.bit_length() - 1):
        both = halves_sum(both, step)
    both = jnp.concatenate(both).astype(F32)
    sum_qkv, sum_proj = both[: 3 * dsh], both[3 * dsh :]
    relative = jnp.stack([final] + [over("rep", final, b) for b in range(1, nq)])
    natural = [pick(relative, jnp.bitwise_xor(group, b)) for b in range(nq)]
    sum_fc = jnp.concatenate([n[:dsh] for n in natural], axis=1).astype(F32)
    sum_out = jnp.concatenate([n[dsh:] for n in natural], axis=0).astype(F32)

    small = rep_sum_small(own[:EXTRA])

    def take(first, rows):
        n = rows * dsh
        return lax.dynamic_slice_in_dim(small[first : first + rows].reshape(-1), me * n, n)

    return (
        out,
        input_grad,
        take(0, 1),
        take(1, 1),
        jnp.concatenate([sum_qkv[j * dsh : (j + 1) * dsh] for j in range(3)], axis=1),
        take(2, 2),
        sum_out,
        take(4, 1),
        take(5, 1),
        take(6, 1),
        sum_fc,
        take(8, nq),
        sum_proj,
        take(7, 1),
    )


def solution(mesh):
    rows = P(("rep", "shard"), None)
    mat = P("shard", None)
    vec = P("shard")
    return jax.shard_map(
        local,
        mesh=mesh,
        in_specs=(
            rows,
            vec,
            vec,
            mat,
            vec,
            mat,
            vec,
            vec,
            vec,
            mat,
            vec,
            mat,
            vec,
            rows,
            rows,
            P(("rep", "shard")),
        ),
        out_specs=(rows, rows, vec, vec, mat, vec, mat, vec, vec, vec, mat, vec, mat, vec),
        check_vma=False,
    )
```

```python
import jax
import jax.numpy as jnp
from jax import lax
from jax.experimental import pallas as pl
from jax.experimental.pallas import tpu as pltpu
from jax.sharding import PartitionSpec as P

F32 = jnp.float32
BF = jnp.bfloat16
HEAD = 64
PR_DEV = 128
PAIR = 2 * HEAD
SCALE = 0.125
EPS = 1e-05
NEG = -1e30
VMEM_LIMIT = 60 * 1024 * 1024
EXTRA = 16


def dot_nt(a, b):
    return lax.dot_general(a, b, (((1,), (1,)), ((), ())), preferred_element_type=F32)


def dot_nn(a, b):
    return lax.dot_general(a, b, (((1,), (0,)), ((), ())), preferred_element_type=F32)


def dot_tn(a, b):
    return lax.dot_general(a, b, (((0,), (0,)), ((), ())), preferred_element_type=F32)


def normalize(values):
    centered = values - jnp.mean(values, axis=-1, keepdims=True)
    inv = lax.rsqrt(jnp.mean(centered * centered, axis=-1, keepdims=True) + EPS)
    return centered * inv, inv


def norm_back(e, z, inv):
    return inv * (
        e - jnp.mean(e, axis=-1, keepdims=True) - z * jnp.mean(e * z, axis=-1, keepdims=True)
    )


def cost(flops, nbytes, trans=0):
    return pl.CostEstimate(flops=int(flops), bytes_accessed=int(nbytes), transcendentals=int(trans))


def fixed(shape):
    return pl.BlockSpec(shape, lambda *_: (0,) * len(shape))


def qkv_call(bundle, got, other, tokens, vecs, where):
    ns, count, width = bundle.shape
    tok = tokens.shape[0]
    cont = tok - PR_DEV
    plen = ns * PR_DEV
    keys = plen + cont
    dsh = width // ns
    base = count - PR_DEV
    rows = got.shape[0] * dsh
    kw = width // 2

    def kern(wh_ref, g_ref, got_ref, other_ref, t_ref, vec_ref, h_ref, q_ref, k_ref, v_ref, wa, wk):
        shard, half, core = wh_ref[0], wh_ref[1], wh_ref[2]
        gain, bias, bq, bv = vec_ref[0:1], vec_ref[1:2], vec_ref[2:3], vec_ref[3:4]

        def keep(n, first, piece):
            m = piece.shape[0] * dsh
            wa[n, pl.ds(first, m), :] = piece[:, :dsh].reshape(m, width)
            low = piece[:, dsh:base, :kw]
            if base != 2 * dsh:
                low = jnp.concatenate([low, piece[:, dsh:base, kw:]], axis=1)
            wk[n, pl.ds(first, m), :] = low.reshape(m, kw)

        keep(half, 0, g_ref[:, :base, :])
        keep(1 - half, pl.multiple_of(core * rows, rows), got_ref[...])
        keep(1 - half, pl.multiple_of((1 - core) * rows, rows), other_ref[...])

        def to_q(h):
            return ((dot_nn(h, wa[0]) + bq).astype(BF).astype(F32) * SCALE).astype(BF)

        step = 4

        def chunk(x, r0):
            h = (normalize(x.astype(F32))[0] * gain + bias).astype(BF)
            at = pl.ds(r0, h.shape[0])
            h_ref[at, :] = h
            k_ref[at, :kw] = dot_nn(h, wk[0]).astype(BF)
            k_ref[at, kw:] = dot_nn(h, wk[1]).astype(BF)
            v_ref[at, :] = (dot_nn(h, wa[1]) + bv).astype(BF)

        for b in range(0, ns, step):
            x = g_ref[b : b + step, base:, :]
            chunk(x.reshape(x.shape[0] * PR_DEV, width), b * PR_DEV)
        chunk(t_ref[PR_DEV:, :], plen)
        own = pl.multiple_of(shard * PR_DEV, PR_DEV)
        q_ref[:PR_DEV, :] = to_q(h_ref[pl.ds(own, PR_DEV), :])
        q_ref[PR_DEV:, :] = to_q(h_ref[plen:, :])

    shape = lambda *r: jax.ShapeDtypeStruct((*r, width), BF)
    vm = pl.BlockSpec(memory_space=pltpu.VMEM)
    return pl.pallas_call(
        kern,
        in_specs=[pl.BlockSpec(memory_space=pltpu.SMEM)] + [vm] * 5,
        out_specs=[vm] * 6,
        out_shape=[
            shape(keys),
            shape(tok),
            shape(keys),
            shape(keys),
            shape(2, width),
            jax.ShapeDtypeStruct((2, width, kw), BF),
        ],
        compiler_params=pltpu.CompilerParams(vmem_limit_bytes=VMEM_LIMIT),
        cost_estimate=cost(2 * width * width * (2 * keys + tok), 2 * width * (6 * keys)),
        name="qkv",
    )(where, bundle, got, other, tokens, vecs)


def attn_fwd(q, k, v, shard, rb):
    tok, width = q.shape
    keys = k.shape[0]
    cont = tok - PR_DEV
    plen = keys - cont
    npair = width // PAIR

    def kern(sh_ref, q_ref, k_ref, v_ref, o_ref, lse_ref):
        sh = sh_ref[0]
        first = lax.broadcasted_iota(jnp.int32, (1, PAIR), 1) < HEAD

        def block(r0, rows, n, offset, masked):
            outs, lses = [], []
            for h in range(2):
                mine = first if h == 0 else jnp.logical_not(first)
                qq = jnp.where(mine, q_ref[pl.ds(r0, rows), :], 0).astype(BF)
                s = dot_nt(qq, k_ref[pl.ds(0, n), :])
                tail = s[:, n - masked :]
                row = lax.broadcasted_iota(jnp.int32, tail.shape, 0)
                col = lax.broadcasted_iota(jnp.int32, tail.shape, 1)
                tail = jnp.where(col <= row + offset, tail, NEG)
                s = tail if masked == n else jnp.concatenate([s[:, : n - masked], tail], axis=1)
                top = jnp.max(s, axis=1, keepdims=True)
                p = jnp.exp(s - top)
                total = jnp.sum(p, axis=1, keepdims=True)
                outs.append(dot_nn(p.astype(BF), v_ref[pl.ds(0, n), :]) * (1.0 / total))
                lses.append(top + jnp.log(total))
            o_ref[pl.ds(r0, rows), :] = jnp.where(first, outs[0], outs[1]).astype(BF)
            turned = jnp.transpose(jnp.where(first, lses[0], lses[1]))
            lse_ref[0, 0:1, pl.ds(r0, rows)] = turned[0:1]
            lse_ref[0, 1:2, pl.ds(r0, rows)] = turned[HEAD : HEAD + 1]

        block(0, PR_DEV, plen, sh * PR_DEV, plen)
        for i in range(cont // rb):
            block(PR_DEV + i * rb, rb, plen + (i + 1) * rb, 0, rb)

    spq = pl.BlockSpec((tok, PAIR), lambda i: (0, i))
    spk = pl.BlockSpec((keys, PAIR), lambda i: (0, i))
    return pl.pallas_call(
        kern,
        grid=(npair,),
        in_specs=[pl.BlockSpec(memory_space=pltpu.SMEM), spq, spk, spk],
        out_specs=[spq, pl.BlockSpec((1, 2, tok), lambda i: (i, 0, 0))],
        out_shape=[
            jax.ShapeDtypeStruct((tok, width), BF),
            jax.ShapeDtypeStruct((npair, 2, tok), F32),
        ],
        compiler_params=pltpu.CompilerParams(vmem_limit_bytes=VMEM_LIMIT),
        cost_estimate=cost(16 * width * tok * keys, 4 * width * (tok + keys)),
        name="attn_fwd",
    )(shard, q, k, v)


def attn_bwd(q, k, v, o, do, lse, shard, rb, low, count, prev=()):
    tok, width = q.shape
    keys = k.shape[0]
    cont = tok - PR_DEV
    plen = keys - cont

    def kern(sh_ref, q_ref, k_ref, v_ref, o_ref, do_ref, lse_ref, *rest):
        dq_ref, dkv_ref, ka, va = rest[len(prev) :]
        sh = sh_ref[0]
        first = lax.broadcasted_iota(jnp.int32, (1, PAIR), 1) < HEAD
        ka[...] = jnp.zeros_like(ka)
        va[...] = jnp.zeros_like(va)
        hr = lax.broadcasted_iota(jnp.int32, (8, PAIR), 0)
        hc = lax.broadcasted_iota(jnp.int32, (8, PAIR), 1)
        pick = jnp.where(hc // HEAD == hr, 1.0, 0.0).astype(F32)

        def block(r0, rows, n, offset, masked):
            prod = o_ref[pl.ds(r0, rows), :].astype(F32) * do_ref[pl.ds(r0, rows), :].astype(F32)
            row_dot = lax.dot_general(
                pick,
                prod,
                (((1,), (1,)), ((), ())),
                precision=lax.Precision.HIGHEST,
                preferred_element_type=F32,
            )
            dqs = []
            for h in range(2):
                mine = first if h == 0 else jnp.logical_not(first)
                qq = jnp.where(mine, q_ref[pl.ds(r0, rows), :], 0).astype(BF)
                gg = jnp.where(mine, do_ref[pl.ds(r0, rows), :], 0).astype(BF)
                kk = k_ref[pl.ds(0, n), :]
                s = dot_nt(kk, qq)
                tail = s[n - masked :]
                col = lax.broadcasted_iota(jnp.int32, tail.shape, 0)
                row = lax.broadcasted_iota(jnp.int32, tail.shape, 1)
                tail = jnp.where(col <= row + offset, tail, NEG)
                s = tail if masked == n else jnp.concatenate([s[: n - masked], tail], axis=0)
                p = jnp.exp(s - lse_ref[0, h : h + 1, pl.ds(r0, rows)])
                dp = dot_nt(v_ref[pl.ds(0, n), :], gg)
                ds = (p * (dp - row_dot[h : h + 1, :])).astype(BF)
                va[pl.ds(0, n), :] += dot_nn(p.astype(BF), gg)
                ka[pl.ds(0, n), :] += dot_nn(ds, qq)
                dqs.append(dot_tn(ds, kk))
            dq_ref[pl.ds(r0, rows), :] = (jnp.where(first, dqs[0], dqs[1]) * SCALE).astype(BF)

        block(0, PR_DEV, plen, sh * PR_DEV, plen)
        for i in range(cont // rb):
            block(PR_DEV + i * rb, rb, plen + (i + 1) * rb, 0, rb)
        dkv_ref[0] = ka[...].astype(BF)
        dkv_ref[1] = va[...].astype(BF)

    spq = pl.BlockSpec((tok, PAIR), lambda i: (0, i + low))
    spk = pl.BlockSpec((keys, PAIR), lambda i: (0, i + low))
    return pl.pallas_call(
        kern,
        grid=(count,),
        in_specs=[
            pl.BlockSpec(memory_space=pltpu.SMEM),
            spq,
            spk,
            spk,
            spq,
            spq,
            pl.BlockSpec((1, 2, tok), lambda i: (i + low, 0, 0)),
        ]
        + [pl.BlockSpec(memory_space=pl.ANY)] * len(prev),
        out_specs=[spq, pl.BlockSpec((2, keys, PAIR), lambda i: (0, 0, i + low))],
        out_shape=[
            jax.ShapeDtypeStruct((tok, width), BF),
            jax.ShapeDtypeStruct((2, keys, width), BF),
        ],
        scratch_shapes=[pltpu.VMEM((keys, PAIR), F32), pltpu.VMEM((keys, PAIR), F32)],
        compiler_params=pltpu.CompilerParams(vmem_limit_bytes=VMEM_LIMIT),
        input_output_aliases={7 + i: i for i in range(len(prev))},
        cost_estimate=cost(40 * count * PAIR * tok * keys, 8 * count * PAIR * (tok + keys)),
        name="attn_bwd",
    )(shard, q, k, v, o, do, lse, *prev)


def out_proj_call(mix, second, tokens, vecs):
    ns, _, width = second.shape
    tok = tokens.shape[0]
    dsh = width // ns

    def kern(o_ref, w_ref, t_ref, vec_ref, x_ref, h_ref):
        wo = w_ref[...].reshape(width, width)
        x1 = t_ref[...].astype(F32) + (dot_nn(o_ref[...], wo) + vec_ref[4:5])
        x_ref[...] = x1
        h_ref[...] = (normalize(x1)[0] * vec_ref[5:6] + vec_ref[6:7]).astype(BF)

    whole = lambda a: pl.BlockSpec(a.shape, lambda i: (0,) * a.ndim)
    return pl.pallas_call(
        kern,
        grid=(1,),
        in_specs=[
            whole(mix),
            pl.BlockSpec((ns, dsh, width), lambda i: (0, 1, 0)),
            whole(tokens),
            whole(vecs),
        ],
        out_specs=[pl.BlockSpec((tok, width), lambda i: (0, 0))] * 2,
        out_shape=[jax.ShapeDtypeStruct((tok, width), F32), jax.ShapeDtypeStruct((tok, width), BF)],
        compiler_params=pltpu.CompilerParams(vmem_limit_bytes=VMEM_LIMIT),
        cost_estimate=cost(2 * width * width * tok, 12 * width * tok),
        name="out_proj",
    )(mix, second, tokens, vecs)


def fc_call(h2, second, got, other, vecs, where):
    ns, _, width = second.shape
    tok = h2.shape[0]
    dsh = width // ns
    half = ns // 2
    nq = len(got) + 1

    def kern(*refs):
        wh_ref, h_ref, own_ref = refs[:3]
        got_refs = refs[3 : 2 + nq]
        other_refs = refs[2 + nq : 1 + 2 * nq]
        vec_ref, g_ref, gp_ref, w_ref = refs[1 + 2 * nq :]
        me, core = wh_ref[0], wh_ref[1]
        step = pl.program_id(0)
        rows = half * dsh

        @pl.when(step == 0)
        def _():
            w_ref[0] = own_ref[...].reshape(width, width)

        for j in range(1, nq):

            @pl.when(step == j)
            def _():
                first = pl.multiple_of(core * rows, rows)
                second_half = pl.multiple_of((1 - core) * rows, rows)
                w_ref[0, pl.ds(first, rows), :] = got_refs[j - 1][...].reshape(rows, width)
                w_ref[0, pl.ds(second_half, rows), :] = other_refs[j - 1][...].reshape(rows, width)

        c = jnp.bitwise_xor(me, step)
        f = dot_nn(h_ref[...], w_ref[0]) + vec_ref[pl.ds(8 + c, 1), :]
        square = f * f
        t = jnp.tanh(0.7978845608028654 * f * (1.0 + 0.044715 * square))
        up = 0.5 * (1.0 + t)
        g_ref[0] = (f * up).astype(BF)
        slope = 0.5 * f * (1.0 - t * t) * (0.7978845608028654 + 0.1070322243 * square)
        gp_ref[0] = (up + slope).astype(BF)

    pick = lambda j, wh: (jnp.bitwise_xor(wh[0], j), 0, 0)
    return pl.pallas_call(
        kern,
        grid_spec=pltpu.PrefetchScalarGridSpec(
            num_scalar_prefetch=1,
            grid=(nq,),
            in_specs=[fixed(h2.shape), fixed((ns, dsh, width))]
            + [fixed(a.shape) for a in got]
            + [fixed(a.shape) for a in other]
            + [fixed(vecs.shape)],
            out_specs=[
                pl.BlockSpec((1, tok, width), pick),
                pl.BlockSpec((1, tok, width), pick),
                pl.BlockSpec((1, width, width), pick),
            ],
        ),
        out_shape=[
            jax.ShapeDtypeStruct((nq, tok, width), BF),
            jax.ShapeDtypeStruct((nq, tok, width), BF),
            jax.ShapeDtypeStruct((nq, width, width), BF),
        ],
        compiler_params=pltpu.CompilerParams(vmem_limit_bytes=VMEM_LIMIT),
        cost_estimate=cost(2 * nq * width * width * tok, 4 * nq * width * (tok + width)),
        name="fc",
    )(where, h2, second, *got, *other, vecs)


def proj_call(g, w_proj, x1, teacher, cotangent, weight, vecs):
    nq, tok, width = g.shape

    def kern(g_ref, w_ref, x_ref, te_ref, co_ref, wt_ref, vec_ref, y_ref, dy_ref, dm_ref, gw_ref, pb_ref, acc, keep):
        i = pl.program_id(0)

        @pl.when(i == 0)
        def _():
            acc[...] = x_ref[...] + vec_ref[7:8]

        @pl.when(i < nq)
        def _():
            keep[i] = g_ref[0]
            acc[...] += dot_nn(g_ref[0], w_ref[...])

        @pl.when(i == nq - 1)
        def _():
            y = acc[...]
            y_ref[...] = y.astype(BF)
            dy = co_ref[...].astype(F32) + wt_ref[...] * (y - te_ref[...].astype(F32))
            dy_ref[...] = dy
            dm = dy.astype(BF)
            dm_ref[...] = dm
            pb_ref[0:1, :] = jnp.sum(dm.astype(F32), axis=0, keepdims=True)
            pb_ref[1:8, :] = jnp.zeros((7, width), F32)

        @pl.when(i >= nq)
        def _():
            gw_ref[...] = dot_tn(keep[i - nq], dm_ref[...]).astype(BF)

    last = nq - 1
    return pl.pallas_call(
        kern,
        grid=(2 * nq,),
        in_specs=[
            pl.BlockSpec((1, tok, width), lambda i: (jnp.minimum(i, last), 0, 0)),
            pl.BlockSpec((width, width), lambda i: (jnp.minimum(i, last), 0)),
        ]
        + [fixed(a.shape) for a in (x1, teacher, cotangent, weight, vecs)],
        out_specs=[
            fixed((tok, width)),
            fixed((tok, width)),
            fixed((tok, width)),
            pl.BlockSpec((width, width), lambda i: (jnp.maximum(i - nq, 0), 0)),
            fixed((8, width)),
        ],
        out_shape=[
            jax.ShapeDtypeStruct((tok, width), BF),
            jax.ShapeDtypeStruct((tok, width), F32),
            jax.ShapeDtypeStruct((tok, width), BF),
            jax.ShapeDtypeStruct((nq * width, width), BF),
            jax.ShapeDtypeStruct((8, width), F32),
        ],
        scratch_shapes=[pltpu.VMEM((tok, width), F32), pltpu.VMEM((nq, tok, width), BF)],
        compiler_params=pltpu.CompilerParams(vmem_limit_bytes=VMEM_LIMIT),
        cost_estimate=cost(4 * nq * width * width * tok, 2 * nq * width * (tok + 2 * width)),
        name="proj",
    )(g, w_proj, x1, teacher, cotangent, weight, vecs)


def mid_call(dm, dy, w_proj, gp, h2, w_fc, x1, mix, second, vecs, core):
    nq, tok, width = gp.shape
    ns = second.shape[0]
    dsh = width // ns
    nz = ns // 2

    def kern(*refs):
        (co_ref, dm_ref, dy_ref, wp_ref, gp_ref, h_ref, wf_ref, x_ref, o_ref, wo_ref, vec_ref) = refs[:11]
        (fm_ref, ft_ref, om_ref, ot_ref, dx_ref, do_ref, sm_ref, fb_ref, ht, dh2) = refs[11:]
        j = pl.program_id(0)
        total = lambda m: jnp.sum(m, axis=0, keepdims=True)

        def split(gw, mine, theirs):
            gw = gw.astype(BF).reshape(nz, 2, dsh, width)
            for c in range(2):

                @pl.when(co_ref[0] == c)
                def _():
                    mine[...] = gw[:, c]
                    theirs[...] = gw[:, 1 - c]

        @pl.when(j == 0)
        def _():
            ht[...] = jnp.transpose(h_ref[...])
            dh2[...] = jnp.zeros_like(dh2)

        @pl.when(j < nq)
        def _():
            dg = dot_nt(dm_ref[...], wp_ref[...])
            df = (dg * gp_ref[0].astype(F32)).astype(BF)
            fb_ref[pl.ds(j, 1), :] = total(df.astype(F32))
            split(dot_nn(ht[...], df), fm_ref.at[0], ft_ref.at[0])
            dh2[...] += dot_nt(df, wf_ref[0])

        @pl.when(j == nq)
        def _():
            z, inv = normalize(x_ref[...])
            grad = dh2[...]
            sm_ref[0:1, :] = total(grad * z)
            sm_ref[1:2, :] = total(grad)
            dx = dy_ref[...] + norm_back(grad * vec_ref[5:6], z, inv)
            dx_ref[...] = dx
            da = dx.astype(BF)
            sm_ref[2:3, :] = total(da.astype(F32))
            do_ref[...] = dot_nt(da, wo_ref[...].reshape(width, width)).astype(BF)
            split(dot_tn(o_ref[...], da), om_ref, ot_ref)

    last = nq - 1
    pick = lambda j: (jnp.minimum(j, last), 0, 0)
    out = pl.BlockSpec((1, nz, dsh, width), lambda j: (jnp.minimum(j, last), 0, 0, 0))
    return pl.pallas_call(
        kern,
        grid=(nq + 1,),
        in_specs=[
            pl.BlockSpec(memory_space=pltpu.SMEM),
            fixed(dm.shape),
            fixed(dy.shape),
            pl.BlockSpec((width, width), lambda j: (jnp.minimum(j, last), 0)),
            pl.BlockSpec((1, tok, width), pick),
            fixed(h2.shape),
            pl.BlockSpec((1, width, width), pick),
            fixed(x1.shape),
            fixed(mix.shape),
            pl.BlockSpec((ns, dsh, width), lambda j: (0, 1, 0)),
            fixed(vecs.shape),
        ],
        out_specs=[
            out,
            out,
            fixed((nz, dsh, width)),
            fixed((nz, dsh, width)),
            fixed((tok, width)),
            fixed((tok, width)),
            fixed((8, width)),
            fixed((nq, width)),
        ],
        out_shape=[
            jax.ShapeDtypeStruct((nq, nz, dsh, width), BF),
            jax.ShapeDtypeStruct((nq, nz, dsh, width), BF),
            jax.ShapeDtypeStruct((nz, dsh, width), BF),
            jax.ShapeDtypeStruct((nz, dsh, width), BF),
            jax.ShapeDtypeStruct((tok, width), F32),
            jax.ShapeDtypeStruct((tok, width), BF),
            jax.ShapeDtypeStruct((8, width), F32),
            jax.ShapeDtypeStruct((nq, width), F32),
        ],
        scratch_shapes=[pltpu.VMEM((width, tok), BF), pltpu.VMEM((tok, width), F32)],
        compiler_params=pltpu.CompilerParams(vmem_limit_bytes=VMEM_LIMIT),
        cost_estimate=cost(
            2 * width * width * tok * (3 * nq + 2), 2 * width * (nq * (tok + 4 * width) + 8 * tok)
        ),
        name="mid",
    )(core, dm, dy, w_proj, gp, h2, w_fc, x1, mix, second, vecs)


def grads_call(h1, dq, dkv, shard, ns):
    keys, width = h1.shape
    tok = dq.shape[0]
    plen = ns * PR_DEV
    dsh = width // ns

    nz = ns // 2

    def kern(sh_ref, h_ref, dq_ref, d_ref, mine, theirs, ht):
        j = pl.program_id(0)

        def split(gw):
            gw = gw.astype(BF).reshape(nz, 2, dsh, width)
            for c in range(2):

                @pl.when(sh_ref[0] % 2 == c)
                def _():
                    mine[...] = gw[:, c]
                    theirs[...] = gw[:, 1 - c]

        @pl.when(j == 0)
        def _():
            ht[...] = jnp.transpose(h_ref[...])

        @pl.when(j < 2)
        def _():
            split(dot_nn(ht[...], d_ref[0]))

        @pl.when(j == 2)
        def _():
            own = pl.ds(pl.multiple_of(sh_ref[0] * PR_DEV, PR_DEV), PR_DEV)
            gq = dot_nn(ht[:, plen:], dq_ref[PR_DEV:, :]) + dot_tn(h_ref[own, :], dq_ref[:PR_DEV, :])
            split(gq)

    return pl.pallas_call(
        kern,
        grid=(3,),
        in_specs=[
            pl.BlockSpec(memory_space=pltpu.SMEM),
            fixed(h1.shape),
            fixed(dq.shape),
            pl.BlockSpec((1, keys, width), lambda j: (jnp.minimum(j, 1), 0, 0)),
        ],
        out_specs=[pl.BlockSpec((nz, dsh, width), lambda j: (0, (j + 1) % 3, 0))] * 2,
        out_shape=[jax.ShapeDtypeStruct((nz, 3 * dsh, width), BF)] * 2,
        scratch_shapes=[pltpu.VMEM((width, keys), BF)],
        compiler_params=pltpu.CompilerParams(vmem_limit_bytes=VMEM_LIMIT),
        cost_estimate=cost(2 * width * width * (2 * keys + tok), 2 * width * 5 * keys),
        name="grads",
    )(shard, h1, dq, dkv)


def dh1_call(bundle, wa, wk, tokens, vecs, dq, dkv, dx1, sums, fc_sums, last, shard):
    ns, rows, width = bundle.shape
    tok = tokens.shape[0]
    cont = tok - PR_DEV
    plen = ns * PR_DEV
    nq = fc_sums.shape[0]
    base = rows - PR_DEV
    kw = width // 2
    step = cont // PR_DEV
    chunks = ns // step

    def kern(*refs):
        (sh_ref, g_ref, wa_ref, wk_ref, t_ref, vec_ref, dq_ref, dk_ref, dv_ref, dx_ref) = refs[:10]
        (s2_ref, fb_ref, s3_ref, o_ref, ig_ref, sm) = refs[10:]
        i = pl.program_id(0)
        wq, wv = wa_ref[0], wa_ref[1]

        def back_kv(dk, dv):
            low = dot_nt(dk[:, :kw], wk_ref[0]) + dot_nt(dk[:, kw:], wk_ref[1])
            return low + dot_nt(dv, wv)

        total = lambda m: jnp.sum(m, axis=0, keepdims=True)

        @pl.when(i == 0)
        def _():
            sm[...] = jnp.zeros_like(sm)

        def add(dh, z):
            sm[0:1, :] += total(dh * z)
            sm[1:2, :] += total(dh)

        dv = dv_ref[0]
        sm[3:4, :] += total(dv.astype(F32))
        dh = back_kv(dk_ref[0], dv)

        @pl.when(i < chunks)
        def _():
            x = g_ref[pl.ds(i * step, step), base : base + PR_DEV, :]
            z, _ = normalize(x.reshape(cont, width).astype(F32))
            add(dh, z)
            o_ref[pl.ds(i * step, step), EXTRA:, :] = dh.astype(BF).reshape(step, PR_DEV, width)

        @pl.when(i == sh_ref[0] // step)
        def _():
            own = pl.ds(pl.multiple_of((sh_ref[0] % step) * PR_DEV, PR_DEV), PR_DEV)
            z, _ = normalize(t_ref[:PR_DEV, :].astype(F32))
            part = dot_nt(dq_ref[:PR_DEV, :], wq)
            add(part, z)
            both = back_kv(dk_ref[0, own, :], dv_ref[0, own, :])
            o_ref[sh_ref[0], EXTRA:, :] = (both + part).astype(BF)

        @pl.when(i == chunks)
        def _():
            z, inv = normalize(t_ref[PR_DEV:, :].astype(F32))
            full = dh + dot_nt(dq_ref[PR_DEV:, :], wq)
            add(full, z)
            ig_ref[PR_DEV:, :] = dx_ref[PR_DEV:, :] + norm_back(full * vec_ref[0:1], z, inv)
            ig_ref[:PR_DEV, :] = dx_ref[:PR_DEV, :]
            sm[2:3, :] = total(dq_ref[...].astype(F32))
            sm[4:5, :] = s2_ref[2:3, :]
            sm[5:7, :] = s2_ref[0:2, :]
            sm[7:8, :] = s3_ref[0:1, :]
            sm[8 : 8 + nq, :] = fb_ref[...]
            small = sm[...].astype(BF)
            for b in range(ns):
                o_ref[b, :EXTRA, :] = small

    chunk = lambda k: pl.BlockSpec((1, cont, width), lambda i: (k, i, 0))
    out = (ns, EXTRA + PR_DEV, width)
    return pl.pallas_call(
        kern,
        grid=(chunks + 1,),
        in_specs=[
            pl.BlockSpec(memory_space=pltpu.SMEM),
            fixed(bundle.shape),
            fixed(wa.shape),
            fixed(wk.shape),
            fixed(tokens.shape),
            fixed(vecs.shape),
            fixed(dq.shape),
            chunk(0),
            chunk(1),
        ]
        + [fixed(a.shape) for a in (dx1, sums, fc_sums, last)],
        out_specs=[fixed(out), fixed((tok, width))],
        out_shape=[jax.ShapeDtypeStruct(out, BF), jax.ShapeDtypeStruct((tok, width), F32)],
        scratch_shapes=[pltpu.VMEM((EXTRA, width), F32)],
        compiler_params=pltpu.CompilerParams(vmem_limit_bytes=VMEM_LIMIT),
        cost_estimate=cost(
            2 * width * width * (2 * (plen + cont) + tok), 2 * width * (5 * plen + 10 * cont)
        ),
        name="dh1",
    )(shard, bundle, wa, wk, tokens, vecs, dq, dkv, dkv, dx1, sums, fc_sums, last)


def finish_call(grad, summed, tokens, vecs):
    tok, width = grad.shape

    def kern(g_ref, s_ref, t_ref, vec_ref, o_ref):
        z, inv = normalize(t_ref[...].astype(F32))
        e = s_ref[...].astype(F32) * vec_ref[0:1]
        o_ref[...] = g_ref[...] + norm_back(e, z, inv)

    block = pl.BlockSpec((PR_DEV, width), lambda i: (0, 0))
    return pl.pallas_call(
        kern,
        grid=(1,),
        in_specs=[block, block, block, pl.BlockSpec(vecs.shape, lambda i: (0, 0))],
        out_specs=block,
        out_shape=jax.ShapeDtypeStruct((tok, width), F32),
        input_output_aliases={0: 0},
        cost_estimate=cost(20 * PR_DEV * width, 12 * PR_DEV * width),
        name="finish",
    )(grad, summed, tokens, vecs)


def over(axis, values, bit):
    n = lax.axis_size(axis)
    return lax.ppermute(values, axis, [(i, i ^ bit) for i in range(n)])


def cross(values, step):
    nr, ns = lax.axis_size("rep"), lax.axis_size("shard")
    pairs = [
        (r * ns + c, (r ^ (1 << ((c % 2) ^ step))) * ns + c) for r in range(nr) for c in range(ns)
    ]
    return lax.ppermute(values, ("rep", "shard"), pairs)


def rep_sum_small(values):
    n = lax.axis_size("rep")
    terms = [values] + [over("rep", values, b) for b in range(1, n)]
    terms = [t.astype(F32) for t in terms]
    while len(terms) > 1:
        terms = [terms[i] + terms[i + 1] for i in range(0, len(terms), 2)]
    return terms[0]


def local(
    tokens,
    ln1_gain,
    ln1_bias,
    w_qkv,
    qv_bias,
    w_out,
    out_bias,
    ln2_gain,
    ln2_bias,
    w_fc,
    fc_bias,
    w_proj,
    proj_bias,
    teacher,
    cotangent,
    valid_mask,
):
    ns = lax.axis_size("shard")
    nr = lax.axis_size("rep")
    me = lax.axis_index("shard").astype(jnp.int32)
    shard = me.reshape(1)
    tok, width = tokens.shape
    nq = min(nr, w_fc.shape[1] // width)
    group = lax.axis_index("rep").astype(jnp.int32) % nq
    dsh = width // ns
    rb = 256

    core = me % 2
    half = lax.axis_index("rep").astype(jnp.int32)
    half = jnp.bitwise_xor(half, half // 2) % 2
    kw = width // 2
    outer = lax.dynamic_slice_in_dim(w_qkv, half * 2 * width, width, 1)
    middle = lax.dynamic_slice_in_dim(w_qkv, width + half * kw, kw, 1)
    if dsh % 32:
        middle = jnp.pad(middle, ((0, 0), (0, kw)))
    else:
        middle = jnp.concatenate([middle[: dsh // 2], middle[dsh // 2 :]], axis=1)
    bundle = lax.all_gather(jnp.concatenate([outer, middle, tokens[:PR_DEV]]), "shard")
    fc_own = lax.dynamic_slice_in_dim(w_fc, group * width, width, 1)
    mask_f = valid_mask.astype(F32)
    counts = jnp.sum(mask_f.reshape(-1, PR_DEV), axis=1).astype(BF)
    parts = [ln1_gain, ln1_bias, qv_bias, out_bias, ln2_gain, ln2_bias, proj_bias, fc_bias]
    offs = [0]
    for p in parts:
        offs.append(offs[-1] + p.shape[0])
    packed = jnp.concatenate(parts + [counts])
    packed = jnp.pad(packed, (0, (-packed.shape[0]) % 128))
    params = lax.all_gather(packed.reshape(1, -1), "shard", axis=0, tiled=True).astype(F32)
    vecs = jnp.concatenate(
        [params[:, offs[i] : offs[i + 1]].reshape(-1, width) for i in range(8)]
        + [jnp.zeros((16 - 8 - nq, width), F32)]
    )
    count = jnp.sum(params[:, offs[8] : offs[8] + counts.shape[0]])
    token_total = rep_sum_small(jnp.full((8, 128), count, F32))[0, 0]
    factor = tok * nr * ns / token_total
    weight = (factor * mask_f).reshape(tok, 1)

    second = jnp.concatenate([fc_own, w_out])
    bundle, second, vecs, weight = lax.optimization_barrier((bundle, second, vecs, weight))
    second = lax.all_gather(second, "shard")
    qkv_piece = lax.dynamic_slice_in_dim(bundle, core * (ns // 2), ns // 2, 0)
    qkv_far = cross(qkv_piece[:, : bundle.shape[1] - PR_DEV], 0)
    qkv_near = over("shard", qkv_far, 1)
    h1, q, k, v, wa, wk = qkv_call(
        bundle, qkv_far, qkv_near, tokens, vecs, jnp.stack([me, half, core])
    )
    piece = lax.dynamic_slice_in_dim(second, core * (ns // 2), ns // 2, 0)[:, :dsh]
    q, k, v, piece, w_proj = lax.optimization_barrier((q, k, v, piece, w_proj))
    full_proj = lax.all_gather(w_proj, "shard", axis=0, tiled=True)
    mix, lse = attn_fwd(q, k, v, shard, rb)
    mix, lse, *got = lax.optimization_barrier(
        (mix, lse, *[over("rep", piece, j) for j in range(1, nq)])
    )
    other = [over("shard", g, 1) for g in got]
    x1, h2 = out_proj_call(mix, second, tokens, vecs)
    g, gp, full_fc = fc_call(h2, second, got, other, vecs, jnp.stack([group, core]))
    out, dy, dm, grad_proj, last = proj_call(g, full_proj, x1, teacher, cotangent, weight, vecs)
    own_proj = lax.psum_scatter(grad_proj, "shard", scatter_dimension=0, tiled=True)
    fc_mine, fc_theirs, out_mine, out_theirs, dx1, do, sums, fc_sums = mid_call(
        dm, dy, full_proj, gp, h2, full_fc, x1, mix, second, vecs, core.reshape(1)
    )
    nz = ns // 2
    z = me // 2
    pick = lambda a, n: lax.dynamic_index_in_dim(a, n, 0, keepdims=False)
    plus = lambda *terms: sum(t.astype(F32) for t in terms).astype(BF)
    hold = lax.optimization_barrier

    def rep_sends(parts):
        return [pick(parts, jnp.bitwise_xor(group, b)) for b in range(nq)]

    def by_rep(sends):
        return sends[:1] + [over("rep", sends[b], b) for b in range(1, nq)]

    def by_z(parts):
        far = [over("shard", pick(parts, jnp.bitwise_xor(z, b)), 2 * b) for b in range(1, nz)]
        return [pick(parts, z)] + far

    def rest_of_rep(part):
        bit = nq
        while bit < nr:
            part = plus(part, over("rep", part, bit))
            bit *= 2
        return part

    first = jnp.where(core == 0, 1, 2)

    def halve(parts):
        at = lambda *ds: jnp.stack([pick(parts, jnp.bitwise_xor(group, d)) for d in ds])
        return at(first, 3), at(0, 3 - first)

    def spread(part, step):
        return jnp.concatenate([part, cross(part, step)])

    def quarters(relative):
        found = []
        for n in range(nq):
            d = jnp.bitwise_xor(group, n)
            found.append(pick(relative, jnp.where(core == 0, d, d % 2 * 2 + d // 2)))
        return found

    npair = width // PAIR
    cuts = [0, npair // 6, npair * 2 // 3, npair]

    def backward(n, prev=()):
        return attn_bwd(q, k, v, mix, do, lse, shard, rb, cuts[n], cuts[n + 1] - cuts[n], prev)

    dq, dkv = backward(0)
    fc_got, out_got = over("shard", fc_theirs, 1), over("shard", out_theirs, 1)
    dq, dkv, fc_got, out_got = hold((dq, dkv, fc_got, out_got))
    fc_half = plus(fc_mine, fc_got)
    out_half = plus(out_mine, out_got)
    out_half = jnp.swapaxes(out_half.reshape(nz, nq, dsh // nq, width), 0, 1)
    away, kept = halve(jnp.concatenate([fc_half, out_half], axis=2))
    dq, dkv, away, kept = hold((dq, dkv, away, kept))
    got = cross(away, 0)
    dq, dkv = backward(1, (dq, dkv))
    dq, dkv, got = hold((dq, dkv, got))
    both = plus(kept, got)
    dq, dkv, both = hold((dq, dkv, both))
    got = cross(both[1], 1)
    dq, dkv = backward(2, (dq, dkv))
    dq, dkv, got, own_proj = hold((dq, dkv, got, own_proj))
    quarter = plus(both[0], got)
    empty = jnp.zeros_like(quarter)
    quarter = jnp.stack(
        [jnp.where(core == 0, quarter, empty), jnp.where(core == 0, empty, quarter)], axis=1
    )
    dq, dkv, quarter = hold((dq, dkv, quarter))
    own_fc = lax.psum_scatter(
        quarter.reshape(-1, width), "shard", scatter_dimension=0, tiled=True
    )
    proj_got = cross(own_proj, 0)
    qkv_mine, qkv_theirs = grads_call(h1, dq, dkv, shard, ns)
    dq, dkv, qkv_mine, qkv_theirs, proj_got = hold((dq, dkv, qkv_mine, qkv_theirs, proj_got))
    qkv_got = over("shard", qkv_theirs, 1)
    proj = plus(own_proj, proj_got)
    proj_got = cross(proj, 1)
    last_part, ig = dh1_call(bundle, wa, wk, tokens, vecs, dq, dkv, dx1, sums, fc_sums, last, shard)
    last_part, qkv_got, proj_got = hold((last_part, qkv_got, proj_got))
    own = lax.psum_scatter(last_part.reshape(-1, width), "shard", scatter_dimension=0, tiled=True)

    qkv_half = plus(qkv_mine, qkv_got).reshape(nz, nq, 3 * dsh // nq, width)
    away, kept = halve(jnp.swapaxes(qkv_half, 0, 1))
    got = cross(away, 0)
    proj = rest_of_rep(plus(proj, proj_got))
    got, proj = hold((got, proj))
    both = plus(kept, got)
    got = cross(both[1], 1)
    part = spread(rest_of_rep(own_fc)[None], 0)
    got, part = hold((got, part))
    qkv_z = by_z(plus(both[0], got))
    part = spread(part, 1)
    part, *qkv_z = hold((part, *qkv_z))
    qkv_part = spread(rest_of_rep(plus(*qkv_z))[None], 0)
    natural = quarters(part)
    sum_fc = jnp.concatenate([n[:dsh] for n in natural], axis=1).astype(F32)
    sum_out = jnp.concatenate([n[dsh:] for n in natural], axis=0).astype(F32)
    sum_proj = proj.astype(F32)
    own, qkv_part, sum_fc = hold((own, qkv_part, sum_fc))

    small = rep_sum_small(own[:EXTRA])
    input_grad = finish_call(ig, own[EXTRA:], tokens, vecs)
    sum_qkv = jnp.concatenate(quarters(spread(qkv_part, 1))).astype(F32)

    def take(first, rows):
        n = rows * dsh
        return lax.dynamic_slice_in_dim(small[first : first + rows].reshape(-1), me * n, n)

    return (
        out,
        input_grad,
        take(0, 1),
        take(1, 1),
        jnp.concatenate([sum_qkv[j * dsh : (j + 1) * dsh] for j in range(3)], axis=1),
        take(2, 2),
        sum_out,
        take(4, 1),
        take(5, 1),
        take(6, 1),
        sum_fc,
        take(8, nq),
        sum_proj,
        take(7, 1),
    )


def solution(mesh):
    rows = P(("rep", "shard"), None)
    mat = P("shard", None)
    vec = P("shard")
    return jax.shard_map(
        local,
        mesh=mesh,
        in_specs=(
            rows,
            vec,
            vec,
            mat,
            vec,
            mat,
            vec,
            vec,
            vec,
            mat,
            vec,
            mat,
            vec,
            rows,
            rows,
            P(("rep", "shard")),
        ),
        out_specs=(rows, rows, vec, vec, mat, vec, mat, vec, vec, vec, mat, vec, mat, vec),
        check_vma=False,
    )
```

```python
import jax
import jax.numpy as jnp
from jax import lax
from jax.experimental import pallas as pl
from jax.experimental.pallas import tpu as pltpu
from jax.sharding import PartitionSpec as P

F32 = jnp.float32
BF = jnp.bfloat16
HEAD = 64
PR_DEV = 128
PAIR = 2 * HEAD
SCALE = 0.125
EPS = 1e-05
NEG = -1e30
VMEM_LIMIT = 60 * 1024 * 1024
EXTRA = 16


def dot_nt(a, b):
    return lax.dot_general(a, b, (((1,), (1,)), ((), ())), preferred_element_type=F32)


def dot_nn(a, b):
    return lax.dot_general(a, b, (((1,), (0,)), ((), ())), preferred_element_type=F32)


def dot_tn(a, b):
    return lax.dot_general(a, b, (((0,), (0,)), ((), ())), preferred_element_type=F32)


def normalize(values):
    centered = values - jnp.mean(values, axis=-1, keepdims=True)
    inv = lax.rsqrt(jnp.mean(centered * centered, axis=-1, keepdims=True) + EPS)
    return centered * inv, inv


def norm_back(e, z, inv):
    return inv * (
        e - jnp.mean(e, axis=-1, keepdims=True) - z * jnp.mean(e * z, axis=-1, keepdims=True)
    )


def cost(flops, nbytes, trans=0):
    return pl.CostEstimate(flops=int(flops), bytes_accessed=int(nbytes), transcendentals=int(trans))


def fixed(shape):
    return pl.BlockSpec(shape, lambda *_: (0,) * len(shape))


def qkv_call(bundle, got, other, tokens, vecs, where):
    ns, count, width = bundle.shape
    tok = tokens.shape[0]
    cont = tok - PR_DEV
    plen = ns * PR_DEV
    keys = plen + cont
    dsh = width // ns
    base = count - PR_DEV
    rows = got.shape[0] * dsh
    kw = width // 2

    def kern(wh_ref, g_ref, got_ref, other_ref, t_ref, vec_ref, h_ref, q_ref, k_ref, v_ref, wa, wk):
        shard, half, core = wh_ref[0], wh_ref[1], wh_ref[2]
        gain, bias, bq, bv = vec_ref[0:1], vec_ref[1:2], vec_ref[2:3], vec_ref[3:4]

        def keep(n, first, piece):
            m = piece.shape[0] * dsh
            wa[n, pl.ds(first, m), :] = piece[:, :dsh].reshape(m, width)
            low = piece[:, dsh:base, :kw]
            if base != 2 * dsh:
                low = jnp.concatenate([low, piece[:, dsh:base, kw:]], axis=1)
            wk[n, pl.ds(first, m), :] = low.reshape(m, kw)

        keep(half, 0, g_ref[:, :base, :])
        keep(1 - half, pl.multiple_of(core * rows, rows), got_ref[...])
        keep(1 - half, pl.multiple_of((1 - core) * rows, rows), other_ref[...])

        def to_q(h):
            return ((dot_nn(h, wa[0]) + bq).astype(BF).astype(F32) * SCALE).astype(BF)

        step = 4

        def chunk(x, r0):
            h = (normalize(x.astype(F32))[0] * gain + bias).astype(BF)
            at = pl.ds(r0, h.shape[0])
            h_ref[at, :] = h
            k_ref[at, :kw] = dot_nn(h, wk[0]).astype(BF)
            k_ref[at, kw:] = dot_nn(h, wk[1]).astype(BF)
            v_ref[at, :] = (dot_nn(h, wa[1]) + bv).astype(BF)

        for b in range(0, ns, step):
            x = g_ref[b : b + step, base:, :]
            chunk(x.reshape(x.shape[0] * PR_DEV, width), b * PR_DEV)
        chunk(t_ref[PR_DEV:, :], plen)
        own = pl.multiple_of(shard * PR_DEV, PR_DEV)
        q_ref[:PR_DEV, :] = to_q(h_ref[pl.ds(own, PR_DEV), :])
        q_ref[PR_DEV:, :] = to_q(h_ref[plen:, :])

    shape = lambda *r: jax.ShapeDtypeStruct((*r, width), BF)
    vm = pl.BlockSpec(memory_space=pltpu.VMEM)
    return pl.pallas_call(
        kern,
        in_specs=[pl.BlockSpec(memory_space=pltpu.SMEM)] + [vm] * 5,
        out_specs=[vm] * 6,
        out_shape=[
            shape(keys),
            shape(tok),
            shape(keys),
            shape(keys),
            shape(2, width),
            jax.ShapeDtypeStruct((2, width, kw), BF),
        ],
        compiler_params=pltpu.CompilerParams(vmem_limit_bytes=VMEM_LIMIT),
        cost_estimate=cost(2 * width * width * (2 * keys + tok), 2 * width * (6 * keys)),
        name="qkv",
    )(where, bundle, got, other, tokens, vecs)


def attn_fwd(q, k, v, shard, rb):
    tok, width = q.shape
    keys = k.shape[0]
    cont = tok - PR_DEV
    plen = keys - cont
    npair = width // PAIR

    def kern(sh_ref, q_ref, k_ref, v_ref, o_ref, lse_ref):
        sh = sh_ref[0]
        first = lax.broadcasted_iota(jnp.int32, (1, PAIR), 1) < HEAD

        def block(r0, rows, n, offset, masked):
            outs, lses = [], []
            for h in range(2):
                mine = first if h == 0 else jnp.logical_not(first)
                qq = jnp.where(mine, q_ref[pl.ds(r0, rows), :], 0).astype(BF)
                s = dot_nt(qq, k_ref[pl.ds(0, n), :])
                tail = s[:, n - masked :]
                row = lax.broadcasted_iota(jnp.int32, tail.shape, 0)
                col = lax.broadcasted_iota(jnp.int32, tail.shape, 1)
                tail = jnp.where(col <= row + offset, tail, NEG)
                s = tail if masked == n else jnp.concatenate([s[:, : n - masked], tail], axis=1)
                top = jnp.max(s, axis=1, keepdims=True)
                p = jnp.exp(s - top)
                total = jnp.sum(p, axis=1, keepdims=True)
                outs.append(dot_nn(p.astype(BF), v_ref[pl.ds(0, n), :]) * (1.0 / total))
                lses.append(top + jnp.log(total))
            o_ref[pl.ds(r0, rows), :] = jnp.where(first, outs[0], outs[1]).astype(BF)
            turned = jnp.transpose(jnp.where(first, lses[0], lses[1]))
            lse_ref[0, 0:1, pl.ds(r0, rows)] = turned[0:1]
            lse_ref[0, 1:2, pl.ds(r0, rows)] = turned[HEAD : HEAD + 1]

        block(0, PR_DEV, plen, sh * PR_DEV, plen)
        for i in range(cont // rb):
            block(PR_DEV + i * rb, rb, plen + (i + 1) * rb, 0, rb)

    spq = pl.BlockSpec((tok, PAIR), lambda i: (0, i))
    spk = pl.BlockSpec((keys, PAIR), lambda i: (0, i))
    return pl.pallas_call(
        kern,
        grid=(npair,),
        in_specs=[pl.BlockSpec(memory_space=pltpu.SMEM), spq, spk, spk],
        out_specs=[spq, pl.BlockSpec((1, 2, tok), lambda i: (i, 0, 0))],
        out_shape=[
            jax.ShapeDtypeStruct((tok, width), BF),
            jax.ShapeDtypeStruct((npair, 2, tok), F32),
        ],
        compiler_params=pltpu.CompilerParams(vmem_limit_bytes=VMEM_LIMIT),
        cost_estimate=cost(16 * width * tok * keys, 4 * width * (tok + keys)),
        name="attn_fwd",
    )(shard, q, k, v)


def attn_bwd(q, k, v, o, do, lse, shard, rb, low, count, prev=()):
    tok, width = q.shape
    keys = k.shape[0]
    cont = tok - PR_DEV
    plen = keys - cont

    def kern(sh_ref, q_ref, k_ref, v_ref, o_ref, do_ref, lse_ref, *rest):
        dq_ref, dkv_ref, ka, va = rest[len(prev) :]
        sh = sh_ref[0]
        first = lax.broadcasted_iota(jnp.int32, (1, PAIR), 1) < HEAD
        ka[...] = jnp.zeros_like(ka)
        va[...] = jnp.zeros_like(va)
        hr = lax.broadcasted_iota(jnp.int32, (8, PAIR), 0)
        hc = lax.broadcasted_iota(jnp.int32, (8, PAIR), 1)
        pick = jnp.where(hc // HEAD == hr, 1.0, 0.0).astype(F32)

        def block(r0, rows, n, offset, masked):
            prod = o_ref[pl.ds(r0, rows), :].astype(F32) * do_ref[pl.ds(r0, rows), :].astype(F32)
            row_dot = lax.dot_general(
                pick,
                prod,
                (((1,), (1,)), ((), ())),
                precision=lax.Precision.HIGHEST,
                preferred_element_type=F32,
            )
            dqs = []
            for h in range(2):
                mine = first if h == 0 else jnp.logical_not(first)
                qq = jnp.where(mine, q_ref[pl.ds(r0, rows), :], 0).astype(BF)
                gg = jnp.where(mine, do_ref[pl.ds(r0, rows), :], 0).astype(BF)
                kk = k_ref[pl.ds(0, n), :]
                s = dot_nt(kk, qq)
                tail = s[n - masked :]
                col = lax.broadcasted_iota(jnp.int32, tail.shape, 0)
                row = lax.broadcasted_iota(jnp.int32, tail.shape, 1)
                tail = jnp.where(col <= row + offset, tail, NEG)
                s = tail if masked == n else jnp.concatenate([s[: n - masked], tail], axis=0)
                p = jnp.exp(s - lse_ref[0, h : h + 1, pl.ds(r0, rows)])
                dp = dot_nt(v_ref[pl.ds(0, n), :], gg)
                ds = (p * (dp - row_dot[h : h + 1, :])).astype(BF)
                va[pl.ds(0, n), :] += dot_nn(p.astype(BF), gg)
                ka[pl.ds(0, n), :] += dot_nn(ds, qq)
                dqs.append(dot_tn(ds, kk))
            dq_ref[pl.ds(r0, rows), :] = (jnp.where(first, dqs[0], dqs[1]) * SCALE).astype(BF)

        block(0, PR_DEV, plen, sh * PR_DEV, plen)
        for i in range(cont // rb):
            block(PR_DEV + i * rb, rb, plen + (i + 1) * rb, 0, rb)
        dkv_ref[0] = ka[...].astype(BF)
        dkv_ref[1] = va[...].astype(BF)

    spq = pl.BlockSpec((tok, PAIR), lambda i: (0, i + low))
    spk = pl.BlockSpec((keys, PAIR), lambda i: (0, i + low))
    return pl.pallas_call(
        kern,
        grid=(count,),
        in_specs=[
            pl.BlockSpec(memory_space=pltpu.SMEM),
            spq,
            spk,
            spk,
            spq,
            spq,
            pl.BlockSpec((1, 2, tok), lambda i: (i + low, 0, 0)),
        ]
        + [pl.BlockSpec(memory_space=pl.ANY)] * len(prev),
        out_specs=[spq, pl.BlockSpec((2, keys, PAIR), lambda i: (0, 0, i + low))],
        out_shape=[
            jax.ShapeDtypeStruct((tok, width), BF),
            jax.ShapeDtypeStruct((2, keys, width), BF),
        ],
        scratch_shapes=[pltpu.VMEM((keys, PAIR), F32), pltpu.VMEM((keys, PAIR), F32)],
        compiler_params=pltpu.CompilerParams(vmem_limit_bytes=VMEM_LIMIT),
        input_output_aliases={7 + i: i for i in range(len(prev))},
        cost_estimate=cost(40 * count * PAIR * tok * keys, 8 * count * PAIR * (tok + keys)),
        name="attn_bwd",
    )(shard, q, k, v, o, do, lse, *prev)


def out_proj_call(mix, second, tokens, vecs):
    ns, _, width = second.shape
    tok = tokens.shape[0]
    dsh = width // ns

    def kern(o_ref, w_ref, t_ref, vec_ref, x_ref, h_ref):
        wo = w_ref[...].reshape(width, width)
        x1 = t_ref[...].astype(F32) + (dot_nn(o_ref[...], wo) + vec_ref[4:5])
        x_ref[...] = x1
        h_ref[...] = (normalize(x1)[0] * vec_ref[5:6] + vec_ref[6:7]).astype(BF)

    whole = lambda a: pl.BlockSpec(a.shape, lambda i: (0,) * a.ndim)
    return pl.pallas_call(
        kern,
        grid=(1,),
        in_specs=[
            whole(mix),
            pl.BlockSpec((ns, dsh, width), lambda i: (0, 1, 0)),
            whole(tokens),
            whole(vecs),
        ],
        out_specs=[pl.BlockSpec((tok, width), lambda i: (0, 0))] * 2,
        out_shape=[jax.ShapeDtypeStruct((tok, width), F32), jax.ShapeDtypeStruct((tok, width), BF)],
        compiler_params=pltpu.CompilerParams(vmem_limit_bytes=VMEM_LIMIT),
        cost_estimate=cost(2 * width * width * tok, 12 * width * tok),
        name="out_proj",
    )(mix, second, tokens, vecs)


def fc_call(h2, second, got, other, vecs, where):
    ns, _, width = second.shape
    tok = h2.shape[0]
    dsh = width // ns
    half = ns // 2
    nq = len(got) + 1

    def kern(*refs):
        wh_ref, h_ref, own_ref = refs[:3]
        got_refs = refs[3 : 2 + nq]
        other_refs = refs[2 + nq : 1 + 2 * nq]
        vec_ref, g_ref, gp_ref, w_ref = refs[1 + 2 * nq :]
        me, core = wh_ref[0], wh_ref[1]
        step = pl.program_id(0)
        rows = half * dsh

        @pl.when(step == 0)
        def _():
            w_ref[0] = own_ref[...].reshape(width, width)

        for j in range(1, nq):

            @pl.when(step == j)
            def _():
                first = pl.multiple_of(core * rows, rows)
                second_half = pl.multiple_of((1 - core) * rows, rows)
                w_ref[0, pl.ds(first, rows), :] = got_refs[j - 1][...].reshape(rows, width)
                w_ref[0, pl.ds(second_half, rows), :] = other_refs[j - 1][...].reshape(rows, width)

        c = jnp.bitwise_xor(me, step)
        f = dot_nn(h_ref[...], w_ref[0]) + vec_ref[pl.ds(8 + c, 1), :]
        square = f * f
        t = jnp.tanh(0.7978845608028654 * f * (1.0 + 0.044715 * square))
        up = 0.5 * (1.0 + t)
        g_ref[0] = (f * up).astype(BF)
        slope = 0.5 * f * (1.0 - t * t) * (0.7978845608028654 + 0.1070322243 * square)
        gp_ref[0] = (up + slope).astype(BF)

    pick = lambda j, wh: (jnp.bitwise_xor(wh[0], j), 0, 0)
    return pl.pallas_call(
        kern,
        grid_spec=pltpu.PrefetchScalarGridSpec(
            num_scalar_prefetch=1,
            grid=(nq,),
            in_specs=[fixed(h2.shape), fixed((ns, dsh, width))]
            + [fixed(a.shape) for a in got]
            + [fixed(a.shape) for a in other]
            + [fixed(vecs.shape)],
            out_specs=[
                pl.BlockSpec((1, tok, width), pick),
                pl.BlockSpec((1, tok, width), pick),
                pl.BlockSpec((1, width, width), pick),
            ],
        ),
        out_shape=[
            jax.ShapeDtypeStruct((nq, tok, width), BF),
            jax.ShapeDtypeStruct((nq, tok, width), BF),
            jax.ShapeDtypeStruct((nq, width, width), BF),
        ],
        compiler_params=pltpu.CompilerParams(vmem_limit_bytes=VMEM_LIMIT),
        cost_estimate=cost(2 * nq * width * width * tok, 4 * nq * width * (tok + width)),
        name="fc",
    )(where, h2, second, *got, *other, vecs)


def proj_call(g, w_proj, x1, teacher, cotangent, weight, vecs):
    nq, tok, width = g.shape

    def kern(g_ref, w_ref, x_ref, te_ref, co_ref, wt_ref, vec_ref, y_ref, dy_ref, dm_ref, gw_ref, pb_ref, acc, keep):
        i = pl.program_id(0)

        @pl.when(i == 0)
        def _():
            acc[...] = x_ref[...] + vec_ref[7:8]

        @pl.when(i < nq)
        def _():
            keep[i] = g_ref[0]
            acc[...] += dot_nn(g_ref[0], w_ref[...])

        @pl.when(i == nq - 1)
        def _():
            y = acc[...]
            y_ref[...] = y.astype(BF)
            dy = co_ref[...].astype(F32) + wt_ref[...] * (y - te_ref[...].astype(F32))
            dy_ref[...] = dy
            dm = dy.astype(BF)
            dm_ref[...] = dm
            pb_ref[0:1, :] = jnp.sum(dm.astype(F32), axis=0, keepdims=True)
            pb_ref[1:8, :] = jnp.zeros((7, width), F32)

        @pl.when(i >= nq)
        def _():
            gw_ref[...] = dot_tn(keep[i - nq], dm_ref[...]).astype(BF)

    last = nq - 1
    return pl.pallas_call(
        kern,
        grid=(2 * nq,),
        in_specs=[
            pl.BlockSpec((1, tok, width), lambda i: (jnp.minimum(i, last), 0, 0)),
            pl.BlockSpec((width, width), lambda i: (jnp.minimum(i, last), 0)),
        ]
        + [fixed(a.shape) for a in (x1, teacher, cotangent, weight, vecs)],
        out_specs=[
            fixed((tok, width)),
            fixed((tok, width)),
            fixed((tok, width)),
            pl.BlockSpec((width, width), lambda i: (jnp.maximum(i - nq, 0), 0)),
            fixed((8, width)),
        ],
        out_shape=[
            jax.ShapeDtypeStruct((tok, width), BF),
            jax.ShapeDtypeStruct((tok, width), F32),
            jax.ShapeDtypeStruct((tok, width), BF),
            jax.ShapeDtypeStruct((nq * width, width), BF),
            jax.ShapeDtypeStruct((8, width), F32),
        ],
        scratch_shapes=[pltpu.VMEM((tok, width), F32), pltpu.VMEM((nq, tok, width), BF)],
        compiler_params=pltpu.CompilerParams(vmem_limit_bytes=VMEM_LIMIT),
        cost_estimate=cost(4 * nq * width * width * tok, 2 * nq * width * (tok + 2 * width)),
        name="proj",
    )(g, w_proj, x1, teacher, cotangent, weight, vecs)


def mid_call(dm, dy, w_proj, gp, h2, w_fc, x1, mix, second, vecs, core):
    nq, tok, width = gp.shape
    ns = second.shape[0]
    dsh = width // ns
    nz = ns // 2

    def kern(*refs):
        (co_ref, dm_ref, dy_ref, wp_ref, gp_ref, h_ref, wf_ref, x_ref, o_ref, wo_ref, vec_ref) = refs[:11]
        (fm_ref, ft_ref, om_ref, ot_ref, dx_ref, do_ref, sm_ref, fb_ref, ht, dh2) = refs[11:]
        j = pl.program_id(0)
        total = lambda m: jnp.sum(m, axis=0, keepdims=True)

        def split(gw, mine, theirs):
            gw = gw.astype(BF).reshape(nz, 2, dsh, width)
            for c in range(2):

                @pl.when(co_ref[0] == c)
                def _():
                    mine[...] = gw[:, c]
                    theirs[...] = gw[:, 1 - c]

        @pl.when(j == 0)
        def _():
            ht[...] = jnp.transpose(h_ref[...])
            dh2[...] = jnp.zeros_like(dh2)

        @pl.when(j < nq)
        def _():
            dg = dot_nt(dm_ref[...], wp_ref[...])
            df = (dg * gp_ref[0].astype(F32)).astype(BF)
            fb_ref[pl.ds(j, 1), :] = total(df.astype(F32))
            split(dot_nn(ht[...], df), fm_ref.at[0], ft_ref.at[0])
            dh2[...] += dot_nt(df, wf_ref[0])

        @pl.when(j == nq)
        def _():
            z, inv = normalize(x_ref[...])
            grad = dh2[...]
            sm_ref[0:1, :] = total(grad * z)
            sm_ref[1:2, :] = total(grad)
            dx = dy_ref[...] + norm_back(grad * vec_ref[5:6], z, inv)
            dx_ref[...] = dx
            da = dx.astype(BF)
            sm_ref[2:3, :] = total(da.astype(F32))
            do_ref[...] = dot_nt(da, wo_ref[...].reshape(width, width)).astype(BF)
            split(dot_tn(o_ref[...], da), om_ref, ot_ref)

    last = nq - 1
    pick = lambda j: (jnp.minimum(j, last), 0, 0)
    out = pl.BlockSpec((1, nz, dsh, width), lambda j: (jnp.minimum(j, last), 0, 0, 0))
    return pl.pallas_call(
        kern,
        grid=(nq + 1,),
        in_specs=[
            pl.BlockSpec(memory_space=pltpu.SMEM),
            fixed(dm.shape),
            fixed(dy.shape),
            pl.BlockSpec((width, width), lambda j: (jnp.minimum(j, last), 0)),
            pl.BlockSpec((1, tok, width), pick),
            fixed(h2.shape),
            pl.BlockSpec((1, width, width), pick),
            fixed(x1.shape),
            fixed(mix.shape),
            pl.BlockSpec((ns, dsh, width), lambda j: (0, 1, 0)),
            fixed(vecs.shape),
        ],
        out_specs=[
            out,
            out,
            fixed((nz, dsh, width)),
            fixed((nz, dsh, width)),
            fixed((tok, width)),
            fixed((tok, width)),
            fixed((8, width)),
            fixed((nq, width)),
        ],
        out_shape=[
            jax.ShapeDtypeStruct((nq, nz, dsh, width), BF),
            jax.ShapeDtypeStruct((nq, nz, dsh, width), BF),
            jax.ShapeDtypeStruct((nz, dsh, width), BF),
            jax.ShapeDtypeStruct((nz, dsh, width), BF),
            jax.ShapeDtypeStruct((tok, width), F32),
            jax.ShapeDtypeStruct((tok, width), BF),
            jax.ShapeDtypeStruct((8, width), F32),
            jax.ShapeDtypeStruct((nq, width), F32),
        ],
        scratch_shapes=[pltpu.VMEM((width, tok), BF), pltpu.VMEM((tok, width), F32)],
        compiler_params=pltpu.CompilerParams(vmem_limit_bytes=VMEM_LIMIT),
        cost_estimate=cost(
            2 * width * width * tok * (3 * nq + 2), 2 * width * (nq * (tok + 4 * width) + 8 * tok)
        ),
        name="mid",
    )(core, dm, dy, w_proj, gp, h2, w_fc, x1, mix, second, vecs)


def grads_call(h1, dq, dkv, shard, ns):
    keys, width = h1.shape
    tok = dq.shape[0]
    plen = ns * PR_DEV
    dsh = width // ns

    nz = ns // 2

    def kern(sh_ref, h_ref, dq_ref, d_ref, mine, theirs, ht):
        j = pl.program_id(0)

        def split(gw):
            gw = gw.astype(BF).reshape(nz, 2, dsh, width)
            for c in range(2):

                @pl.when(sh_ref[0] % 2 == c)
                def _():
                    mine[...] = gw[:, c]
                    theirs[...] = gw[:, 1 - c]

        @pl.when(j == 0)
        def _():
            ht[...] = jnp.transpose(h_ref[...])

        @pl.when(j < 2)
        def _():
            split(dot_nn(ht[...], d_ref[0]))

        @pl.when(j == 2)
        def _():
            own = pl.ds(pl.multiple_of(sh_ref[0] * PR_DEV, PR_DEV), PR_DEV)
            gq = dot_nn(ht[:, plen:], dq_ref[PR_DEV:, :]) + dot_tn(h_ref[own, :], dq_ref[:PR_DEV, :])
            split(gq)

    return pl.pallas_call(
        kern,
        grid=(3,),
        in_specs=[
            pl.BlockSpec(memory_space=pltpu.SMEM),
            fixed(h1.shape),
            fixed(dq.shape),
            pl.BlockSpec((1, keys, width), lambda j: (jnp.minimum(j, 1), 0, 0)),
        ],
        out_specs=[pl.BlockSpec((nz, dsh, width), lambda j: (0, (j + 1) % 3, 0))] * 2,
        out_shape=[jax.ShapeDtypeStruct((nz, 3 * dsh, width), BF)] * 2,
        scratch_shapes=[pltpu.VMEM((width, keys), BF)],
        compiler_params=pltpu.CompilerParams(vmem_limit_bytes=VMEM_LIMIT),
        cost_estimate=cost(2 * width * width * (2 * keys + tok), 2 * width * 5 * keys),
        name="grads",
    )(shard, h1, dq, dkv)


def small_layout(dsh, nq):
    return [(n, rows * dsh) for n, rows in ((0, 1), (1, 1), (2, 2), (4, 1), (5, 1), (6, 1), (8, nq), (7, 1))]


def dh1_call(bundle, wa, wk, tokens, vecs, dq, dkv, dx1, sums, fc_sums, last, shard):
    ns, rows, width = bundle.shape
    tok = tokens.shape[0]
    cont = tok - PR_DEV
    plen = ns * PR_DEV
    nq = fc_sums.shape[0]
    base = rows - PR_DEV
    kw = width // 2
    step = cont // PR_DEV
    chunks = ns // step

    def kern(*refs):
        (sh_ref, g_ref, wa_ref, wk_ref, t_ref, vec_ref, dq_ref, dk_ref, dv_ref, dx_ref) = refs[:10]
        (s2_ref, fb_ref, s3_ref, o_ref, ig_ref, sm, part) = refs[10:]
        i = pl.program_id(0)
        wq, wv = wa_ref[0], wa_ref[1]

        def back_kv(dk, dv):
            low = dot_nt(dk[:, :kw], wk_ref[0]) + dot_nt(dk[:, kw:], wk_ref[1])
            return low + dot_nt(dv, wv)

        total = lambda m: jnp.sum(m, axis=0, keepdims=True)

        @pl.when(i == 0)
        def _():
            sm[...] = jnp.zeros_like(sm)
            part[...] = jnp.zeros_like(part)

        def add(dh, z):
            sm[0:1, :] += total(dh * z)
            sm[1:2, :] += total(dh)

        dv = dv_ref[0]
        sm[3:4, :] += total(dv.astype(F32))
        dh = back_kv(dk_ref[0], dv)

        @pl.when(i < chunks)
        def _():
            x = g_ref[pl.ds(i * step, step), base : base + PR_DEV, :]
            z, _ = normalize(x.reshape(cont, width).astype(F32))
            add(dh, z)
            o_ref[pl.ds(i * step, step), EXTRA:, :] = dh.astype(BF).reshape(step, PR_DEV, width)

        @pl.when(i == sh_ref[0] // step)
        def _():
            own = pl.ds(pl.multiple_of((sh_ref[0] % step) * PR_DEV, PR_DEV), PR_DEV)
            z, _ = normalize(t_ref[:PR_DEV, :].astype(F32))
            part = dot_nt(dq_ref[:PR_DEV, :], wq)
            add(part, z)
            both = back_kv(dk_ref[0, own, :], dv_ref[0, own, :])
            o_ref[sh_ref[0], EXTRA:, :] = (both + part).astype(BF)

        @pl.when(i == chunks)
        def _():
            z, inv = normalize(t_ref[PR_DEV:, :].astype(F32))
            full = dh + dot_nt(dq_ref[PR_DEV:, :], wq)
            add(full, z)
            ig_ref[PR_DEV:, :] = dx_ref[PR_DEV:, :] + norm_back(full * vec_ref[0:1], z, inv)
            ig_ref[:PR_DEV, :] = dx_ref[:PR_DEV, :]
            sm[2:3, :] = total(dq_ref[...].astype(F32))
            sm[4:5, :] = s2_ref[2:3, :]
            sm[5:7, :] = s2_ref[0:2, :]
            sm[7:8, :] = s3_ref[0:1, :]
            sm[8 : 8 + nq, :] = fb_ref[...]
            for b in range(ns):
                for n, (first, size) in enumerate(small_layout(width // ns, nq)):
                    row, off = divmod(b * size, width)
                    part[n : n + 1, :size] = sm[first + row : first + row + 1, off : off + size]
                o_ref[b, :EXTRA, :] = part[...].astype(BF)

    chunk = lambda k: pl.BlockSpec((1, cont, width), lambda i: (k, i, 0))
    out = (ns, EXTRA + PR_DEV, width)
    return pl.pallas_call(
        kern,
        grid=(chunks + 1,),
        in_specs=[
            pl.BlockSpec(memory_space=pltpu.SMEM),
            fixed(bundle.shape),
            fixed(wa.shape),
            fixed(wk.shape),
            fixed(tokens.shape),
            fixed(vecs.shape),
            fixed(dq.shape),
            chunk(0),
            chunk(1),
        ]
        + [fixed(a.shape) for a in (dx1, sums, fc_sums, last)],
        out_specs=[fixed(out), fixed((tok, width))],
        out_shape=[jax.ShapeDtypeStruct(out, BF), jax.ShapeDtypeStruct((tok, width), F32)],
        scratch_shapes=[pltpu.VMEM((EXTRA, width), F32)] * 2,
        compiler_params=pltpu.CompilerParams(vmem_limit_bytes=VMEM_LIMIT),
        cost_estimate=cost(
            2 * width * width * (2 * (plen + cont) + tok), 2 * width * (5 * plen + 10 * cont)
        ),
        name="dh1",
    )(shard, bundle, wa, wk, tokens, vecs, dq, dkv, dkv, dx1, sums, fc_sums, last)


def finish_call(grad, summed, tokens, vecs):
    tok, width = grad.shape

    def kern(g_ref, s_ref, t_ref, vec_ref, o_ref):
        z, inv = normalize(t_ref[...].astype(F32))
        e = s_ref[EXTRA:, :].astype(F32) * vec_ref[0:1]
        o_ref[...] = g_ref[...] + norm_back(e, z, inv)

    block = pl.BlockSpec((PR_DEV, width), lambda i: (0, 0))
    return pl.pallas_call(
        kern,
        grid=(1,),
        in_specs=[
            block,
            pl.BlockSpec(summed.shape, lambda i: (0, 0)),
            block,
            pl.BlockSpec(vecs.shape, lambda i: (0, 0)),
        ],
        out_specs=block,
        out_shape=jax.ShapeDtypeStruct((tok, width), F32),
        input_output_aliases={0: 0},
        cost_estimate=cost(20 * PR_DEV * width, 12 * PR_DEV * width),
        name="finish",
    )(grad, summed, tokens, vecs)


def over(axis, values, bit):
    n = lax.axis_size(axis)
    return lax.ppermute(values, axis, [(i, i ^ bit) for i in range(n)])


def cross(values, step):
    nr, ns = lax.axis_size("rep"), lax.axis_size("shard")
    pairs = [
        (r * ns + c, (r ^ (1 << ((c % 2) ^ step))) * ns + c) for r in range(nr) for c in range(ns)
    ]
    return lax.ppermute(values, ("rep", "shard"), pairs)


def rep_sum_small(values):
    n = lax.axis_size("rep")
    terms = [values] + [over("rep", values, b) for b in range(1, n)]
    terms = [t.astype(F32) for t in terms]
    while len(terms) > 1:
        terms = [terms[i] + terms[i + 1] for i in range(0, len(terms), 2)]
    return terms[0]


def small_call(terms, layout):
    def kern(*refs):
        values = [r[...].astype(F32) for r in refs[: len(terms)]]
        while len(values) > 1:
            values = [values[i] + values[i + 1] for i in range(0, len(values), 2)]
        for n, (_, size) in enumerate(layout):
            refs[len(terms) + n][...] = values[0][n, :size]

    return pl.pallas_call(
        kern,
        out_shape=[jax.ShapeDtypeStruct((size,), F32) for _, size in layout],
        cost_estimate=cost(terms[0].size * len(terms), 2 * terms[0].size * len(terms)),
        name="small",
    )(*terms)


def local(
    tokens,
    ln1_gain,
    ln1_bias,
    w_qkv,
    qv_bias,
    w_out,
    out_bias,
    ln2_gain,
    ln2_bias,
    w_fc,
    fc_bias,
    w_proj,
    proj_bias,
    teacher,
    cotangent,
    valid_mask,
):
    ns = lax.axis_size("shard")
    nr = lax.axis_size("rep")
    me = lax.axis_index("shard").astype(jnp.int32)
    shard = me.reshape(1)
    tok, width = tokens.shape
    nq = min(nr, w_fc.shape[1] // width)
    group = lax.axis_index("rep").astype(jnp.int32) % nq
    dsh = width // ns
    rb = 256

    core = me % 2
    half = lax.axis_index("rep").astype(jnp.int32)
    half = jnp.bitwise_xor(half, half // 2) % 2
    kw = width // 2
    outer = lax.dynamic_slice_in_dim(w_qkv, half * 2 * width, width, 1)
    middle = lax.dynamic_slice_in_dim(w_qkv, width + half * kw, kw, 1)
    if dsh % 32:
        middle = jnp.pad(middle, ((0, 0), (0, kw)))
    else:
        middle = jnp.concatenate([middle[: dsh // 2], middle[dsh // 2 :]], axis=1)
    bundle = lax.all_gather(jnp.concatenate([outer, middle, tokens[:PR_DEV]]), "shard")
    fc_own = lax.dynamic_slice_in_dim(w_fc, group * width, width, 1)
    mask_f = valid_mask.astype(F32)
    counts = jnp.sum(mask_f.reshape(-1, PR_DEV), axis=1).astype(BF)
    parts = [ln1_gain, ln1_bias, qv_bias, out_bias, ln2_gain, ln2_bias, proj_bias, fc_bias]
    offs = [0]
    for p in parts:
        offs.append(offs[-1] + p.shape[0])
    packed = jnp.concatenate(parts + [counts])
    packed = jnp.pad(packed, (0, (-packed.shape[0]) % 128))
    params = lax.all_gather(packed.reshape(1, -1), "shard", axis=0, tiled=True).astype(F32)
    vecs = jnp.concatenate(
        [params[:, offs[i] : offs[i + 1]].reshape(-1, width) for i in range(8)]
        + [jnp.zeros((16 - 8 - nq, width), F32)]
    )
    count = jnp.sum(params[:, offs[8] : offs[8] + counts.shape[0]])
    token_total = rep_sum_small(jnp.full((8, 128), count, F32))[0, 0]
    factor = tok * nr * ns / token_total
    weight = (factor * mask_f).reshape(tok, 1)

    second = jnp.concatenate([fc_own, w_out])
    second, vecs, weight = lax.optimization_barrier((second, vecs, weight))
    second = lax.all_gather(second, "shard")
    bundle, w_proj = lax.optimization_barrier((bundle, w_proj))
    full_proj = lax.all_gather(w_proj, "shard", axis=0, tiled=True)
    qkv_piece = lax.dynamic_slice_in_dim(bundle, core * (ns // 2), ns // 2, 0)
    qkv_far = cross(qkv_piece[:, : bundle.shape[1] - PR_DEV], 0)
    qkv_near = over("shard", qkv_far, 1)
    h1, q, k, v, wa, wk = qkv_call(
        bundle, qkv_far, qkv_near, tokens, vecs, jnp.stack([me, half, core])
    )
    q, k, v, second = lax.optimization_barrier((q, k, v, second))
    piece = lax.dynamic_slice_in_dim(second, core * (ns // 2), ns // 2, 0)[:, :dsh]
    q, k, v, piece = lax.optimization_barrier((q, k, v, piece))
    mix, lse = attn_fwd(q, k, v, shard, rb)
    mix, lse, *got = lax.optimization_barrier(
        (mix, lse, *[over("rep", piece, j) for j in range(1, nq)])
    )
    other = [over("shard", g, 1) for g in got]
    x1, h2 = out_proj_call(mix, second, tokens, vecs)
    g, gp, full_fc = fc_call(h2, second, got, other, vecs, jnp.stack([group, core]))
    out, dy, dm, grad_proj, last = proj_call(g, full_proj, x1, teacher, cotangent, weight, vecs)
    own_proj = lax.psum_scatter(grad_proj, "shard", scatter_dimension=0, tiled=True)
    fc_mine, fc_theirs, out_mine, out_theirs, dx1, do, sums, fc_sums = mid_call(
        dm, dy, full_proj, gp, h2, full_fc, x1, mix, second, vecs, core.reshape(1)
    )
    nz = ns // 2
    z = me // 2
    pick = lambda a, n: lax.dynamic_index_in_dim(a, n, 0, keepdims=False)
    plus = lambda *terms: sum(t.astype(F32) for t in terms).astype(BF)
    hold = lax.optimization_barrier

    def rep_sends(parts):
        return [pick(parts, jnp.bitwise_xor(group, b)) for b in range(nq)]

    def by_rep(sends):
        return sends[:1] + [over("rep", sends[b], b) for b in range(1, nq)]

    def by_z(parts):
        far = [over("shard", pick(parts, jnp.bitwise_xor(z, b)), 2 * b) for b in range(1, nz)]
        return [pick(parts, z)] + far

    def rest_of_rep(part):
        bit = nq
        while bit < nr:
            part = plus(part, over("rep", part, bit))
            bit *= 2
        return part

    first = jnp.where(core == 0, 1, 2)

    def halve(parts):
        at = lambda *ds: jnp.stack([pick(parts, jnp.bitwise_xor(group, d)) for d in ds])
        return at(first, 3), at(0, 3 - first)

    def spread(part, step):
        return jnp.concatenate([part, cross(part, step)])

    def quarters(relative):
        found = []
        for n in range(nq):
            d = jnp.bitwise_xor(group, n)
            found.append(pick(relative, jnp.where(core == 0, d, d % 2 * 2 + d // 2)))
        return found

    npair = width // PAIR
    cuts = [0, npair // 6, npair * 2 // 3, npair]

    def backward(n, prev=()):
        return attn_bwd(q, k, v, mix, do, lse, shard, rb, cuts[n], cuts[n + 1] - cuts[n], prev)

    dq, dkv = backward(0)
    fc_got, out_got = over("shard", fc_theirs, 1), over("shard", out_theirs, 1)
    dq, dkv, fc_got, out_got = hold((dq, dkv, fc_got, out_got))
    fc_half = plus(fc_mine, fc_got)
    out_half = plus(out_mine, out_got)
    out_half = jnp.swapaxes(out_half.reshape(nz, nq, dsh // nq, width), 0, 1)
    away, kept = halve(jnp.concatenate([fc_half, out_half], axis=2))
    dq, dkv, away, kept = hold((dq, dkv, away, kept))
    got = cross(away, 0)
    dq, dkv = backward(1, (dq, dkv))
    dq, dkv, got = hold((dq, dkv, got))
    both = plus(kept, got)
    dq, dkv, both = hold((dq, dkv, both))
    got = cross(both[1], 1)
    dq, dkv = backward(2, (dq, dkv))
    dq, dkv, got, own_proj = hold((dq, dkv, got, own_proj))
    quarter = plus(both[0], got)
    empty = jnp.zeros_like(quarter)
    quarter = jnp.stack(
        [jnp.where(core == 0, quarter, empty), jnp.where(core == 0, empty, quarter)], axis=1
    )
    dq, dkv, quarter = hold((dq, dkv, quarter))
    own_fc = lax.psum_scatter(
        quarter.reshape(-1, width), "shard", scatter_dimension=0, tiled=True
    )
    proj_got = cross(own_proj, 0)
    qkv_mine, qkv_theirs = grads_call(h1, dq, dkv, shard, ns)
    dq, dkv, qkv_mine, qkv_theirs, proj_got = hold((dq, dkv, qkv_mine, qkv_theirs, proj_got))
    qkv_got = over("shard", qkv_theirs, 1)
    proj = plus(own_proj, proj_got)
    proj_got = cross(proj, 1)
    last_part, ig = dh1_call(bundle, wa, wk, tokens, vecs, dq, dkv, dx1, sums, fc_sums, last, shard)
    last_part, qkv_got, proj_got = hold((last_part, qkv_got, proj_got))
    own = lax.psum_scatter(last_part.reshape(-1, width), "shard", scatter_dimension=0, tiled=True)

    qkv_half = plus(qkv_mine, qkv_got).reshape(nz, nq, 3 * dsh // nq, width)
    away, kept = halve(jnp.swapaxes(qkv_half, 0, 1))
    got = cross(away, 0)
    proj = rest_of_rep(plus(proj, proj_got))
    got, proj = hold((got, proj))
    both = plus(kept, got)
    got = cross(both[1], 1)
    part = spread(rest_of_rep(own_fc)[None], 0)
    got, part = hold((got, part))
    qkv_z = by_z(plus(both[0], got))
    part = spread(part, 1)
    natural = quarters(part)
    sum_fc = jnp.concatenate([n[:dsh] for n in natural], axis=1).astype(F32)
    sum_out = jnp.concatenate([n[dsh:] for n in natural], axis=0).astype(F32)
    sum_proj = proj.astype(F32)
    sum_fc, sum_out, sum_proj, *qkv_z = hold((sum_fc, sum_out, sum_proj, *qkv_z))
    qkv_part = rest_of_rep(plus(*qkv_z))[None]
    own, qkv_part = hold((own, qkv_part))
    qkv_part = spread(qkv_part, 0)

    layout = small_layout(dsh, nq)
    mine = own[:EXTRA, : max(size for _, size in layout)]
    small = small_call([mine] + [over("rep", mine, b) for b in range(1, nr)], layout)
    input_grad = finish_call(ig, own, tokens, vecs)
    sum_qkv = jnp.concatenate(quarters(spread(qkv_part, 1))).astype(F32)

    return (
        out,
        input_grad,
        small[0],
        small[1],
        jnp.concatenate([sum_qkv[j * dsh : (j + 1) * dsh] for j in range(3)], axis=1),
        small[2],
        sum_out,
        small[3],
        small[4],
        small[5],
        sum_fc,
        small[6],
        sum_proj,
        small[7],
    )


def solution(mesh):
    rows = P(("rep", "shard"), None)
    mat = P("shard", None)
    vec = P("shard")
    return jax.shard_map(
        local,
        mesh=mesh,
        in_specs=(
            rows,
            vec,
            vec,
            mat,
            vec,
            mat,
            vec,
            vec,
            vec,
            mat,
            vec,
            mat,
            vec,
            rows,
            rows,
            P(("rep", "shard")),
        ),
        out_specs=(rows, rows, vec, vec, mat, vec, mat, vec, vec, vec, mat, vec, mat, vec),
        check_vma=False,
    )
```

```python
import jax
import jax.numpy as jnp
from jax import lax
from jax.experimental import pallas as pl
from jax.experimental.pallas import tpu as pltpu
from jax.sharding import PartitionSpec as P

F32 = jnp.float32
BF = jnp.bfloat16
HEAD = 64
PR_DEV = 128
PAIR = 2 * HEAD
SCALE = 0.125
EPS = 1e-05
NEG = -1e30
VMEM_LIMIT = 60 * 1024 * 1024
EXTRA = 16


def dot_nt(a, b):
    return lax.dot_general(a, b, (((1,), (1,)), ((), ())), preferred_element_type=F32)


def dot_nn(a, b):
    return lax.dot_general(a, b, (((1,), (0,)), ((), ())), preferred_element_type=F32)


def dot_tn(a, b):
    return lax.dot_general(a, b, (((0,), (0,)), ((), ())), preferred_element_type=F32)


def normalize(values):
    centered = values - jnp.mean(values, axis=-1, keepdims=True)
    inv = lax.rsqrt(jnp.mean(centered * centered, axis=-1, keepdims=True) + EPS)
    return centered * inv, inv


def norm_back(e, z, inv):
    return inv * (
        e - jnp.mean(e, axis=-1, keepdims=True) - z * jnp.mean(e * z, axis=-1, keepdims=True)
    )


def cost(flops, nbytes, trans=0):
    return pl.CostEstimate(flops=int(flops), bytes_accessed=int(nbytes), transcendentals=int(trans))


def fixed(shape):
    return pl.BlockSpec(shape, lambda *_: (0,) * len(shape))


def pack_call(tokens, w_qkv, half):
    dsh, width = w_qkv.shape[0], tokens.shape[1]
    kw = width // 2
    rows = dsh if dsh % 32 else dsh // 2

    def kern(half_ref, t_ref, w_ref, o_ref):
        o_ref[:PR_DEV, :] = t_ref[...]
        for n in range(2):

            @pl.when(half_ref[0] == n)
            def _():
                o_ref[PR_DEV : PR_DEV + dsh, :] = w_ref[:, n * 2 * width : (n * 2 + 1) * width]
                first = width + n * kw
                o_ref[PR_DEV + dsh :, :kw] = w_ref[:rows, first : first + kw]
                if rows < dsh:
                    o_ref[PR_DEV + dsh :, kw:] = w_ref[rows:, first : first + kw]
                else:
                    o_ref[PR_DEV + dsh :, kw:] = jnp.zeros((rows, kw), BF)

    out = (PR_DEV + dsh + rows, width)
    return pl.pallas_call(
        kern,
        grid=(1,),
        in_specs=[
            pl.BlockSpec(memory_space=pltpu.SMEM),
            pl.BlockSpec((PR_DEV, width), lambda i: (0, 0)),
            fixed(w_qkv.shape),
        ],
        out_specs=fixed(out),
        out_shape=jax.ShapeDtypeStruct(out, BF),
        cost_estimate=cost(1, 4 * out[0] * width),
        name="pack",
    )(half, tokens, w_qkv)


def qkv_call(bundle, got, other, tokens, vecs, where):
    ns, count, width = bundle.shape
    tok = tokens.shape[0]
    cont = tok - PR_DEV
    plen = ns * PR_DEV
    keys = plen + cont
    dsh = width // ns
    base = count - PR_DEV
    rows = got.shape[0] * dsh
    kw = width // 2

    def kern(wh_ref, g_ref, got_ref, other_ref, t_ref, vec_ref, h_ref, q_ref, k_ref, v_ref, wa, wk):
        shard, half, core = wh_ref[0], wh_ref[1], wh_ref[2]
        gain, bias, bq, bv = vec_ref[0:1], vec_ref[1:2], vec_ref[2:3], vec_ref[3:4]

        def keep(n, first, piece):
            m = piece.shape[0] * dsh
            wa[n, pl.ds(first, m), :] = piece[:, :dsh].reshape(m, width)
            low = piece[:, dsh:base, :kw]
            if base != 2 * dsh:
                low = jnp.concatenate([low, piece[:, dsh:base, kw:]], axis=1)
            wk[n, pl.ds(first, m), :] = low.reshape(m, kw)

        keep(half, 0, g_ref[:, PR_DEV:, :])
        keep(1 - half, pl.multiple_of(core * rows, rows), got_ref[...])
        keep(1 - half, pl.multiple_of((1 - core) * rows, rows), other_ref[...])

        def to_q(h):
            return ((dot_nn(h, wa[0]) + bq).astype(BF).astype(F32) * SCALE).astype(BF)

        step = 4

        def chunk(x, r0):
            h = (normalize(x.astype(F32))[0] * gain + bias).astype(BF)
            at = pl.ds(r0, h.shape[0])
            h_ref[at, :] = h
            k_ref[at, :kw] = dot_nn(h, wk[0]).astype(BF)
            k_ref[at, kw:] = dot_nn(h, wk[1]).astype(BF)
            v_ref[at, :] = (dot_nn(h, wa[1]) + bv).astype(BF)

        for b in range(0, ns, step):
            x = g_ref[b : b + step, :PR_DEV, :]
            chunk(x.reshape(x.shape[0] * PR_DEV, width), b * PR_DEV)
        chunk(t_ref[PR_DEV:, :], plen)
        own = pl.multiple_of(shard * PR_DEV, PR_DEV)
        q_ref[:PR_DEV, :] = to_q(h_ref[pl.ds(own, PR_DEV), :])
        q_ref[PR_DEV:, :] = to_q(h_ref[plen:, :])

    shape = lambda *r: jax.ShapeDtypeStruct((*r, width), BF)
    vm = pl.BlockSpec(memory_space=pltpu.VMEM)
    return pl.pallas_call(
        kern,
        in_specs=[pl.BlockSpec(memory_space=pltpu.SMEM)] + [vm] * 5,
        out_specs=[vm] * 6,
        out_shape=[
            shape(keys),
            shape(tok),
            shape(keys),
            shape(keys),
            shape(2, width),
            jax.ShapeDtypeStruct((2, width, kw), BF),
        ],
        compiler_params=pltpu.CompilerParams(vmem_limit_bytes=VMEM_LIMIT),
        cost_estimate=cost(2 * width * width * (2 * keys + tok), 2 * width * (6 * keys)),
        name="qkv",
    )(where, bundle, got, other, tokens, vecs)


def attn_fwd(q, k, v, shard, rb):
    tok, width = q.shape
    keys = k.shape[0]
    cont = tok - PR_DEV
    plen = keys - cont
    npair = width // PAIR

    def kern(sh_ref, q_ref, k_ref, v_ref, o_ref, lse_ref):
        sh = sh_ref[0]
        first = lax.broadcasted_iota(jnp.int32, (1, PAIR), 1) < HEAD

        def block(r0, rows, n, offset, masked):
            outs, lses = [], []
            for h in range(2):
                mine = first if h == 0 else jnp.logical_not(first)
                qq = jnp.where(mine, q_ref[pl.ds(r0, rows), :], 0).astype(BF)
                s = dot_nt(qq, k_ref[pl.ds(0, n), :])
                tail = s[:, n - masked :]
                row = lax.broadcasted_iota(jnp.int32, tail.shape, 0)
                col = lax.broadcasted_iota(jnp.int32, tail.shape, 1)
                tail = jnp.where(col <= row + offset, tail, NEG)
                s = tail if masked == n else jnp.concatenate([s[:, : n - masked], tail], axis=1)
                top = jnp.max(s, axis=1, keepdims=True)
                p = jnp.exp(s - top)
                total = jnp.sum(p, axis=1, keepdims=True)
                outs.append(dot_nn(p.astype(BF), v_ref[pl.ds(0, n), :]) * (1.0 / total))
                lses.append(top + jnp.log(total))
            o_ref[pl.ds(r0, rows), :] = jnp.where(first, outs[0], outs[1]).astype(BF)
            turned = jnp.transpose(jnp.where(first, lses[0], lses[1]))
            lse_ref[0, 0:1, pl.ds(r0, rows)] = turned[0:1]
            lse_ref[0, 1:2, pl.ds(r0, rows)] = turned[HEAD : HEAD + 1]

        block(0, PR_DEV, plen, sh * PR_DEV, plen)
        for i in range(cont // rb):
            block(PR_DEV + i * rb, rb, plen + (i + 1) * rb, 0, rb)

    spq = pl.BlockSpec((tok, PAIR), lambda i: (0, i))
    spk = pl.BlockSpec((keys, PAIR), lambda i: (0, i))
    return pl.pallas_call(
        kern,
        grid=(npair,),
        in_specs=[pl.BlockSpec(memory_space=pltpu.SMEM), spq, spk, spk],
        out_specs=[spq, pl.BlockSpec((1, 2, tok), lambda i: (i, 0, 0))],
        out_shape=[
            jax.ShapeDtypeStruct((tok, width), BF),
            jax.ShapeDtypeStruct((npair, 2, tok), F32),
        ],
        compiler_params=pltpu.CompilerParams(vmem_limit_bytes=VMEM_LIMIT),
        cost_estimate=cost(16 * width * tok * keys, 4 * width * (tok + keys)),
        name="attn_fwd",
    )(shard, q, k, v)


def attn_bwd(q, k, v, o, do, lse, shard, rb, low, count, prev=()):
    tok, width = q.shape
    keys = k.shape[0]
    cont = tok - PR_DEV
    plen = keys - cont

    def kern(sh_ref, q_ref, k_ref, v_ref, o_ref, do_ref, lse_ref, *rest):
        dq_ref, dkv_ref, ka, va = rest[len(prev) :]
        sh = sh_ref[0]
        first = lax.broadcasted_iota(jnp.int32, (1, PAIR), 1) < HEAD
        ka[...] = jnp.zeros_like(ka)
        va[...] = jnp.zeros_like(va)
        hr = lax.broadcasted_iota(jnp.int32, (8, PAIR), 0)
        hc = lax.broadcasted_iota(jnp.int32, (8, PAIR), 1)
        pick = jnp.where(hc // HEAD == hr, 1.0, 0.0).astype(F32)

        def block(r0, rows, n, offset, masked):
            prod = o_ref[pl.ds(r0, rows), :].astype(F32) * do_ref[pl.ds(r0, rows), :].astype(F32)
            row_dot = lax.dot_general(
                pick,
                prod,
                (((1,), (1,)), ((), ())),
                precision=lax.Precision.HIGHEST,
                preferred_element_type=F32,
            )
            dqs = []
            for h in range(2):
                mine = first if h == 0 else jnp.logical_not(first)
                qq = jnp.where(mine, q_ref[pl.ds(r0, rows), :], 0).astype(BF)
                gg = jnp.where(mine, do_ref[pl.ds(r0, rows), :], 0).astype(BF)
                kk = k_ref[pl.ds(0, n), :]
                s = dot_nt(kk, qq)
                tail = s[n - masked :]
                col = lax.broadcasted_iota(jnp.int32, tail.shape, 0)
                row = lax.broadcasted_iota(jnp.int32, tail.shape, 1)
                tail = jnp.where(col <= row + offset, tail, NEG)
                s = tail if masked == n else jnp.concatenate([s[: n - masked], tail], axis=0)
                p = jnp.exp(s - lse_ref[0, h : h + 1, pl.ds(r0, rows)])
                dp = dot_nt(v_ref[pl.ds(0, n), :], gg)
                ds = (p * (dp - row_dot[h : h + 1, :])).astype(BF)
                va[pl.ds(0, n), :] += dot_nn(p.astype(BF), gg)
                ka[pl.ds(0, n), :] += dot_nn(ds, qq)
                dqs.append(dot_tn(ds, kk))
            dq_ref[pl.ds(r0, rows), :] = (jnp.where(first, dqs[0], dqs[1]) * SCALE).astype(BF)

        block(0, PR_DEV, plen, sh * PR_DEV, plen)
        for i in range(cont // rb):
            block(PR_DEV + i * rb, rb, plen + (i + 1) * rb, 0, rb)
        dkv_ref[0] = ka[...].astype(BF)
        dkv_ref[1] = va[...].astype(BF)

    spq = pl.BlockSpec((tok, PAIR), lambda i: (0, i + low))
    spk = pl.BlockSpec((keys, PAIR), lambda i: (0, i + low))
    return pl.pallas_call(
        kern,
        grid=(count,),
        in_specs=[
            pl.BlockSpec(memory_space=pltpu.SMEM),
            spq,
            spk,
            spk,
            spq,
            spq,
            pl.BlockSpec((1, 2, tok), lambda i: (i + low, 0, 0)),
        ]
        + [pl.BlockSpec(memory_space=pl.ANY)] * len(prev),
        out_specs=[spq, pl.BlockSpec((2, keys, PAIR), lambda i: (0, 0, i + low))],
        out_shape=[
            jax.ShapeDtypeStruct((tok, width), BF),
            jax.ShapeDtypeStruct((2, keys, width), BF),
        ],
        scratch_shapes=[pltpu.VMEM((keys, PAIR), F32), pltpu.VMEM((keys, PAIR), F32)],
        compiler_params=pltpu.CompilerParams(vmem_limit_bytes=VMEM_LIMIT),
        input_output_aliases={7 + i: i for i in range(len(prev))},
        cost_estimate=cost(40 * count * PAIR * tok * keys, 8 * count * PAIR * (tok + keys)),
        name="attn_bwd",
    )(shard, q, k, v, o, do, lse, *prev)


def out_proj_call(mix, second, tokens, vecs):
    ns, _, width = second.shape
    tok = tokens.shape[0]
    dsh = width // ns

    def kern(o_ref, w_ref, t_ref, vec_ref, x_ref, h_ref):
        wo = w_ref[...].reshape(width, width)
        x1 = t_ref[...].astype(F32) + (dot_nn(o_ref[...], wo) + vec_ref[4:5])
        x_ref[...] = x1
        h_ref[...] = (normalize(x1)[0] * vec_ref[5:6] + vec_ref[6:7]).astype(BF)

    whole = lambda a: pl.BlockSpec(a.shape, lambda i: (0,) * a.ndim)
    return pl.pallas_call(
        kern,
        grid=(1,),
        in_specs=[
            whole(mix),
            pl.BlockSpec((ns, dsh, width), lambda i: (0, 1, 0)),
            whole(tokens),
            whole(vecs),
        ],
        out_specs=[pl.BlockSpec((tok, width), lambda i: (0, 0))] * 2,
        out_shape=[jax.ShapeDtypeStruct((tok, width), F32), jax.ShapeDtypeStruct((tok, width), BF)],
        compiler_params=pltpu.CompilerParams(vmem_limit_bytes=VMEM_LIMIT),
        cost_estimate=cost(2 * width * width * tok, 12 * width * tok),
        name="out_proj",
    )(mix, second, tokens, vecs)


def fc_call(h2, second, got, other, vecs, where):
    ns, _, width = second.shape
    tok = h2.shape[0]
    dsh = width // ns
    half = ns // 2
    nq = len(got) + 1

    def kern(*refs):
        wh_ref, h_ref, own_ref = refs[:3]
        got_refs = refs[3 : 2 + nq]
        other_refs = refs[2 + nq : 1 + 2 * nq]
        vec_ref, g_ref, gp_ref, w_ref = refs[1 + 2 * nq :]
        me, core = wh_ref[0], wh_ref[1]
        step = pl.program_id(0)
        rows = half * dsh

        @pl.when(step == 0)
        def _():
            w_ref[0] = own_ref[...].reshape(width, width)

        for j in range(1, nq):

            @pl.when(step == j)
            def _():
                first = pl.multiple_of(core * rows, rows)
                second_half = pl.multiple_of((1 - core) * rows, rows)
                w_ref[0, pl.ds(first, rows), :] = got_refs[j - 1][...].reshape(rows, width)
                w_ref[0, pl.ds(second_half, rows), :] = other_refs[j - 1][...].reshape(rows, width)

        c = jnp.bitwise_xor(me, step)
        f = dot_nn(h_ref[...], w_ref[0]) + vec_ref[pl.ds(8 + c, 1), :]
        square = f * f
        t = jnp.tanh(0.7978845608028654 * f * (1.0 + 0.044715 * square))
        up = 0.5 * (1.0 + t)
        g_ref[0] = (f * up).astype(BF)
        slope = 0.5 * f * (1.0 - t * t) * (0.7978845608028654 + 0.1070322243 * square)
        gp_ref[0] = (up + slope).astype(BF)

    pick = lambda j, wh: (jnp.bitwise_xor(wh[0], j), 0, 0)
    return pl.pallas_call(
        kern,
        grid_spec=pltpu.PrefetchScalarGridSpec(
            num_scalar_prefetch=1,
            grid=(nq,),
            in_specs=[fixed(h2.shape), fixed((ns, dsh, width))]
            + [fixed(a.shape) for a in got]
            + [fixed(a.shape) for a in other]
            + [fixed(vecs.shape)],
            out_specs=[
                pl.BlockSpec((1, tok, width), pick),
                pl.BlockSpec((1, tok, width), pick),
                pl.BlockSpec((1, width, width), pick),
            ],
        ),
        out_shape=[
            jax.ShapeDtypeStruct((nq, tok, width), BF),
            jax.ShapeDtypeStruct((nq, tok, width), BF),
            jax.ShapeDtypeStruct((nq, width, width), BF),
        ],
        compiler_params=pltpu.CompilerParams(vmem_limit_bytes=VMEM_LIMIT),
        cost_estimate=cost(2 * nq * width * width * tok, 4 * nq * width * (tok + width)),
        name="fc",
    )(where, h2, second, *got, *other, vecs)


def proj_call(g, w_proj, x1, teacher, cotangent, weight, vecs):
    nq, tok, width = g.shape

    def kern(g_ref, w_ref, x_ref, te_ref, co_ref, wt_ref, vec_ref, y_ref, dy_ref, dm_ref, gw_ref, pb_ref, acc, keep):
        i = pl.program_id(0)

        @pl.when(i == 0)
        def _():
            acc[...] = x_ref[...] + vec_ref[7:8]

        @pl.when(i < nq)
        def _():
            keep[i] = g_ref[0]
            acc[...] += dot_nn(g_ref[0], w_ref[...])

        @pl.when(i == nq - 1)
        def _():
            y = acc[...]
            y_ref[...] = y.astype(BF)
            dy = co_ref[...].astype(F32) + wt_ref[...] * (y - te_ref[...].astype(F32))
            dy_ref[...] = dy
            dm = dy.astype(BF)
            dm_ref[...] = dm
            pb_ref[0:1, :] = jnp.sum(dm.astype(F32), axis=0, keepdims=True)
            pb_ref[1:8, :] = jnp.zeros((7, width), F32)

        @pl.when(i >= nq)
        def _():
            gw_ref[...] = dot_tn(keep[i - nq], dm_ref[...]).astype(BF)

    last = nq - 1
    return pl.pallas_call(
        kern,
        grid=(2 * nq,),
        in_specs=[
            pl.BlockSpec((1, tok, width), lambda i: (jnp.minimum(i, last), 0, 0)),
            pl.BlockSpec((width, width), lambda i: (jnp.minimum(i, last), 0)),
        ]
        + [fixed(a.shape) for a in (x1, teacher, cotangent, weight, vecs)],
        out_specs=[
            fixed((tok, width)),
            fixed((tok, width)),
            fixed((tok, width)),
            pl.BlockSpec((width, width), lambda i: (jnp.maximum(i - nq, 0), 0)),
            fixed((8, width)),
        ],
        out_shape=[
            jax.ShapeDtypeStruct((tok, width), BF),
            jax.ShapeDtypeStruct((tok, width), F32),
            jax.ShapeDtypeStruct((tok, width), BF),
            jax.ShapeDtypeStruct((nq * width, width), BF),
            jax.ShapeDtypeStruct((8, width), F32),
        ],
        scratch_shapes=[pltpu.VMEM((tok, width), F32), pltpu.VMEM((nq, tok, width), BF)],
        compiler_params=pltpu.CompilerParams(vmem_limit_bytes=VMEM_LIMIT),
        cost_estimate=cost(4 * nq * width * width * tok, 2 * nq * width * (tok + 2 * width)),
        name="proj",
    )(g, w_proj, x1, teacher, cotangent, weight, vecs)


def mid_call(dm, dy, w_proj, gp, h2, w_fc, x1, mix, second, vecs, core):
    nq, tok, width = gp.shape
    ns = second.shape[0]
    dsh = width // ns
    nz = ns // 2

    def kern(*refs):
        (co_ref, dm_ref, dy_ref, wp_ref, gp_ref, h_ref, wf_ref, x_ref, o_ref, wo_ref, vec_ref) = refs[:11]
        (fm_ref, ft_ref, om_ref, ot_ref, dx_ref, do_ref, sm_ref, fb_ref, ht, dh2) = refs[11:]
        j = pl.program_id(0)
        total = lambda m: jnp.sum(m, axis=0, keepdims=True)

        def split(gw, mine, theirs):
            gw = gw.astype(BF).reshape(nz, 2, dsh, width)
            for c in range(2):

                @pl.when(co_ref[0] == c)
                def _():
                    mine[...] = gw[:, c]
                    theirs[...] = gw[:, 1 - c]

        @pl.when(j == 0)
        def _():
            ht[...] = jnp.transpose(h_ref[...])
            dh2[...] = jnp.zeros_like(dh2)

        @pl.when(j < nq)
        def _():
            dg = dot_nt(dm_ref[...], wp_ref[...])
            df = (dg * gp_ref[0].astype(F32)).astype(BF)
            fb_ref[pl.ds(j, 1), :] = total(df.astype(F32))
            split(dot_nn(ht[...], df), fm_ref.at[0], ft_ref.at[0])
            dh2[...] += dot_nt(df, wf_ref[0])

        @pl.when(j == nq)
        def _():
            z, inv = normalize(x_ref[...])
            grad = dh2[...]
            sm_ref[0:1, :] = total(grad * z)
            sm_ref[1:2, :] = total(grad)
            dx = dy_ref[...] + norm_back(grad * vec_ref[5:6], z, inv)
            dx_ref[...] = dx
            da = dx.astype(BF)
            sm_ref[2:3, :] = total(da.astype(F32))
            do_ref[...] = dot_nt(da, wo_ref[...].reshape(width, width)).astype(BF)
            split(dot_tn(o_ref[...], da), om_ref, ot_ref)

    last = nq - 1
    pick = lambda j: (jnp.minimum(j, last), 0, 0)
    out = pl.BlockSpec((1, nz, dsh, width), lambda j: (jnp.minimum(j, last), 0, 0, 0))
    return pl.pallas_call(
        kern,
        grid=(nq + 1,),
        in_specs=[
            pl.BlockSpec(memory_space=pltpu.SMEM),
            fixed(dm.shape),
            fixed(dy.shape),
            pl.BlockSpec((width, width), lambda j: (jnp.minimum(j, last), 0)),
            pl.BlockSpec((1, tok, width), pick),
            fixed(h2.shape),
            pl.BlockSpec((1, width, width), pick),
            fixed(x1.shape),
            fixed(mix.shape),
            pl.BlockSpec((ns, dsh, width), lambda j: (0, 1, 0)),
            fixed(vecs.shape),
        ],
        out_specs=[
            out,
            out,
            fixed((nz, dsh, width)),
            fixed((nz, dsh, width)),
            fixed((tok, width)),
            fixed((tok, width)),
            fixed((8, width)),
            fixed((nq, width)),
        ],
        out_shape=[
            jax.ShapeDtypeStruct((nq, nz, dsh, width), BF),
            jax.ShapeDtypeStruct((nq, nz, dsh, width), BF),
            jax.ShapeDtypeStruct((nz, dsh, width), BF),
            jax.ShapeDtypeStruct((nz, dsh, width), BF),
            jax.ShapeDtypeStruct((tok, width), F32),
            jax.ShapeDtypeStruct((tok, width), BF),
            jax.ShapeDtypeStruct((8, width), F32),
            jax.ShapeDtypeStruct((nq, width), F32),
        ],
        scratch_shapes=[pltpu.VMEM((width, tok), BF), pltpu.VMEM((tok, width), F32)],
        compiler_params=pltpu.CompilerParams(vmem_limit_bytes=VMEM_LIMIT),
        cost_estimate=cost(
            2 * width * width * tok * (3 * nq + 2), 2 * width * (nq * (tok + 4 * width) + 8 * tok)
        ),
        name="mid",
    )(core, dm, dy, w_proj, gp, h2, w_fc, x1, mix, second, vecs)


def grads_call(h1, dq, dkv, shard, ns):
    keys, width = h1.shape
    tok = dq.shape[0]
    plen = ns * PR_DEV
    dsh = width // ns

    nz = ns // 2

    def kern(sh_ref, h_ref, dq_ref, d_ref, mine, theirs, ht):
        j = pl.program_id(0)

        def split(gw):
            gw = gw.astype(BF).reshape(nz, 2, dsh, width)
            for c in range(2):

                @pl.when(sh_ref[0] % 2 == c)
                def _():
                    mine[...] = gw[:, c]
                    theirs[...] = gw[:, 1 - c]

        @pl.when(j == 0)
        def _():
            ht[...] = jnp.transpose(h_ref[...])

        @pl.when(j < 2)
        def _():
            split(dot_nn(ht[...], d_ref[0]))

        @pl.when(j == 2)
        def _():
            own = pl.ds(pl.multiple_of(sh_ref[0] * PR_DEV, PR_DEV), PR_DEV)
            gq = dot_nn(ht[:, plen:], dq_ref[PR_DEV:, :]) + dot_tn(h_ref[own, :], dq_ref[:PR_DEV, :])
            split(gq)

    return pl.pallas_call(
        kern,
        grid=(3,),
        in_specs=[
            pl.BlockSpec(memory_space=pltpu.SMEM),
            fixed(h1.shape),
            fixed(dq.shape),
            pl.BlockSpec((1, keys, width), lambda j: (jnp.minimum(j, 1), 0, 0)),
        ],
        out_specs=[pl.BlockSpec((nz, dsh, width), lambda j: (0, (j + 1) % 3, 0))] * 2,
        out_shape=[jax.ShapeDtypeStruct((nz, 3 * dsh, width), BF)] * 2,
        scratch_shapes=[pltpu.VMEM((width, keys), BF)],
        compiler_params=pltpu.CompilerParams(vmem_limit_bytes=VMEM_LIMIT),
        cost_estimate=cost(2 * width * width * (2 * keys + tok), 2 * width * 5 * keys),
        name="grads",
    )(shard, h1, dq, dkv)


def small_layout(dsh, nq):
    return [(n, rows * dsh) for n, rows in ((0, 1), (1, 1), (2, 2), (4, 1), (5, 1), (6, 1), (8, nq), (7, 1))]


def dh1_call(bundle, wa, wk, tokens, vecs, dq, dkv, dx1, sums, fc_sums, last, shard):
    ns, _, width = bundle.shape
    tok = tokens.shape[0]
    cont = tok - PR_DEV
    plen = ns * PR_DEV
    nq = fc_sums.shape[0]
    kw = width // 2
    step = cont // PR_DEV
    chunks = ns // step

    def kern(*refs):
        (sh_ref, g_ref, wa_ref, wk_ref, t_ref, vec_ref, dq_ref, dk_ref, dv_ref, dx_ref) = refs[:10]
        (s2_ref, fb_ref, s3_ref, o_ref, ig_ref, sm, part) = refs[10:]
        i = pl.program_id(0)
        wq, wv = wa_ref[0], wa_ref[1]

        def back_kv(dk, dv):
            low = dot_nt(dk[:, :kw], wk_ref[0]) + dot_nt(dk[:, kw:], wk_ref[1])
            return low + dot_nt(dv, wv)

        total = lambda m: jnp.sum(m, axis=0, keepdims=True)

        @pl.when(i == 0)
        def _():
            sm[...] = jnp.zeros_like(sm)
            part[...] = jnp.zeros_like(part)

        def add(dh, z):
            sm[0:1, :] += total(dh * z)
            sm[1:2, :] += total(dh)

        dv = dv_ref[0]
        sm[3:4, :] += total(dv.astype(F32))
        dh = back_kv(dk_ref[0], dv)

        @pl.when(i < chunks)
        def _():
            z, _ = normalize(g_ref[...].reshape(cont, width).astype(F32))
            add(dh, z)
            o_ref[pl.ds(i * step, step), EXTRA:, :] = dh.astype(BF).reshape(step, PR_DEV, width)

        @pl.when(i == sh_ref[0] // step)
        def _():
            own = pl.ds(pl.multiple_of((sh_ref[0] % step) * PR_DEV, PR_DEV), PR_DEV)
            z, _ = normalize(t_ref[:PR_DEV, :].astype(F32))
            part = dot_nt(dq_ref[:PR_DEV, :], wq)
            add(part, z)
            both = back_kv(dk_ref[0, own, :], dv_ref[0, own, :])
            o_ref[sh_ref[0], EXTRA:, :] = (both + part).astype(BF)

        @pl.when(i == chunks)
        def _():
            z, inv = normalize(t_ref[PR_DEV:, :].astype(F32))
            full = dh + dot_nt(dq_ref[PR_DEV:, :], wq)
            add(full, z)
            ig_ref[PR_DEV:, :] = dx_ref[PR_DEV:, :] + norm_back(full * vec_ref[0:1], z, inv)
            ig_ref[:PR_DEV, :] = dx_ref[:PR_DEV, :]
            sm[2:3, :] = total(dq_ref[...].astype(F32))
            sm[4:5, :] = s2_ref[2:3, :]
            sm[5:7, :] = s2_ref[0:2, :]
            sm[7:8, :] = s3_ref[0:1, :]
            sm[8 : 8 + nq, :] = fb_ref[...]
            for b in range(ns):
                for n, (first, size) in enumerate(small_layout(width // ns, nq)):
                    row, off = divmod(b * size, width)
                    part[n : n + 1, :size] = sm[first + row : first + row + 1, off : off + size]
                o_ref[b, :EXTRA, :] = part[...].astype(BF)

    chunk = lambda k: pl.BlockSpec((1, cont, width), lambda i: (k, i, 0))
    out = (ns, EXTRA + PR_DEV, width)
    return pl.pallas_call(
        kern,
        grid=(chunks + 1,),
        in_specs=[
            pl.BlockSpec(memory_space=pltpu.SMEM),
            pl.BlockSpec((step, PR_DEV, width), lambda i: (jnp.minimum(i, chunks - 1), 0, 0)),
            fixed(wa.shape),
            fixed(wk.shape),
            fixed(tokens.shape),
            fixed(vecs.shape),
            fixed(dq.shape),
            chunk(0),
            chunk(1),
        ]
        + [fixed(a.shape) for a in (dx1, sums, fc_sums, last)],
        out_specs=[fixed(out), fixed((tok, width))],
        out_shape=[jax.ShapeDtypeStruct(out, BF), jax.ShapeDtypeStruct((tok, width), F32)],
        scratch_shapes=[pltpu.VMEM((EXTRA, width), F32)] * 2,
        compiler_params=pltpu.CompilerParams(vmem_limit_bytes=VMEM_LIMIT),
        cost_estimate=cost(
            2 * width * width * (2 * (plen + cont) + tok), 2 * width * (5 * plen + 10 * cont)
        ),
        name="dh1",
    )(shard, bundle, wa, wk, tokens, vecs, dq, dkv, dkv, dx1, sums, fc_sums, last)


def finish_call(grad, summed, tokens, vecs):
    tok, width = grad.shape

    def kern(g_ref, s_ref, t_ref, vec_ref, o_ref):
        z, inv = normalize(t_ref[...].astype(F32))
        e = s_ref[EXTRA:, :].astype(F32) * vec_ref[0:1]
        o_ref[...] = g_ref[...] + norm_back(e, z, inv)

    block = pl.BlockSpec((PR_DEV, width), lambda i: (0, 0))
    return pl.pallas_call(
        kern,
        grid=(1,),
        in_specs=[
            block,
            pl.BlockSpec(summed.shape, lambda i: (0, 0)),
            block,
            pl.BlockSpec(vecs.shape, lambda i: (0, 0)),
        ],
        out_specs=block,
        out_shape=jax.ShapeDtypeStruct((tok, width), F32),
        input_output_aliases={0: 0},
        cost_estimate=cost(20 * PR_DEV * width, 12 * PR_DEV * width),
        name="finish",
    )(grad, summed, tokens, vecs)


def over(axis, values, bit):
    n = lax.axis_size(axis)
    return lax.ppermute(values, axis, [(i, i ^ bit) for i in range(n)])


def cross(values, step):
    nr, ns = lax.axis_size("rep"), lax.axis_size("shard")
    pairs = [
        (r * ns + c, (r ^ (1 << ((c % 2) ^ step))) * ns + c) for r in range(nr) for c in range(ns)
    ]
    return lax.ppermute(values, ("rep", "shard"), pairs)


def rep_sum_small(values):
    n = lax.axis_size("rep")
    terms = [values] + [over("rep", values, b) for b in range(1, n)]
    terms = [t.astype(F32) for t in terms]
    while len(terms) > 1:
        terms = [terms[i] + terms[i + 1] for i in range(0, len(terms), 2)]
    return terms[0]


def small_call(terms, layout):
    def kern(*refs):
        values = [r[...].astype(F32) for r in refs[: len(terms)]]
        while len(values) > 1:
            values = [values[i] + values[i + 1] for i in range(0, len(values), 2)]
        for n, (_, size) in enumerate(layout):
            refs[len(terms) + n][...] = values[0][n, :size]

    return pl.pallas_call(
        kern,
        out_shape=[jax.ShapeDtypeStruct((size,), F32) for _, size in layout],
        cost_estimate=cost(terms[0].size * len(terms), 2 * terms[0].size * len(terms)),
        name="small",
    )(*terms)


def local(
    tokens,
    ln1_gain,
    ln1_bias,
    w_qkv,
    qv_bias,
    w_out,
    out_bias,
    ln2_gain,
    ln2_bias,
    w_fc,
    fc_bias,
    w_proj,
    proj_bias,
    teacher,
    cotangent,
    valid_mask,
):
    ns = lax.axis_size("shard")
    nr = lax.axis_size("rep")
    me = lax.axis_index("shard").astype(jnp.int32)
    shard = me.reshape(1)
    tok, width = tokens.shape
    nq = min(nr, w_fc.shape[1] // width)
    group = lax.axis_index("rep").astype(jnp.int32) % nq
    dsh = width // ns
    rb = 256

    core = me % 2
    half = lax.axis_index("rep").astype(jnp.int32)
    half = jnp.bitwise_xor(half, half // 2) % 2
    bundle = lax.all_gather(pack_call(tokens, w_qkv, half.reshape(1)), "shard")
    fc_own = lax.dynamic_slice_in_dim(w_fc, group * width, width, 1)
    mask_f = valid_mask.astype(F32)
    counts = jnp.sum(mask_f.reshape(-1, PR_DEV), axis=1).astype(BF)
    parts = [ln1_gain, ln1_bias, qv_bias, out_bias, ln2_gain, ln2_bias, proj_bias, fc_bias]
    offs = [0]
    for p in parts:
        offs.append(offs[-1] + p.shape[0])
    packed = jnp.concatenate(parts + [counts])
    packed = jnp.pad(packed, (0, (-packed.shape[0]) % 128))
    params = lax.all_gather(packed.reshape(1, -1), "shard", axis=0, tiled=True).astype(F32)
    vecs = jnp.concatenate(
        [params[:, offs[i] : offs[i + 1]].reshape(-1, width) for i in range(8)]
        + [jnp.zeros((16 - 8 - nq, width), F32)]
    )
    count = jnp.sum(params[:, offs[8] : offs[8] + counts.shape[0]])
    token_total = rep_sum_small(jnp.full((8, 128), count, F32))[0, 0]
    factor = tok * nr * ns / token_total
    weight = (factor * mask_f).reshape(tok, 1)

    second = jnp.concatenate([fc_own, w_out])
    second, vecs, weight = lax.optimization_barrier((second, vecs, weight))
    second = lax.all_gather(second, "shard")
    bundle, w_proj = lax.optimization_barrier((bundle, w_proj))
    full_proj = lax.all_gather(w_proj, "shard", axis=0, tiled=True)
    qkv_piece = lax.dynamic_slice_in_dim(bundle, core * (ns // 2), ns // 2, 0)
    qkv_far = cross(qkv_piece[:, PR_DEV:], 0)
    qkv_near = over("shard", qkv_far, 1)
    h1, q, k, v, wa, wk = qkv_call(
        bundle, qkv_far, qkv_near, tokens, vecs, jnp.stack([me, half, core])
    )
    q, k, v, second = lax.optimization_barrier((q, k, v, second))
    piece = lax.dynamic_slice_in_dim(second, core * (ns // 2), ns // 2, 0)[:, :dsh]
    q, k, v, piece = lax.optimization_barrier((q, k, v, piece))
    mix, lse = attn_fwd(q, k, v, shard, rb)
    mix, lse, *got = lax.optimization_barrier(
        (mix, lse, *[over("rep", piece, j) for j in range(1, nq)])
    )
    other = [over("shard", g, 1) for g in got]
    x1, h2 = out_proj_call(mix, second, tokens, vecs)
    g, gp, full_fc = fc_call(h2, second, got, other, vecs, jnp.stack([group, core]))
    out, dy, dm, grad_proj, last = proj_call(g, full_proj, x1, teacher, cotangent, weight, vecs)
    own_proj = lax.psum_scatter(grad_proj, "shard", scatter_dimension=0, tiled=True)
    fc_mine, fc_theirs, out_mine, out_theirs, dx1, do, sums, fc_sums = mid_call(
        dm, dy, full_proj, gp, h2, full_fc, x1, mix, second, vecs, core.reshape(1)
    )
    nz = ns // 2
    z = me // 2
    pick = lambda a, n: lax.dynamic_index_in_dim(a, n, 0, keepdims=False)
    plus = lambda *terms: sum(t.astype(F32) for t in terms).astype(BF)
    hold = lax.optimization_barrier

    def rep_sends(parts):
        return [pick(parts, jnp.bitwise_xor(group, b)) for b in range(nq)]

    def by_rep(sends):
        return sends[:1] + [over("rep", sends[b], b) for b in range(1, nq)]

    def by_z(parts):
        far = [over("shard", pick(parts, jnp.bitwise_xor(z, b)), 2 * b) for b in range(1, nz)]
        return [pick(parts, z)] + far

    def rest_of_rep(part):
        bit = nq
        while bit < nr:
            part = plus(part, over("rep", part, bit))
            bit *= 2
        return part

    first = jnp.where(core == 0, 1, 2)

    def halve(parts):
        at = lambda *ds: jnp.stack([pick(parts, jnp.bitwise_xor(group, d)) for d in ds])
        return at(first, 3), at(0, 3 - first)

    def spread(part, step):
        return jnp.concatenate([part, cross(part, step)])

    def quarters(relative):
        found = []
        for n in range(nq):
            d = jnp.bitwise_xor(group, n)
            found.append(pick(relative, jnp.where(core == 0, d, d % 2 * 2 + d // 2)))
        return found

    npair = width // PAIR
    cuts = [0, npair // 6, npair * 2 // 3, npair]

    def backward(n, prev=()):
        return attn_bwd(q, k, v, mix, do, lse, shard, rb, cuts[n], cuts[n + 1] - cuts[n], prev)

    dq, dkv = backward(0)
    fc_got, out_got = over("shard", fc_theirs, 1), over("shard", out_theirs, 1)
    dq, dkv, fc_got, out_got = hold((dq, dkv, fc_got, out_got))
    fc_half = plus(fc_mine, fc_got)
    out_half = plus(out_mine, out_got)
    out_half = jnp.swapaxes(out_half.reshape(nz, nq, dsh // nq, width), 0, 1)
    away, kept = halve(jnp.concatenate([fc_half, out_half], axis=2))
    dq, dkv, away, kept = hold((dq, dkv, away, kept))
    got = cross(away, 0)
    dq, dkv = backward(1, (dq, dkv))
    dq, dkv, got = hold((dq, dkv, got))
    both = plus(kept, got)
    dq, dkv, both = hold((dq, dkv, both))
    got = cross(both[1], 1)
    dq, dkv = backward(2, (dq, dkv))
    dq, dkv, got, own_proj = hold((dq, dkv, got, own_proj))
    quarter = plus(both[0], got)
    slot = lax.broadcasted_iota(jnp.int32, (1, 2, 1, 1), 1)
    quarter = jnp.where(slot == core, quarter[:, None], jnp.zeros((), BF))
    dq, dkv, quarter = hold((dq, dkv, quarter))
    own_fc = lax.psum_scatter(
        quarter.reshape(-1, width), "shard", scatter_dimension=0, tiled=True
    )
    proj_got = cross(own_proj, 0)
    qkv_mine, qkv_theirs = grads_call(h1, dq, dkv, shard, ns)
    dq, dkv, qkv_mine, qkv_theirs, proj_got = hold((dq, dkv, qkv_mine, qkv_theirs, proj_got))
    qkv_got = over("shard", qkv_theirs, 1)
    proj = plus(own_proj, proj_got)
    proj_got = cross(proj, 1)
    last_part, ig = dh1_call(bundle, wa, wk, tokens, vecs, dq, dkv, dx1, sums, fc_sums, last, shard)
    last_part, qkv_got, proj_got = hold((last_part, qkv_got, proj_got))
    own = lax.psum_scatter(last_part.reshape(-1, width), "shard", scatter_dimension=0, tiled=True)

    qkv_half = plus(qkv_mine, qkv_got).reshape(nz, nq, 3 * dsh // nq, width)
    away, kept = halve(jnp.swapaxes(qkv_half, 0, 1))
    got = cross(away, 0)
    proj = rest_of_rep(plus(proj, proj_got))
    got, proj = hold((got, proj))
    both = plus(kept, got)
    got = cross(both[1], 1)
    part = spread(rest_of_rep(own_fc)[None], 0)
    got, part = hold((got, part))
    qkv_z = by_z(plus(both[0], got))
    part = spread(part, 1)
    natural = quarters(part)
    sum_fc = jnp.concatenate([n[:dsh] for n in natural], axis=1).astype(F32)
    sum_out = jnp.concatenate([n[dsh:] for n in natural], axis=0).astype(F32)
    sum_proj = proj.astype(F32)
    sum_fc, sum_out, sum_proj, *qkv_z = hold((sum_fc, sum_out, sum_proj, *qkv_z))
    qkv_part = rest_of_rep(plus(*qkv_z))[None]
    own, qkv_part = hold((own, qkv_part))
    qkv_part = spread(qkv_part, 0)

    layout = small_layout(dsh, nq)
    mine = own[:EXTRA, : max(size for _, size in layout)]
    small = small_call([mine] + [over("rep", mine, b) for b in range(1, nr)], layout)
    input_grad = finish_call(ig, own, tokens, vecs)
    sum_qkv = jnp.concatenate(quarters(spread(qkv_part, 1))).astype(F32)

    return (
        out,
        input_grad,
        small[0],
        small[1],
        jnp.concatenate([sum_qkv[j * dsh : (j + 1) * dsh] for j in range(3)], axis=1),
        small[2],
        sum_out,
        small[3],
        small[4],
        small[5],
        sum_fc,
        small[6],
        sum_proj,
        small[7],
    )


def solution(mesh):
    rows = P(("rep", "shard"), None)
    mat = P("shard", None)
    vec = P("shard")
    return jax.shard_map(
        local,
        mesh=mesh,
        in_specs=(
            rows,
            vec,
            vec,
            mat,
            vec,
            mat,
            vec,
            vec,
            vec,
            mat,
            vec,
            mat,
            vec,
            rows,
            rows,
            P(("rep", "shard")),
        ),
        out_specs=(rows, rows, vec, vec, mat, vec, mat, vec, vec, vec, mat, vec, mat, vec),
        check_vma=False,
    )
```

```python
import jax
import jax.numpy as jnp
from jax import lax
from jax.experimental import pallas as pl
from jax.experimental.pallas import tpu as pltpu
from jax.sharding import PartitionSpec as P

F32 = jnp.float32
BF = jnp.bfloat16
HEAD = 64
PR_DEV = 128
PAIR = 2 * HEAD
SCALE = 0.125
EPS = 1e-05
NEG = -1e30
VMEM_LIMIT = 60 * 1024 * 1024
EXTRA = 8


def dot_nt(a, b):
    return lax.dot_general(a, b, (((1,), (1,)), ((), ())), preferred_element_type=F32)


def dot_nn(a, b):
    return lax.dot_general(a, b, (((1,), (0,)), ((), ())), preferred_element_type=F32)


def dot_tn(a, b):
    return lax.dot_general(a, b, (((0,), (0,)), ((), ())), preferred_element_type=F32)


def normalize(values):
    centered = values - jnp.mean(values, axis=-1, keepdims=True)
    inv = lax.rsqrt(jnp.mean(centered * centered, axis=-1, keepdims=True) + EPS)
    return centered * inv, inv


def norm_back(e, z, inv):
    return inv * (
        e - jnp.mean(e, axis=-1, keepdims=True) - z * jnp.mean(e * z, axis=-1, keepdims=True)
    )


def cost(flops, nbytes, trans=0):
    return pl.CostEstimate(flops=int(flops), bytes_accessed=int(nbytes), transcendentals=int(trans))


def fixed(shape):
    return pl.BlockSpec(shape, lambda *_: (0,) * len(shape))


def pack_call(tokens, w_qkv, half):
    dsh, width = w_qkv.shape[0], tokens.shape[1]
    kw = width // 2
    rows = dsh if dsh % 32 else dsh // 2

    def kern(half_ref, t_ref, w_ref, o_ref):
        o_ref[:PR_DEV, :] = t_ref[...]
        for n in range(2):

            @pl.when(half_ref[0] == n)
            def _():
                o_ref[PR_DEV : PR_DEV + dsh, :] = w_ref[:, n * 2 * width : (n * 2 + 1) * width]
                first = width + n * kw
                o_ref[PR_DEV + dsh :, :kw] = w_ref[:rows, first : first + kw]
                if rows < dsh:
                    o_ref[PR_DEV + dsh :, kw:] = w_ref[rows:, first : first + kw]
                else:
                    o_ref[PR_DEV + dsh :, kw:] = jnp.zeros((rows, kw), BF)

    out = (PR_DEV + dsh + rows, width)
    return pl.pallas_call(
        kern,
        grid=(1,),
        in_specs=[
            pl.BlockSpec(memory_space=pltpu.SMEM),
            pl.BlockSpec((PR_DEV, width), lambda i: (0, 0)),
            fixed(w_qkv.shape),
        ],
        out_specs=fixed(out),
        out_shape=jax.ShapeDtypeStruct(out, BF),
        cost_estimate=cost(1, 4 * out[0] * width),
        name="pack",
    )(half, tokens, w_qkv)


def qkv_call(bundle, got, other, tokens, vecs, where):
    ns, count, width = bundle.shape
    tok = tokens.shape[0]
    cont = tok - PR_DEV
    plen = ns * PR_DEV
    keys = plen + cont
    dsh = width // ns
    base = count - PR_DEV
    rows = got.shape[0] * dsh
    kw = width // 2

    def kern(wh_ref, g_ref, got_ref, other_ref, t_ref, vec_ref, h_ref, q_ref, k_ref, v_ref, wa, wk):
        shard, half, core = wh_ref[0], wh_ref[1], wh_ref[2]
        gain, bias, bq, bv = vec_ref[0:1], vec_ref[1:2], vec_ref[2:3], vec_ref[3:4]

        def keep(n, first, piece):
            m = piece.shape[0] * dsh
            wa[n, pl.ds(first, m), :] = piece[:, :dsh].reshape(m, width)
            low = piece[:, dsh:base, :kw]
            if base != 2 * dsh:
                low = jnp.concatenate([low, piece[:, dsh:base, kw:]], axis=1)
            wk[n, pl.ds(first, m), :] = low.reshape(m, kw)

        keep(half, 0, g_ref[:, PR_DEV:, :])
        keep(1 - half, pl.multiple_of(core * rows, rows), got_ref[...])
        keep(1 - half, pl.multiple_of((1 - core) * rows, rows), other_ref[...])

        def to_q(h):
            return ((dot_nn(h, wa[0]) + bq).astype(BF).astype(F32) * SCALE).astype(BF)

        step = 4

        def chunk(x, r0):
            h = (normalize(x.astype(F32))[0] * gain + bias).astype(BF)
            at = pl.ds(r0, h.shape[0])
            h_ref[at, :] = h
            k_ref[at, :kw] = dot_nn(h, wk[0]).astype(BF)
            k_ref[at, kw:] = dot_nn(h, wk[1]).astype(BF)
            v_ref[at, :] = (dot_nn(h, wa[1]) + bv).astype(BF)

        for b in range(0, ns, step):
            x = g_ref[b : b + step, :PR_DEV, :]
            chunk(x.reshape(x.shape[0] * PR_DEV, width), b * PR_DEV)
        chunk(t_ref[PR_DEV:, :], plen)
        own = pl.multiple_of(shard * PR_DEV, PR_DEV)
        q_ref[:PR_DEV, :] = to_q(h_ref[pl.ds(own, PR_DEV), :])
        q_ref[PR_DEV:, :] = to_q(h_ref[plen:, :])

    shape = lambda *r: jax.ShapeDtypeStruct((*r, width), BF)
    vm = pl.BlockSpec(memory_space=pltpu.VMEM)
    return pl.pallas_call(
        kern,
        in_specs=[pl.BlockSpec(memory_space=pltpu.SMEM)] + [vm] * 5,
        out_specs=[vm] * 6,
        out_shape=[
            shape(keys),
            shape(tok),
            shape(keys),
            shape(keys),
            shape(2, width),
            jax.ShapeDtypeStruct((2, width, kw), BF),
        ],
        compiler_params=pltpu.CompilerParams(vmem_limit_bytes=VMEM_LIMIT),
        cost_estimate=cost(2 * width * width * (2 * keys + tok), 2 * width * (6 * keys)),
        name="qkv",
    )(where, bundle, got, other, tokens, vecs)


def attn_fwd(q, k, v, shard, rb):
    tok, width = q.shape
    keys = k.shape[0]
    cont = tok - PR_DEV
    plen = keys - cont
    npair = width // PAIR

    def kern(sh_ref, q_ref, k_ref, v_ref, o_ref, lse_ref):
        sh = sh_ref[0]
        first = lax.broadcasted_iota(jnp.int32, (1, PAIR), 1) < HEAD

        def block(r0, rows, n, offset, masked):
            outs, lses = [], []
            for h in range(2):
                mine = first if h == 0 else jnp.logical_not(first)
                qq = jnp.where(mine, q_ref[pl.ds(r0, rows), :], 0).astype(BF)
                s = dot_nt(qq, k_ref[pl.ds(0, n), :])
                tail = s[:, n - masked :]
                row = lax.broadcasted_iota(jnp.int32, tail.shape, 0)
                col = lax.broadcasted_iota(jnp.int32, tail.shape, 1)
                tail = jnp.where(col <= row + offset, tail, NEG)
                s = tail if masked == n else jnp.concatenate([s[:, : n - masked], tail], axis=1)
                top = jnp.max(s, axis=1, keepdims=True)
                p = jnp.exp(s - top)
                total = jnp.sum(p, axis=1, keepdims=True)
                outs.append(dot_nn(p.astype(BF), v_ref[pl.ds(0, n), :]) * (1.0 / total))
                lses.append(top + jnp.log(total))
            o_ref[pl.ds(r0, rows), :] = jnp.where(first, outs[0], outs[1]).astype(BF)
            turned = jnp.transpose(jnp.where(first, lses[0], lses[1]))
            lse_ref[0, 0:1, pl.ds(r0, rows)] = turned[0:1]
            lse_ref[0, 1:2, pl.ds(r0, rows)] = turned[HEAD : HEAD + 1]

        block(0, PR_DEV, plen, sh * PR_DEV, plen)
        for i in range(cont // rb):
            block(PR_DEV + i * rb, rb, plen + (i + 1) * rb, 0, rb)

    spq = pl.BlockSpec((tok, PAIR), lambda i: (0, i))
    spk = pl.BlockSpec((keys, PAIR), lambda i: (0, i))
    return pl.pallas_call(
        kern,
        grid=(npair,),
        in_specs=[pl.BlockSpec(memory_space=pltpu.SMEM), spq, spk, spk],
        out_specs=[spq, pl.BlockSpec((1, 2, tok), lambda i: (i, 0, 0))],
        out_shape=[
            jax.ShapeDtypeStruct((tok, width), BF),
            jax.ShapeDtypeStruct((npair, 2, tok), F32),
        ],
        compiler_params=pltpu.CompilerParams(vmem_limit_bytes=VMEM_LIMIT),
        cost_estimate=cost(16 * width * tok * keys, 4 * width * (tok + keys)),
        name="attn_fwd",
    )(shard, q, k, v)


def attn_bwd(q, k, v, o, do, lse, shard, rb, low, count, prev=()):
    tok, width = q.shape
    keys = k.shape[0]
    cont = tok - PR_DEV
    plen = keys - cont

    def kern(sh_ref, q_ref, k_ref, v_ref, o_ref, do_ref, lse_ref, *rest):
        dq_ref, dkv_ref, ka, va = rest[len(prev) :]
        sh = sh_ref[0]
        first = lax.broadcasted_iota(jnp.int32, (1, PAIR), 1) < HEAD
        ka[...] = jnp.zeros_like(ka)
        va[...] = jnp.zeros_like(va)
        hr = lax.broadcasted_iota(jnp.int32, (8, PAIR), 0)
        hc = lax.broadcasted_iota(jnp.int32, (8, PAIR), 1)
        pick = jnp.where(hc // HEAD == hr, 1.0, 0.0).astype(F32)

        def block(r0, rows, n, offset, masked):
            prod = o_ref[pl.ds(r0, rows), :].astype(F32) * do_ref[pl.ds(r0, rows), :].astype(F32)
            row_dot = lax.dot_general(
                pick,
                prod,
                (((1,), (1,)), ((), ())),
                precision=lax.Precision.HIGHEST,
                preferred_element_type=F32,
            )
            dqs = []
            for h in range(2):
                mine = first if h == 0 else jnp.logical_not(first)
                qq = jnp.where(mine, q_ref[pl.ds(r0, rows), :], 0).astype(BF)
                gg = jnp.where(mine, do_ref[pl.ds(r0, rows), :], 0).astype(BF)
                kk = k_ref[pl.ds(0, n), :]
                s = dot_nt(kk, qq)
                tail = s[n - masked :]
                col = lax.broadcasted_iota(jnp.int32, tail.shape, 0)
                row = lax.broadcasted_iota(jnp.int32, tail.shape, 1)
                tail = jnp.where(col <= row + offset, tail, NEG)
                s = tail if masked == n else jnp.concatenate([s[: n - masked], tail], axis=0)
                p = jnp.exp(s - lse_ref[0, h : h + 1, pl.ds(r0, rows)])
                dp = dot_nt(v_ref[pl.ds(0, n), :], gg)
                ds = (p * (dp - row_dot[h : h + 1, :])).astype(BF)
                va[pl.ds(0, n), :] += dot_nn(p.astype(BF), gg)
                ka[pl.ds(0, n), :] += dot_nn(ds, qq)
                dqs.append(dot_tn(ds, kk))
            dq_ref[pl.ds(r0, rows), :] = (jnp.where(first, dqs[0], dqs[1]) * SCALE).astype(BF)

        block(0, PR_DEV, plen, sh * PR_DEV, plen)
        for i in range(cont // rb):
            block(PR_DEV + i * rb, rb, plen + (i + 1) * rb, 0, rb)
        dkv_ref[0] = ka[...].astype(BF)
        dkv_ref[1] = va[...].astype(BF)

    spq = pl.BlockSpec((tok, PAIR), lambda i: (0, i + low))
    spk = pl.BlockSpec((keys, PAIR), lambda i: (0, i + low))
    return pl.pallas_call(
        kern,
        grid=(count,),
        in_specs=[
            pl.BlockSpec(memory_space=pltpu.SMEM),
            spq,
            spk,
            spk,
            spq,
            spq,
            pl.BlockSpec((1, 2, tok), lambda i: (i + low, 0, 0)),
        ]
        + [pl.BlockSpec(memory_space=pl.ANY)] * len(prev),
        out_specs=[spq, pl.BlockSpec((2, keys, PAIR), lambda i: (0, 0, i + low))],
        out_shape=[
            jax.ShapeDtypeStruct((tok, width), BF),
            jax.ShapeDtypeStruct((2, keys, width), BF),
        ],
        scratch_shapes=[pltpu.VMEM((keys, PAIR), F32), pltpu.VMEM((keys, PAIR), F32)],
        compiler_params=pltpu.CompilerParams(vmem_limit_bytes=VMEM_LIMIT),
        input_output_aliases={7 + i: i for i in range(len(prev))},
        cost_estimate=cost(40 * count * PAIR * tok * keys, 8 * count * PAIR * (tok + keys)),
        name="attn_bwd",
    )(shard, q, k, v, o, do, lse, *prev)


def out_proj_call(mix, second, tokens, vecs):
    ns, _, width = second.shape
    tok = tokens.shape[0]
    dsh = width // ns

    def kern(o_ref, w_ref, t_ref, vec_ref, x_ref, h_ref):
        wo = w_ref[...].reshape(width, width)
        x1 = t_ref[...].astype(F32) + (dot_nn(o_ref[...], wo) + vec_ref[4:5])
        x_ref[...] = x1
        h_ref[...] = (normalize(x1)[0] * vec_ref[5:6] + vec_ref[6:7]).astype(BF)

    whole = lambda a: pl.BlockSpec(a.shape, lambda i: (0,) * a.ndim)
    return pl.pallas_call(
        kern,
        grid=(1,),
        in_specs=[
            whole(mix),
            pl.BlockSpec((ns, dsh, width), lambda i: (0, 1, 0)),
            whole(tokens),
            whole(vecs),
        ],
        out_specs=[pl.BlockSpec((tok, width), lambda i: (0, 0))] * 2,
        out_shape=[jax.ShapeDtypeStruct((tok, width), F32), jax.ShapeDtypeStruct((tok, width), BF)],
        compiler_params=pltpu.CompilerParams(vmem_limit_bytes=VMEM_LIMIT),
        cost_estimate=cost(2 * width * width * tok, 12 * width * tok),
        name="out_proj",
    )(mix, second, tokens, vecs)


def fc_call(h2, second, got, other, vecs, where):
    ns, _, width = second.shape
    tok = h2.shape[0]
    dsh = width // ns
    half = ns // 2
    nq = len(got) + 1

    def kern(*refs):
        wh_ref, h_ref, own_ref = refs[:3]
        got_refs = refs[3 : 2 + nq]
        other_refs = refs[2 + nq : 1 + 2 * nq]
        vec_ref, g_ref, gp_ref, w_ref = refs[1 + 2 * nq :]
        me, core = wh_ref[0], wh_ref[1]
        step = pl.program_id(0)
        rows = half * dsh

        @pl.when(step == 0)
        def _():
            w_ref[0] = own_ref[...].reshape(width, width)

        for j in range(1, nq):

            @pl.when(step == j)
            def _():
                first = pl.multiple_of(core * rows, rows)
                second_half = pl.multiple_of((1 - core) * rows, rows)
                w_ref[0, pl.ds(first, rows), :] = got_refs[j - 1][...].reshape(rows, width)
                w_ref[0, pl.ds(second_half, rows), :] = other_refs[j - 1][...].reshape(rows, width)

        c = jnp.bitwise_xor(me, step)
        f = dot_nn(h_ref[...], w_ref[0]) + vec_ref[pl.ds(8 + c, 1), :]
        square = f * f
        t = jnp.tanh(0.7978845608028654 * f * (1.0 + 0.044715 * square))
        up = 0.5 * (1.0 + t)
        g_ref[0] = (f * up).astype(BF)
        slope = 0.5 * f * (1.0 - t * t) * (0.7978845608028654 + 0.1070322243 * square)
        gp_ref[0] = (up + slope).astype(BF)

    pick = lambda j, wh: (jnp.bitwise_xor(wh[0], j), 0, 0)
    return pl.pallas_call(
        kern,
        grid_spec=pltpu.PrefetchScalarGridSpec(
            num_scalar_prefetch=1,
            grid=(nq,),
            in_specs=[fixed(h2.shape), fixed((ns, dsh, width))]
            + [fixed(a.shape) for a in got]
            + [fixed(a.shape) for a in other]
            + [fixed(vecs.shape)],
            out_specs=[
                pl.BlockSpec((1, tok, width), pick),
                pl.BlockSpec((1, tok, width), pick),
                pl.BlockSpec((1, width, width), pick),
            ],
        ),
        out_shape=[
            jax.ShapeDtypeStruct((nq, tok, width), BF),
            jax.ShapeDtypeStruct((nq, tok, width), BF),
            jax.ShapeDtypeStruct((nq, width, width), BF),
        ],
        compiler_params=pltpu.CompilerParams(vmem_limit_bytes=VMEM_LIMIT),
        cost_estimate=cost(2 * nq * width * width * tok, 4 * nq * width * (tok + width)),
        name="fc",
    )(where, h2, second, *got, *other, vecs)


def proj_call(g, w_proj, x1, teacher, cotangent, weight, vecs):
    nq, tok, width = g.shape

    def kern(g_ref, w_ref, x_ref, te_ref, co_ref, wt_ref, vec_ref, y_ref, dy_ref, dm_ref, gw_ref, pb_ref, acc, keep):
        i = pl.program_id(0)

        @pl.when(i == 0)
        def _():
            acc[...] = x_ref[...] + vec_ref[7:8]

        @pl.when(i < nq)
        def _():
            keep[i] = g_ref[0]
            acc[...] += dot_nn(g_ref[0], w_ref[...])

        @pl.when(i == nq - 1)
        def _():
            y = acc[...]
            y_ref[...] = y.astype(BF)
            dy = co_ref[...].astype(F32) + wt_ref[...] * (y - te_ref[...].astype(F32))
            dy_ref[...] = dy
            dm = dy.astype(BF)
            dm_ref[...] = dm
            pb_ref[0:1, :] = jnp.sum(dm.astype(F32), axis=0, keepdims=True)
            pb_ref[1:8, :] = jnp.zeros((7, width), F32)

        @pl.when(i >= nq)
        def _():
            gw_ref[...] = dot_tn(keep[i - nq], dm_ref[...]).astype(BF)

    last = nq - 1
    return pl.pallas_call(
        kern,
        grid=(2 * nq,),
        in_specs=[
            pl.BlockSpec((1, tok, width), lambda i: (jnp.minimum(i, last), 0, 0)),
            pl.BlockSpec((width, width), lambda i: (jnp.minimum(i, last), 0)),
        ]
        + [fixed(a.shape) for a in (x1, teacher, cotangent, weight, vecs)],
        out_specs=[
            fixed((tok, width)),
            fixed((tok, width)),
            fixed((tok, width)),
            pl.BlockSpec((width, width), lambda i: (jnp.maximum(i - nq, 0), 0)),
            fixed((8, width)),
        ],
        out_shape=[
            jax.ShapeDtypeStruct((tok, width), BF),
            jax.ShapeDtypeStruct((tok, width), F32),
            jax.ShapeDtypeStruct((tok, width), BF),
            jax.ShapeDtypeStruct((nq * width, width), BF),
            jax.ShapeDtypeStruct((8, width), F32),
        ],
        scratch_shapes=[pltpu.VMEM((tok, width), F32), pltpu.VMEM((nq, tok, width), BF)],
        compiler_params=pltpu.CompilerParams(vmem_limit_bytes=VMEM_LIMIT),
        cost_estimate=cost(4 * nq * width * width * tok, 2 * nq * width * (tok + 2 * width)),
        name="proj",
    )(g, w_proj, x1, teacher, cotangent, weight, vecs)


def mid_call(dm, dy, w_proj, gp, h2, w_fc, x1, mix, second, vecs, core):
    nq, tok, width = gp.shape
    ns = second.shape[0]
    dsh = width // ns
    nz = ns // 2

    def kern(*refs):
        (co_ref, dm_ref, dy_ref, wp_ref, gp_ref, h_ref, wf_ref, x_ref, o_ref, wo_ref, vec_ref) = refs[:11]
        (fm_ref, ft_ref, om_ref, ot_ref, dx_ref, do_ref, sm_ref, fb_ref, ht, dh2) = refs[11:]
        j = pl.program_id(0)
        total = lambda m: jnp.sum(m, axis=0, keepdims=True)

        def split(gw, mine, theirs):
            gw = gw.astype(BF).reshape(nz, 2, dsh, width)
            for c in range(2):

                @pl.when(co_ref[0] == c)
                def _():
                    mine[...] = gw[:, c]
                    theirs[...] = gw[:, 1 - c]

        @pl.when(j == 0)
        def _():
            ht[...] = jnp.transpose(h_ref[...])
            dh2[...] = jnp.zeros_like(dh2)

        @pl.when(j < nq)
        def _():
            dg = dot_nt(dm_ref[...], wp_ref[...])
            df = (dg * gp_ref[0].astype(F32)).astype(BF)
            fb_ref[pl.ds(j, 1), :] = total(df.astype(F32))
            split(dot_nn(ht[...], df), fm_ref.at[0], ft_ref.at[0])
            dh2[...] += dot_nt(df, wf_ref[0])

        @pl.when(j == nq)
        def _():
            z, inv = normalize(x_ref[...])
            grad = dh2[...]
            sm_ref[0:1, :] = total(grad * z)
            sm_ref[1:2, :] = total(grad)
            dx = dy_ref[...] + norm_back(grad * vec_ref[5:6], z, inv)
            dx_ref[...] = dx
            da = dx.astype(BF)
            sm_ref[2:3, :] = total(da.astype(F32))
            do_ref[...] = dot_nt(da, wo_ref[...].reshape(width, width)).astype(BF)
            split(dot_tn(o_ref[...], da), om_ref, ot_ref)

    last = nq - 1
    pick = lambda j: (jnp.minimum(j, last), 0, 0)
    out = pl.BlockSpec((1, nz, dsh, width), lambda j: (jnp.minimum(j, last), 0, 0, 0))
    return pl.pallas_call(
        kern,
        grid=(nq + 1,),
        in_specs=[
            pl.BlockSpec(memory_space=pltpu.SMEM),
            fixed(dm.shape),
            fixed(dy.shape),
            pl.BlockSpec((width, width), lambda j: (jnp.minimum(j, last), 0)),
            pl.BlockSpec((1, tok, width), pick),
            fixed(h2.shape),
            pl.BlockSpec((1, width, width), pick),
            fixed(x1.shape),
            fixed(mix.shape),
            pl.BlockSpec((ns, dsh, width), lambda j: (0, 1, 0)),
            fixed(vecs.shape),
        ],
        out_specs=[
            out,
            out,
            fixed((nz, dsh, width)),
            fixed((nz, dsh, width)),
            fixed((tok, width)),
            fixed((tok, width)),
            fixed((8, width)),
            fixed((nq, width)),
        ],
        out_shape=[
            jax.ShapeDtypeStruct((nq, nz, dsh, width), BF),
            jax.ShapeDtypeStruct((nq, nz, dsh, width), BF),
            jax.ShapeDtypeStruct((nz, dsh, width), BF),
            jax.ShapeDtypeStruct((nz, dsh, width), BF),
            jax.ShapeDtypeStruct((tok, width), F32),
            jax.ShapeDtypeStruct((tok, width), BF),
            jax.ShapeDtypeStruct((8, width), F32),
            jax.ShapeDtypeStruct((nq, width), F32),
        ],
        scratch_shapes=[pltpu.VMEM((width, tok), BF), pltpu.VMEM((tok, width), F32)],
        compiler_params=pltpu.CompilerParams(vmem_limit_bytes=VMEM_LIMIT),
        cost_estimate=cost(
            2 * width * width * tok * (3 * nq + 2), 2 * width * (nq * (tok + 4 * width) + 8 * tok)
        ),
        name="mid",
    )(core, dm, dy, w_proj, gp, h2, w_fc, x1, mix, second, vecs)


def grads_call(h1, dq, dkv, shard, ns):
    keys, width = h1.shape
    tok = dq.shape[0]
    plen = ns * PR_DEV
    dsh = width // ns

    nz = ns // 2

    def kern(sh_ref, h_ref, dq_ref, d_ref, mine, theirs, ht):
        j = pl.program_id(0)

        def split(gw):
            gw = gw.astype(BF).reshape(nz, 2, dsh, width)
            for c in range(2):

                @pl.when(sh_ref[0] % 2 == c)
                def _():
                    mine[...] = gw[:, c]
                    theirs[...] = gw[:, 1 - c]

        @pl.when(j == 0)
        def _():
            ht[...] = jnp.transpose(h_ref[...])

        @pl.when(j < 2)
        def _():
            split(dot_nn(ht[...], d_ref[0]))

        @pl.when(j == 2)
        def _():
            own = pl.ds(pl.multiple_of(sh_ref[0] * PR_DEV, PR_DEV), PR_DEV)
            gq = dot_nn(ht[:, plen:], dq_ref[PR_DEV:, :]) + dot_tn(h_ref[own, :], dq_ref[:PR_DEV, :])
            split(gq)

    return pl.pallas_call(
        kern,
        grid=(3,),
        in_specs=[
            pl.BlockSpec(memory_space=pltpu.SMEM),
            fixed(h1.shape),
            fixed(dq.shape),
            pl.BlockSpec((1, keys, width), lambda j: (jnp.minimum(j, 1), 0, 0)),
        ],
        out_specs=[pl.BlockSpec((nz, dsh, width), lambda j: (0, (j + 1) % 3, 0))] * 2,
        out_shape=[jax.ShapeDtypeStruct((nz, 3 * dsh, width), BF)] * 2,
        scratch_shapes=[pltpu.VMEM((width, keys), BF)],
        compiler_params=pltpu.CompilerParams(vmem_limit_bytes=VMEM_LIMIT),
        cost_estimate=cost(2 * width * width * (2 * keys + tok), 2 * width * 5 * keys),
        name="grads",
    )(shard, h1, dq, dkv)


def small_layout(dsh, nq):
    return [(n, rows * dsh) for n, rows in ((0, 1), (1, 1), (2, 2), (4, 1), (5, 1), (6, 1), (8, nq), (7, 1))]


def dh1_call(bundle, wa, wk, tokens, vecs, dq, dkv, dx1, sums, fc_sums, last, shard):
    ns, _, width = bundle.shape
    tok = tokens.shape[0]
    cont = tok - PR_DEV
    plen = ns * PR_DEV
    nq = fc_sums.shape[0]
    kw = width // 2
    step = cont // PR_DEV
    chunks = ns // step

    def kern(*refs):
        (sh_ref, g_ref, wa_ref, wk_ref, t_ref, vec_ref, dq_ref, dk_ref, dv_ref, dx_ref) = refs[:10]
        (s2_ref, fb_ref, s3_ref, o_ref, ig_ref, sm, part) = refs[10:]
        i = pl.program_id(0)
        wq, wv = wa_ref[0], wa_ref[1]

        def back_kv(dk, dv):
            low = dot_nt(dk[:, :kw], wk_ref[0]) + dot_nt(dk[:, kw:], wk_ref[1])
            return low + dot_nt(dv, wv)

        total = lambda m: jnp.sum(m, axis=0, keepdims=True)

        @pl.when(i == 0)
        def _():
            sm[...] = jnp.zeros_like(sm)
            part[...] = jnp.zeros_like(part)

        def add(dh, z):
            sm[0:1, :] += total(dh * z)
            sm[1:2, :] += total(dh)

        dv = dv_ref[0]
        sm[3:4, :] += total(dv.astype(F32))
        dh = back_kv(dk_ref[0], dv)

        @pl.when(i < chunks)
        def _():
            z, _ = normalize(g_ref[...].reshape(cont, width).astype(F32))
            add(dh, z)
            o_ref[pl.ds(i * step, step), EXTRA:, :] = dh.astype(BF).reshape(step, PR_DEV, width)

        @pl.when(i == sh_ref[0] // step)
        def _():
            own = pl.ds(pl.multiple_of((sh_ref[0] % step) * PR_DEV, PR_DEV), PR_DEV)
            z, _ = normalize(t_ref[:PR_DEV, :].astype(F32))
            part = dot_nt(dq_ref[:PR_DEV, :], wq)
            add(part, z)
            both = back_kv(dk_ref[0, own, :], dv_ref[0, own, :])
            o_ref[sh_ref[0], EXTRA:, :] = (both + part).astype(BF)

        @pl.when(i == chunks)
        def _():
            z, inv = normalize(t_ref[PR_DEV:, :].astype(F32))
            full = dh + dot_nt(dq_ref[PR_DEV:, :], wq)
            add(full, z)
            ig_ref[PR_DEV:, :] = dx_ref[PR_DEV:, :] + norm_back(full * vec_ref[0:1], z, inv)
            ig_ref[:PR_DEV, :] = dx_ref[:PR_DEV, :]
            sm[2:3, :] = total(dq_ref[...].astype(F32))
            sm[4:5, :] = s2_ref[2:3, :]
            sm[5:7, :] = s2_ref[0:2, :]
            sm[7:8, :] = s3_ref[0:1, :]
            sm[8 : 8 + nq, :] = fb_ref[...]
            for b in range(ns):
                for n, (first, size) in enumerate(small_layout(width // ns, nq)):
                    row, off = divmod(b * size, width)
                    part[n : n + 1, :size] = sm[first + row : first + row + 1, off : off + size]
                o_ref[b, :EXTRA, :] = part[...].astype(BF)

    chunk = lambda k: pl.BlockSpec((1, cont, width), lambda i: (k, i, 0))
    out = (ns, EXTRA + PR_DEV, width)
    return pl.pallas_call(
        kern,
        grid=(chunks + 1,),
        in_specs=[
            pl.BlockSpec(memory_space=pltpu.SMEM),
            pl.BlockSpec((step, PR_DEV, width), lambda i: (jnp.minimum(i, chunks - 1), 0, 0)),
            fixed(wa.shape),
            fixed(wk.shape),
            fixed(tokens.shape),
            fixed(vecs.shape),
            fixed(dq.shape),
            chunk(0),
            chunk(1),
        ]
        + [fixed(a.shape) for a in (dx1, sums, fc_sums, last)],
        out_specs=[fixed(out), fixed((tok, width))],
        out_shape=[jax.ShapeDtypeStruct(out, BF), jax.ShapeDtypeStruct((tok, width), F32)],
        scratch_shapes=[pltpu.VMEM((2 * EXTRA, width), F32), pltpu.VMEM((EXTRA, width), F32)],
        compiler_params=pltpu.CompilerParams(vmem_limit_bytes=VMEM_LIMIT),
        cost_estimate=cost(
            2 * width * width * (2 * (plen + cont) + tok), 2 * width * (5 * plen + 10 * cont)
        ),
        name="dh1",
    )(shard, bundle, wa, wk, tokens, vecs, dq, dkv, dkv, dx1, sums, fc_sums, last)


def finish_call(grad, summed, tokens, vecs):
    tok, width = grad.shape

    def kern(g_ref, s_ref, t_ref, vec_ref, o_ref):
        z, inv = normalize(t_ref[...].astype(F32))
        e = s_ref[EXTRA:, :].astype(F32) * vec_ref[0:1]
        o_ref[...] = g_ref[...] + norm_back(e, z, inv)

    block = pl.BlockSpec((PR_DEV, width), lambda i: (0, 0))
    return pl.pallas_call(
        kern,
        grid=(1,),
        in_specs=[
            block,
            pl.BlockSpec(summed.shape, lambda i: (0, 0)),
            block,
            pl.BlockSpec(vecs.shape, lambda i: (0, 0)),
        ],
        out_specs=block,
        out_shape=jax.ShapeDtypeStruct((tok, width), F32),
        input_output_aliases={0: 0},
        cost_estimate=cost(20 * PR_DEV * width, 12 * PR_DEV * width),
        name="finish",
    )(grad, summed, tokens, vecs)


def over(axis, values, bit):
    n = lax.axis_size(axis)
    return lax.ppermute(values, axis, [(i, i ^ bit) for i in range(n)])


def cross(values, step):
    nr, ns = lax.axis_size("rep"), lax.axis_size("shard")
    pairs = [
        (r * ns + c, (r ^ (1 << ((c % 2) ^ step))) * ns + c) for r in range(nr) for c in range(ns)
    ]
    return lax.ppermute(values, ("rep", "shard"), pairs)


def rep_sum_small(values):
    n = lax.axis_size("rep")
    terms = [values] + [over("rep", values, b) for b in range(1, n)]
    terms = [t.astype(F32) for t in terms]
    while len(terms) > 1:
        terms = [terms[i] + terms[i + 1] for i in range(0, len(terms), 2)]
    return terms[0]


def small_call(terms, layout):
    def kern(*refs):
        values = [r[...].astype(F32) for r in refs[: len(terms)]]
        while len(values) > 1:
            values = [values[i] + values[i + 1] for i in range(0, len(values), 2)]
        for n, (_, size) in enumerate(layout):
            refs[len(terms) + n][...] = values[0][n, :size]

    return pl.pallas_call(
        kern,
        out_shape=[jax.ShapeDtypeStruct((size,), F32) for _, size in layout],
        cost_estimate=cost(terms[0].size * len(terms), 2 * terms[0].size * len(terms)),
        name="small",
    )(*terms)


def local(
    tokens,
    ln1_gain,
    ln1_bias,
    w_qkv,
    qv_bias,
    w_out,
    out_bias,
    ln2_gain,
    ln2_bias,
    w_fc,
    fc_bias,
    w_proj,
    proj_bias,
    teacher,
    cotangent,
    valid_mask,
):
    ns = lax.axis_size("shard")
    nr = lax.axis_size("rep")
    me = lax.axis_index("shard").astype(jnp.int32)
    shard = me.reshape(1)
    tok, width = tokens.shape
    nq = min(nr, w_fc.shape[1] // width)
    group = lax.axis_index("rep").astype(jnp.int32) % nq
    dsh = width // ns
    rb = 256

    core = me % 2
    half = lax.axis_index("rep").astype(jnp.int32)
    half = jnp.bitwise_xor(half, half // 2) % 2
    bundle = lax.all_gather(pack_call(tokens, w_qkv, half.reshape(1)), "shard")
    fc_own = lax.dynamic_slice_in_dim(w_fc, group * width, width, 1)
    mask_f = valid_mask.astype(F32)
    counts = jnp.sum(mask_f.reshape(-1, PR_DEV), axis=1).astype(BF)
    parts = [ln1_gain, ln1_bias, qv_bias, out_bias, ln2_gain, ln2_bias, proj_bias, fc_bias]
    offs = [0]
    for p in parts:
        offs.append(offs[-1] + p.shape[0])
    packed = jnp.concatenate(parts + [counts])
    packed = jnp.pad(packed, (0, (-packed.shape[0]) % 128))
    params = lax.all_gather(packed.reshape(1, -1), "shard", axis=0, tiled=True).astype(F32)
    vecs = jnp.concatenate(
        [params[:, offs[i] : offs[i + 1]].reshape(-1, width) for i in range(8)]
        + [jnp.zeros((16 - 8 - nq, width), F32)]
    )
    count = jnp.sum(params[:, offs[8] : offs[8] + counts.shape[0]])
    token_total = rep_sum_small(jnp.full((8, 128), count, F32))[0, 0]
    factor = tok * nr * ns / token_total
    weight = (factor * mask_f).reshape(tok, 1)

    second = jnp.concatenate([fc_own, w_out])
    second, vecs, weight = lax.optimization_barrier((second, vecs, weight))
    second = lax.all_gather(second, "shard")
    bundle, w_proj = lax.optimization_barrier((bundle, w_proj))
    full_proj = lax.all_gather(w_proj, "shard", axis=0, tiled=True)
    qkv_piece = lax.dynamic_slice_in_dim(bundle, core * (ns // 2), ns // 2, 0)
    qkv_far = cross(qkv_piece[:, PR_DEV:], 0)
    qkv_near = over("shard", qkv_far, 1)
    h1, q, k, v, wa, wk = qkv_call(
        bundle, qkv_far, qkv_near, tokens, vecs, jnp.stack([me, half, core])
    )
    q, k, v, second = lax.optimization_barrier((q, k, v, second))
    piece = lax.dynamic_slice_in_dim(second, core * (ns // 2), ns // 2, 0)[:, :dsh]
    q, k, v, piece = lax.optimization_barrier((q, k, v, piece))
    mix, lse = attn_fwd(q, k, v, shard, rb)
    mix, lse, *got = lax.optimization_barrier(
        (mix, lse, *[over("rep", piece, j) for j in range(1, nq)])
    )
    other = [over("shard", g, 1) for g in got]
    x1, h2 = out_proj_call(mix, second, tokens, vecs)
    g, gp, full_fc = fc_call(h2, second, got, other, vecs, jnp.stack([group, core]))
    out, dy, dm, grad_proj, last = proj_call(g, full_proj, x1, teacher, cotangent, weight, vecs)
    own_proj = lax.psum_scatter(grad_proj, "shard", scatter_dimension=0, tiled=True)
    fc_mine, fc_theirs, out_mine, out_theirs, dx1, do, sums, fc_sums = mid_call(
        dm, dy, full_proj, gp, h2, full_fc, x1, mix, second, vecs, core.reshape(1)
    )
    nz = ns // 2
    z = me // 2
    pick = lambda a, n: lax.dynamic_index_in_dim(a, n, 0, keepdims=False)
    plus = lambda *terms: sum(t.astype(F32) for t in terms).astype(BF)
    hold = lax.optimization_barrier

    def rep_sends(parts):
        return [pick(parts, jnp.bitwise_xor(group, b)) for b in range(nq)]

    def by_rep(sends):
        return sends[:1] + [over("rep", sends[b], b) for b in range(1, nq)]

    def by_z(parts):
        far = [over("shard", pick(parts, jnp.bitwise_xor(z, b)), 2 * b) for b in range(1, nz)]
        return [pick(parts, z)] + far

    def rest_of_rep(part):
        bit = nq
        while bit < nr:
            part = plus(part, over("rep", part, bit))
            bit *= 2
        return part

    first = jnp.where(core == 0, 1, 2)

    def halve(parts):
        at = lambda *ds: jnp.stack([pick(parts, jnp.bitwise_xor(group, d)) for d in ds])
        return at(first, 3), at(0, 3 - first)

    def spread(part, step):
        return jnp.concatenate([part, cross(part, step)])

    def quarters(relative):
        found = []
        for n in range(nq):
            d = jnp.bitwise_xor(group, n)
            found.append(pick(relative, jnp.where(core == 0, d, d % 2 * 2 + d // 2)))
        return found

    npair = width // PAIR
    cuts = [0, npair // 6, npair * 2 // 3, npair]

    def backward(n, prev=()):
        return attn_bwd(q, k, v, mix, do, lse, shard, rb, cuts[n], cuts[n + 1] - cuts[n], prev)

    dq, dkv = backward(0)
    fc_got, out_got = over("shard", fc_theirs, 1), over("shard", out_theirs, 1)
    dq, dkv, fc_got, out_got = hold((dq, dkv, fc_got, out_got))
    fc_half = plus(fc_mine, fc_got)
    out_half = plus(out_mine, out_got)
    out_half = jnp.swapaxes(out_half.reshape(nz, nq, dsh // nq, width), 0, 1)
    away, kept = halve(jnp.concatenate([fc_half, out_half], axis=2))
    dq, dkv, away, kept = hold((dq, dkv, away, kept))
    got = cross(away, 0)
    dq, dkv = backward(1, (dq, dkv))
    dq, dkv, got = hold((dq, dkv, got))
    both = plus(kept, got)
    dq, dkv, both = hold((dq, dkv, both))
    got = cross(both[1], 1)
    dq, dkv = backward(2, (dq, dkv))
    dq, dkv, got, own_proj = hold((dq, dkv, got, own_proj))
    quarter = plus(both[0], got)
    slot = lax.broadcasted_iota(jnp.int32, (1, 2, 1, 1), 1)
    quarter = jnp.where(slot == core, quarter[:, None], jnp.zeros((), BF))
    dq, dkv, quarter = hold((dq, dkv, quarter))
    own_fc = lax.psum_scatter(
        quarter.reshape(-1, width), "shard", scatter_dimension=0, tiled=True
    )
    proj_got = cross(own_proj, 0)
    qkv_mine, qkv_theirs = grads_call(h1, dq, dkv, shard, ns)
    dq, dkv, qkv_mine, qkv_theirs, proj_got = hold((dq, dkv, qkv_mine, qkv_theirs, proj_got))
    qkv_got = over("shard", qkv_theirs, 1)
    proj = plus(own_proj, proj_got)
    proj_got = cross(proj, 1)
    last_part, ig = dh1_call(bundle, wa, wk, tokens, vecs, dq, dkv, dx1, sums, fc_sums, last, shard)
    last_part, qkv_got, proj_got = hold((last_part, qkv_got, proj_got))
    own = lax.psum_scatter(last_part.reshape(-1, width), "shard", scatter_dimension=0, tiled=True)

    qkv_half = plus(qkv_mine, qkv_got).reshape(nz, nq, 3 * dsh // nq, width)
    away, kept = halve(jnp.swapaxes(qkv_half, 0, 1))
    got = cross(away, 0)
    proj = rest_of_rep(plus(proj, proj_got))
    got, proj = hold((got, proj))
    both = plus(kept, got)
    got = cross(both[1], 1)
    part = spread(rest_of_rep(own_fc)[None], 0)
    got, part = hold((got, part))
    qkv_z = by_z(plus(both[0], got))
    part = spread(part, 1)
    natural = quarters(part)
    sum_fc = jnp.concatenate([n[:dsh] for n in natural], axis=1).astype(F32)
    sum_out = jnp.concatenate([n[dsh:] for n in natural], axis=0).astype(F32)
    sum_proj = proj.astype(F32)
    sum_fc, sum_out, sum_proj, *qkv_z = hold((sum_fc, sum_out, sum_proj, *qkv_z))
    qkv_part = rest_of_rep(plus(*qkv_z))[None]
    own, qkv_part = hold((own, qkv_part))
    qkv_part = spread(qkv_part, 0)

    layout = small_layout(dsh, nq)
    mine = own[:EXTRA, : max(size for _, size in layout)]
    small = small_call([mine] + [over("rep", mine, b) for b in range(1, nr)], layout)
    input_grad = finish_call(ig, own, tokens, vecs)
    sum_qkv = jnp.concatenate(quarters(spread(qkv_part, 1))).astype(F32)

    return (
        out,
        input_grad,
        small[0],
        small[1],
        jnp.concatenate([sum_qkv[j * dsh : (j + 1) * dsh] for j in range(3)], axis=1),
        small[2],
        sum_out,
        small[3],
        small[4],
        small[5],
        sum_fc,
        small[6],
        sum_proj,
        small[7],
    )


def solution(mesh):
    rows = P(("rep", "shard"), None)
    mat = P("shard", None)
    vec = P("shard")
    return jax.shard_map(
        local,
        mesh=mesh,
        in_specs=(
            rows,
            vec,
            vec,
            mat,
            vec,
            mat,
            vec,
            vec,
            vec,
            mat,
            vec,
            mat,
            vec,
            rows,
            rows,
            P(("rep", "shard")),
        ),
        out_specs=(rows, rows, vec, vec, mat, vec, mat, vec, vec, vec, mat, vec, mat, vec),
        check_vma=False,
    )
```
